32 devices in a mesh: dp: 8 (over z, x), mp: 4 (over y, core).
Axes of the slice: x: 2, y: 2, z: 4, core: 2. Of those that a mesh axis runs over, the one named last changes fastest.
Arguments:
- tokens: bfloat16 [8192, 768], P('dp'), may hold values from -6 to 6
- cotangent: bfloat16 [8192, 768], P('dp'), may hold values from -6 to 6
- lengths: int32 [32], P('dp'), may hold values from 32 to 256, as said below
- w_qkv: bfloat16 [768, 3, 768], P('dp', None, 'mp'), may hold values from -0.21875 to 0.21875
- qv_bias: bfloat16 [2, 4, 192], P(None, 'mp', 'dp'), may hold values from -3 to 3
- w_out: bfloat16 [768, 768], P('mp', 'dp'), may hold values from -1.75 to 1.75
- w_in: bfloat16 [768, 3072], P('dp', 'mp'), may hold values from -0.21875 to 0.21875
- in_bias: bfloat16 [4, 768], P('mp', 'dp'), may hold values from -3 to 3
- w_down: bfloat16 [3072, 768], P('mp', 'dp'), may hold values from -0.109375 to 0.109375
- pilot: bfloat16 [3072, 768], P('mp', 'dp'), may hold values from -0.109375 to 0.109375
- gains: bfloat16 [2, 768], P(None, 'dp'), may hold values from 0.25 to 1.75
- shifts: bfloat16 [4, 768], P(None, 'dp'), may hold values from -3 to 3
Outputs:
- output: bfloat16 [8192, 768], P('dp')
- input_grad: float32 [8192, 768], P('dp')
- along: float32 [8192, 768], P('dp')
- grad_qkv: float32 [768, 3, 768], P('dp', None, 'mp')
- grad_qv_bias: float32 [2, 4, 192], P(None, 'mp', 'dp')
- grad_out: float32 [768, 768], P('mp', 'dp')
- grad_in: float32 [768, 3072], P('dp', 'mp')
- grad_in_bias: float32 [4, 768], P('mp', 'dp')
- grad_down: float32 [3072, 768], P('mp', 'dp')
- grad_gains: float32 [2, 768], P(None, 'dp')
- grad_shifts: float32 [4, 768], P(None, 'dp')
The draws below stay inside these ranges and needn't reach their ends.
Inputs may be any that keep to these rules, and one draw needn't show every extreme that they name: `lengths`: the number of real tokens of a sequence, the rest of its 256 positions being padding; some sequence is full.
All inputs are finite; a program needn't handle non-finite values.
Results may differ from the reference program's by a relative error of at most 0.02.
Values may be sent and summed in bfloat16 or wider, within the bound.
A program may use at most 128 MiB of HBM per device.

```python
import jax
import jax.numpy as jnp
from jax import lax

D = 768
HEADS = 12
FF = 3072
SEQ_LEN = 256
MB = 2
SB = 2
SEQS = 32
TOKEN_COUNT = 8192
N_DP = 8
N_MP = 4


def draw_lengths(key, part):
    base = jax.random.randint(key, (SEQS,), SEQ_LEN // 8, SEQ_LEN + 1)
    spot = jax.random.randint(jax.random.fold_in(key, 7), (), 0, SEQS)
    return base.at[spot].set(SEQ_LEN).astype(jnp.int32)


def level_of(rng, shape, pieces, smallest, high):
    factor_of, own = 1.0, jax.random.fold_in(rng, 6)
    for position, blocks in pieces:
        draws = jnp.exp(jax.random.uniform(jax.random.fold_in(own, position), (blocks,), jnp.float32, smallest / len(pieces), high / len(pieces)))
        factor_of = factor_of * jnp.repeat(draws, shape[position] // blocks).reshape([-1 if axis == position else 1 for axis in range(len(shape))])
    return factor_of


def gaussian(stream_key, shape, spread, limit, pieces=(), held_as=jnp.bfloat16):
    drawn = spread * jax.random.normal(stream_key, shape, jnp.float32)
    if pieces:
        drawn = drawn * level_of(stream_key, shape, pieces, -0.22, 0.18)
    return jnp.clip(drawn, -limit, limit).astype(held_as)


def setup_inputs(seed: int = 0) -> dict:
    arg_keys = jax.random.split(jax.random.key(seed), 13)
    tokens = gaussian(arg_keys[0], (TOKEN_COUNT, D), 1.0, 6.0, ((0, 8),))
    cotangent = gaussian(arg_keys[1], (TOKEN_COUNT, D), 1.0, 6.0, ((0, 8),))
    lengths = draw_lengths(jax.random.fold_in(arg_keys[12], 71), 0)
    w_qkv = gaussian(arg_keys[3], (D, 3, D), D ** -0.5, 0.21875, ((0, 8), (2, 4)))
    qv_bias = gaussian(arg_keys[4], (2, N_MP, D // N_MP), 0.5, 3.0, ((1, 4), (2, 8)))
    w_out = gaussian(arg_keys[5], (D, D), (D // 64) ** -0.5, 1.75, ((0, 4), (1, 8)))
    w_in = gaussian(arg_keys[6], (D, FF), D ** -0.5, 0.21875, ((0, 8), (1, 4)))
    in_bias = gaussian(arg_keys[7], (N_MP, FF // N_MP), 0.5, 3.0, ((0, 4), (1, 8)))
    w_down = gaussian(arg_keys[8], (FF, D), FF ** -0.5, 0.109375, ((0, 4), (1, 8)))
    pilot = gaussian(arg_keys[9], (FF, D), FF ** -0.5, 0.109375, ((0, 4), (1, 8)))
    gains = jnp.clip(1.0 + 0.15 * jax.random.normal(arg_keys[10], (2, D), jnp.float32), 0.25, 1.75).astype(jnp.bfloat16)
    shifts = gaussian(arg_keys[11], (4, D), 0.5, 3.0, ((1, 8),))
    return dict(tokens=tokens, cotangent=cotangent, lengths=lengths, w_qkv=w_qkv, qv_bias=qv_bias, w_out=w_out, w_in=w_in, in_bias=in_bias, w_down=w_down, pilot=pilot, gains=gains, shifts=shifts)


epsilon = 1e-06
highest = lax.Precision.HIGHEST

@jax.custom_vjp
def low(v):
    return lax.optimization_barrier(v.astype(jnp.bfloat16)).astype(jnp.float32)

@jax.custom_vjp
def low_back(v):
    return v

def low_keep(v):
    return (low(v), None)

def low_pass(kept, grad):
    return (grad,)

def back_keep(v):
    return (v, None)

def back_low(kept, grad):
    return (low(grad),)
low.defvjp(low_keep, low_pass)
low_back.defvjp(back_keep, back_low)

def both_ways(value):
    return low(low_back(value))

def affine_norm(stream, gain, shift):
    centered_input = stream - lax.optimization_barrier(jnp.mean(stream, -1, keepdims=True))
    return centered_input * lax.rsqrt(lax.optimization_barrier(jnp.mean(centered_input * centered_input, -1, keepdims=True)) + epsilon) * gain + shift

def forward(params, inputs, keep, tangent):
    w_qkv, qv_bias, w_out, w_in, in_bias, w_down, gains, shifts = params
    row_count = inputs.shape[0]
    seq_count = keep.shape[0]
    head_dim = D // HEADS
    projected = jnp.dot(inputs, w_qkv.reshape(D, 3 * D), precision=highest).reshape(row_count, 3, D)
    bias_rows = jnp.stack([qv_bias[0], jnp.zeros_like(qv_bias[0]), qv_bias[1]])
    projected = both_ways(projected + bias_rows)
    split_heads = projected.reshape(seq_count, SEQ_LEN, 3, HEADS, head_dim)
    queries = split_heads[:, :, 0]
    key_matrix_rows = split_heads[:, :, 1]
    value_rows = split_heads[:, :, 2]
    scores = low_back(jnp.einsum('bqhd,bkhd->bhqk', queries, key_matrix_rows, precision=highest) * head_dim ** (-0.5))
    scores = jnp.where(keep[:, None, None, :], scores, -1000000000.0)
    weights = low(jax.nn.softmax(scores, axis=-1))
    context = both_ways(jnp.einsum('bhqk,bkhd->bqhd', weights, value_rows, precision=highest).reshape(row_count, D))
    attended = low_back(jnp.dot(context, w_out, precision=highest))
    normed = affine_norm(inputs + attended + shifts[0], gains[0], shifts[1])
    hidden_pre = low_back(jnp.dot(low(normed), w_in, precision=highest) + in_bias)
    hidden = low(jax.nn.gelu(hidden_pre, approximate=False))
    branch = low_back(jnp.dot(hidden, w_down, precision=highest))
    stream = normed + branch + shifts[2]
    output = affine_norm(stream, gains[1], shifts[3])
    centered_input = stream - lax.optimization_barrier(jnp.mean(stream, -1, keepdims=True))
    inverse_deviation = lax.rsqrt(lax.optimization_barrier(jnp.mean(centered_input * centered_input, -1, keepdims=True)) + epsilon)
    normalized_input = centered_input * inverse_deviation
    tangent_total_sum = jnp.dot(hidden, tangent, precision=highest)
    along = gains[1] * inverse_deviation * (tangent_total_sum - lax.optimization_barrier(jnp.mean(tangent_total_sum, -1, keepdims=True)) - normalized_input * lax.optimization_barrier(jnp.mean(tangent_total_sum * normalized_input, -1, keepdims=True)))
    return (output, along)

def reference(tokens, cotangent, lengths, w_qkv, qv_bias, w_out, w_in, in_bias, w_down, pilot, gains, shifts):
    params = (w_qkv.astype(jnp.float32), qv_bias.astype(jnp.float32).reshape(2, D), w_out.astype(jnp.float32), w_in.astype(jnp.float32), in_bias.astype(jnp.float32).reshape(FF), w_down.astype(jnp.float32), gains.astype(jnp.float32), shifts.astype(jnp.float32))
    tangent = pilot.astype(jnp.float32)
    group_rows = MB * SB * SEQ_LEN
    inputs_all = tokens.astype(jnp.float32).reshape(N_DP, group_rows, D)
    upstream_all = cotangent.astype(jnp.float32).reshape(N_DP, group_rows, D)
    lengths_all = lengths.reshape(N_DP, MB * SB)
    positions = jnp.arange(SEQ_LEN, dtype=jnp.int32)

    def step(totals, item):
        inputs, upstream, seq_lengths = item
        keep = positions[None, :] < seq_lengths[:, None]
        output, back, along = jax.vjp(lambda prm, xin: forward(prm, xin, keep, tangent), params, inputs, has_aux=True)
        masked = upstream * keep.reshape(-1, 1).astype(jnp.float32)
        grads, input_grad = back(masked)
        totals = jax.tree.map(lambda total, term: total + term, totals, grads)
        return (totals, (output, input_grad, along))
    zeros = jax.tree.map(jnp.zeros_like, params)
    totals, (outputs, input_grads, alongs) = lax.scan(step, zeros, (inputs_all, upstream_all, lengths_all))
    g_qkv, g_qvb, g_out, g_in, g_ib, g_down, g_gains, g_shifts = totals
    return (outputs.reshape(TOKEN_COUNT, D).astype(jnp.bfloat16), input_grads.reshape(TOKEN_COUNT, D), alongs.reshape(TOKEN_COUNT, D), g_qkv, g_qvb.reshape(2, N_MP, D // N_MP), g_out, g_in, g_ib.reshape(N_MP, FF // N_MP), g_down, g_gains, g_shifts)
```

```python
import functools
import math

import jax
import jax.numpy as jnp
from jax import lax
from jax.experimental import pallas as pl
from jax.experimental.pallas import tpu as pltpu
from jax.sharding import PartitionSpec as P

HEAD_DIM = 64
SEQ_LEN = 256
EPSILON = 1e-06
NZ, NX, NY, NC = 4, 2, 2, 2
BLOCKS = NZ * NX
GROUP = NY * NC
SMALL_ROWS = 16
BIAS_ROW = 6
QKV_ROW = BIAS_ROW + GROUP
FWD_ROWS = 48
BWD_ROWS = 48
F32 = jnp.float32
BF16 = jnp.bfloat16
QKV, IN, DOWN, PILOT = range(4)


def nt(a, b):
    return lax.dot_general(a, b, (((1,), (1,)), ((), ())), preferred_element_type=F32)


def tn(a, b):
    return lax.dot_general(a, b, (((0,), (0,)), ((), ())), preferred_element_type=F32)


def nn(a, b):
    return jnp.dot(a, b, preferred_element_type=F32)


def row_mean(v):
    return jnp.mean(v, -1, keepdims=True)


def col_sum(v):
    return jnp.sum(v, 0, keepdims=True)


def layer_kernel(
    inner,
    lens,
    tok,
    cot,
    shard_a,
    shard_i,
    shard_d,
    shard_p,
    small,
    out_o,
    along_o,
    ig_o,
    grad_a,
    grad_i,
    grad_d,
    small_sum,
    w_a,
    w_i,
    w_d,
    w_p,
    g_i,
    g_d,
    r_core,
    r_yf,
    r_xf,
    r_xs,
    r_ys,
    r_z,
    par,
    par_in,
    gs,
    gs_in,
    xs,
    cots,
    qkv,
    prob,
    ctx,
    acc,
    xh1,
    rs1,
    low,
    low_t,
    hid,
    gder,
    xh2,
    rs2,
    sgrad,
    bl,
    bl_t,
    qg,
    own,
    s_load,
    s_z,
    r_zs,
    s_x,
    r_x,
    s_y,
    r_y,
    s_dx,
    r_dx,
    s_dy,
    r_dy,
    s_c,
    r_c,
    s_rc,
    r_rc,
    s_red,
    r_red,
    s_rz,
    r_rz,
    s_sm,
    r_sm,
    s_out,
    r_out,
    s_own,
):
    weights = (w_a, w_i, w_d, w_p)
    shards = (shard_a, shard_i, shard_d, shard_p)
    width = xs.shape[1]
    block = w_a.shape[3]
    head_cols = ctx.shape[2]
    qkv_cols = 3 * head_cols
    heads_here = head_cols // HEAD_DIM
    rows = xs.shape[0]
    scale = HEAD_DIM ** (-0.5)

    dp = lax.axis_index("dp")
    mp = lax.axis_index("mp")
    spot = dp // inner
    rest = dp - spot * inner
    z, x = spot // NX, spot % NX
    y, c = mp // NC, mp % NC
    far_y, far_x, far_c = 1 - y, 1 - x, 1 - c
    mine = mp
    over_y = far_y * NC + c
    x_peer = {"dp": (z * NX + far_x) * inner + rest, "mp": mp}
    y_peer = {"dp": dp, "mp": over_y}
    c_peer = {"dp": dp, "mp": y * NC + far_c}

    def z_at(step):
        return (z + step) % NZ

    def z_from(step):
        return (z + NZ - step) % NZ

    def z_peer(step):
        return {"dp": (z_at(step) * NX + x) * inner + rest, "mp": mp}

    sends = []

    def remote(src, dst, send, recv, peer):
        return pltpu.make_async_remote_copy(
            src_ref=src,
            dst_ref=dst,
            send_sem=send,
            recv_sem=recv,
            device_id=peer,
            device_id_type=pl.DeviceIdType.MESH,
        )

    def push(src, dst, send, recv, peer, chunk=None):
        copy = remote(src, dst, send, recv, peer)
        copy.start()
        sends.append((chunk, copy))

    def arrived(dst, send, recv):
        remote(dst, dst, send, recv, c_peer).wait_recv()

    barrier = pltpu.get_barrier_semaphore()
    peers = [x_peer, y_peer, c_peer] + [z_peer(step) for step in range(1, NZ)]
    for peer in peers:
        pl.semaphore_signal(barrier, inc=1, device_id=peer, device_id_type=pl.DeviceIdType.MESH)
    pl.semaphore_wait(barrier, len(peers))

    loads = []
    for k in range(4):
        loads.append(
            pltpu.make_async_copy(shards[k], weights[k].at[mine, z, x], s_load.at[k])
        )
    my_rows = pl.ds(mp * rows, rows)
    loads.append(pltpu.make_async_copy(tok.at[my_rows], xs, s_load.at[4]))
    loads.append(pltpu.make_async_copy(cot.at[my_rows], cots, s_load.at[5]))

    def send_z(k):
        for step in range(1, NZ):
            push(
                shards[k],
                weights[k].at[mine, z, x],
                s_z.at[k, step],
                r_zs.at[k, step],
                z_peer(step),
                k,
            )

    def send_own(k):
        for sem_s, sem_r, peer in ((s_x, r_x, x_peer), (s_y, r_y, y_peer)):
            push(shards[k], weights[k].at[mine, z, x], sem_s.at[k, 0], sem_r.at[k, 0], peer, k)

    def forward_z(k, step):
        src = weights[k].at[mine, z_from(step), x]
        arrived(src, s_z.at[k, step], r_zs.at[k, step])
        push(src, src, s_x.at[k, step], r_x.at[k, step], x_peer, k)
        push(src, src, s_y.at[k, step], r_y.at[k, step], y_peer, k)

    first = pl.ds(0, FWD_ROWS)
    second = pl.ds(FWD_ROWS, block - FWD_ROWS)

    def forward_diagonal(k, step):
        from_x = weights[k].at[mine, z_from(step), far_x]
        arrived(from_x, s_x.at[k, step], r_x.at[k, step])
        part = weights[k].at[mine, z_from(step), far_x, first]
        push(part, part, s_dy.at[k, step], r_dy.at[k, step], y_peer, k)
        from_y = weights[k].at[over_y, z_from(step), x]
        arrived(from_y, s_y.at[k, step], r_y.at[k, step])
        part = weights[k].at[over_y, z_from(step), x, second]
        push(part, part, s_dx.at[k, step], r_dx.at[k, step], x_peer, k)

    def to_core(k, index, block_index, column):
        src = weights[k].at[block_index, :, column]
        push(src, src, s_c.at[k, index], r_c.at[k, index], c_peer, k)

    def finish(k):
        for step in range(NZ):
            arrived(
                weights[k].at[over_y, z_from(step), far_x, first],
                s_dy.at[k, step],
                r_dy.at[k, step],
            )
            arrived(
                weights[k].at[over_y, z_from(step), far_x, second],
                s_dx.at[k, step],
                r_dx.at[k, step],
            )
        to_core(k, 3, over_y, far_x)
        for index, (block_index, column) in enumerate(
            (
                (y * NC + far_c, x),
                (y * NC + far_c, far_x),
                (far_y * NC + far_c, x),
                (far_y * NC + far_c, far_x),
            )
        ):
            arrived(
                weights[k].at[block_index, :, column], s_c.at[k, index], r_c.at[k, index]
            )

    def small_stage(which, buf, buf_in, stage):
        if stage < 3:
            peer = (c_peer, y_peer, x_peer)[stage]
            push(buf.at[stage], buf_in.at[stage], s_sm.at[which, stage], r_sm.at[which, stage], peer)
        else:
            for step in range(1, NZ):
                push(
                    buf.at[3],
                    buf_in.at[2 + step],
                    s_sm.at[which, 2 + step],
                    r_sm.at[which, 2 + step],
                    z_peer(step),
                )

    def small_add(which, buf, buf_in, stage):
        arrived(buf_in.at[stage], s_sm.at[which, stage], r_sm.at[which, stage])
        buf[stage + 1] = buf[stage] + buf_in[stage]

    def small_last(which, buf, buf_in):
        for step in range(1, NZ):
            arrived(buf_in.at[2 + step], s_sm.at[which, 2 + step], r_sm.at[which, 2 + step])
        total = jnp.zeros(buf.shape[1:], F32)
        for place in range(NZ):
            term = buf[3]
            for step in range(1, NZ):
                term = jnp.where(z_from(step) == place, buf_in[2 + step], term)
            total = total + term
        return total

    load_small = pltpu.make_async_copy(small, par.at[0], s_load.at[6])
    load_small.start()
    send_z(QKV)
    for copy in loads:
        copy.start()
    send_own(QKV)
    load_small.wait()
    small_stage(0, par, par_in, 0)
    send_z(IN)
    small_add(0, par, par_in, 0)
    small_stage(0, par, par_in, 1)
    forward_z(QKV, 1)
    small_add(0, par, par_in, 1)
    small_stage(0, par, par_in, 2)
    forward_z(QKV, 3)
    small_add(0, par, par_in, 2)
    small_stage(0, par, par_in, 3)
    forward_z(QKV, 2)
    send_z(DOWN)
    send_z(PILOT)
    for copy in loads:
        copy.wait()
    to_core(QKV, 0, mine, x)
    send_own(IN)
    for step in range(NZ):
        forward_diagonal(QKV, step)
    to_core(QKV, 1, mine, far_x)
    to_core(QKV, 2, over_y, x)
    par[4] = small_last(0, par, par_in)
    for step in (1, 3, 2):
        forward_z(IN, step)
    to_core(IN, 0, mine, x)
    finish(QKV)

    length = lens[mp]
    key_keep = lax.broadcasted_iota(jnp.int32, (rows, rows), 1) < length
    row_keep = (lax.broadcasted_iota(jnp.int32, (rows, 1), 0) < length).astype(F32)

    def par_row(index):
        return par[4, index : index + 1, :]

    def square(ref, m, start, stop):
        value = ref[m, :, :, :, start:stop]
        return value.reshape(width, stop - start)

    def project(m, carry):
        bias = par[4, pl.ds(QKV_ROW + m, 1), :qkv_cols]
        qkv[m] = (nn(xs[...], square(w_a, m, 0, qkv_cols)) + bias).astype(BF16)
        return carry

    lax.fori_loop(0, GROUP, project, 0)

    def attend(m, carry):
        part = qkv[m]
        for h in range(heads_here):
            lo = h * HEAD_DIM
            q = part[:, lo : lo + HEAD_DIM]
            k = part[:, head_cols + lo : head_cols + lo + HEAD_DIM]
            v = part[:, 2 * head_cols + lo : 2 * head_cols + lo + HEAD_DIM]
            score = jnp.where(key_keep, nt(q, k) * scale, -1000000000.0)
            expo = jnp.exp(score - jnp.max(score, -1, keepdims=True))
            weight = expo / jnp.sum(expo, -1, keepdims=True)
            prob[m * heads_here + h] = weight
            ctx[m, :, lo : lo + HEAD_DIM] = nn(weight.astype(BF16), v).astype(BF16)
        return carry

    for step in range(NZ):
        forward_diagonal(IN, step)
    to_core(IN, 1, mine, far_x)
    to_core(IN, 2, over_y, x)
    send_own(DOWN)
    lax.fori_loop(0, GROUP, attend, 0)
    for step in (1, 3, 2):
        forward_z(DOWN, step)
    to_core(DOWN, 0, mine, x)

    acc[...] = jnp.zeros_like(acc)

    def attended(m, carry):
        acc[...] += nt(ctx[m], square(w_a, m, qkv_cols, width))
        return carry

    lax.fori_loop(0, GROUP, attended, 0)
    opening = xs[...].astype(F32) + acc[...] + par_row(2)
    centered = opening - row_mean(opening)
    rstd = lax.rsqrt(row_mean(centered * centered) + EPSILON)
    rs1[...] = rstd
    xhat = centered * rstd
    xh1[...] = xhat
    normed_low = (xhat * par_row(0) + par_row(3)).astype(BF16)
    low[...] = normed_low
    finish(IN)
    for step in range(NZ):
        forward_diagonal(DOWN, step)
    to_core(DOWN, 1, mine, far_x)
    to_core(DOWN, 2, over_y, x)
    send_own(PILOT)

    def expand(m, carry):
        pre = nn(low[...], square(w_i, m, 0, width)) + par[4, pl.ds(BIAS_ROW + m, 1), :]
        gate = 0.5 + 0.5 * lax.erf(pre * math.sqrt(0.5))
        hid[m] = (pre * gate).astype(BF16)
        gder[m] = gate + pre * (jnp.exp(-0.5 * pre * pre) * (1.0 / math.sqrt(2.0 * math.pi)))
        return carry

    lax.fori_loop(0, GROUP, expand, 0)
    low_t[...] = low[...].T
    for step in (1, 3, 2):
        forward_z(PILOT, step)
    to_core(PILOT, 0, mine, x)
    finish(DOWN)

    acc[...] = xh1[...] * par_row(0) + par_row(3) + par_row(4)

    def contract(m, carry):
        acc[...] += nt(hid[m], square(w_d, m, 0, width))
        return carry

    lax.fori_loop(0, GROUP, contract, 0)
    for step in range(NZ):
        forward_diagonal(PILOT, step)
    to_core(PILOT, 1, mine, far_x)
    to_core(PILOT, 2, over_y, x)

    stream = acc[...]
    centered = stream - row_mean(stream)
    rstd = lax.rsqrt(row_mean(centered * centered) + EPSILON)
    rs2[...] = rstd
    xhat = centered * rstd
    xh2[...] = xhat
    own[0] = (xhat * par_row(1) + par_row(5)).astype(BF16)

    outs = (out_o, along_o, ig_o)

    def send_result(index):
        dst = outs[index].at[my_rows]
        pltpu.make_async_copy(own.at[index], dst, s_own.at[index]).start()
        push(own.at[index], dst, s_out.at[index, 0], r_out.at[index, 0], y_peer)
        push(own.at[index], dst, s_out.at[index, 1], r_out.at[index, 1], c_peer)

    def forward_result(index):
        part = outs[index].at[pl.ds(over_y * rows, rows)]
        arrived(part, s_out.at[index, 0], r_out.at[index, 0])
        push(part, part, s_out.at[index, 2], r_out.at[index, 2], c_peer)

    def finish_result(index):
        pltpu.make_async_copy(own.at[index], outs[index].at[my_rows], s_own.at[index]).wait()
        near = outs[index].at[pl.ds((y * NC + far_c) * rows, rows)]
        arrived(near, s_out.at[index, 1], r_out.at[index, 1])
        far = outs[index].at[pl.ds((far_y * NC + far_c) * rows, rows)]
        arrived(far, s_out.at[index, 2], r_out.at[index, 2])

    send_result(0)

    gs[0] = jnp.zeros(gs.shape[1:], F32)

    def norm_back(grad, xhat, rstd, gain):
        hat = grad * gain
        return rstd * (hat - row_mean(hat) - xhat * row_mean(hat * xhat))

    masked = cots[...].astype(F32) * row_keep
    xhat = xh2[...]
    gs[0, 1:2, :] = col_sum(masked * xhat)
    gs[0, 5:6, :] = col_sum(masked)
    stream_grad = norm_back(masked, xhat, rs2[...], par_row(1))
    gs[0, 4:5, :] = col_sum(stream_grad)
    sgrad[...] = stream_grad
    bl[...] = stream_grad.astype(BF16)
    bl_t[...] = bl[...].T
    acc[...] = stream_grad

    def block_of(i):
        other = i < NY
        return jnp.where(other, i * NC + far_c, (i - NY) * NC + c)

    slab = NX * block

    def outer(left_t, right, ref, m, start, stop):
        def one(zz, carry):
            top = pl.multiple_of(zz * slab, slab)
            value = nn(left_t[pl.ds(top, slab), :], right[...])
            ref[m, zz, :, :, start:stop] = value.astype(BF16).reshape(NX, block, stop - start)
            return carry

        lax.fori_loop(0, NZ, one, 0)

    def to_partner(ref, k, i):
        src = ref.at[i * NC + far_c]
        copy = remote(src, r_core.at[k, i], s_rc.at[k, i], r_rc.at[k, i], c_peer)
        return copy

    pre_low = own.at[1]

    def back_ff(i, carry):
        m = block_of(i)
        outer(bl_t, hid.at[m], g_d, m, 0, width)
        grad = nn(bl[...], square(w_d, m, 0, width)) * gder[m]
        pre_low[...] = grad.astype(BF16)
        gs[0, pl.ds(BIAS_ROW + m, 1), :] = col_sum(pre_low[...].astype(F32))
        outer(low_t, pre_low, g_i, m, 0, width)
        acc[...] += nt(pre_low[...], square(w_i, m, 0, width))

        @pl.when(i < NY)
        def _():
            to_partner(g_d, 0, i).start()
            to_partner(g_i, 1, i).start()

        return carry

    lax.fori_loop(0, GROUP, back_ff, 0)

    top_rows = pl.ds(0, BWD_ROWS)
    low_rows = pl.ds(BWD_ROWS, block - BWD_ROWS)

    def add_core(k, ref):
        for yy in range(NY):
            m = yy * NC + c
            to_partner(ref, k, yy).wait_recv()

            def one(zz, carry):
                ref[m, zz] = ref[m, zz] + r_core[k, yy, zz]
                return carry

            lax.fori_loop(0, NZ, one, 0)

    def reduce_first(k, ref):
        push(
            ref.at[over_y, :, :, top_rows], r_yf.at[k], s_red.at[k, 0], r_red.at[k, 0], y_peer
        )
        for yy in range(NY):
            push(
                ref.at[yy * NC + c, :, far_x, low_rows],
                r_xf.at[k, yy],
                s_red.at[k, 1 + yy],
                r_red.at[k, 1 + yy],
                x_peer,
            )

    def reduce_second(k, ref):
        arrived(r_yf.at[k], s_red.at[k, 0], r_red.at[k, 0])
        ref[mine, :, :, top_rows, :] = ref[mine, :, :, top_rows, :] + r_yf[k]
        push(
            ref.at[mine, :, far_x, top_rows], r_xs.at[k], s_red.at[k, 3], r_red.at[k, 3], x_peer
        )
        for yy in range(NY):
            m = yy * NC + c
            arrived(r_xf.at[k, yy], s_red.at[k, 1 + yy], r_red.at[k, 1 + yy])
            ref[m, :, x, low_rows, :] = ref[m, :, x, low_rows, :] + r_xf[k, yy]
        push(
            ref.at[over_y, :, x, low_rows], r_ys.at[k], s_red.at[k, 4], r_red.at[k, 4], y_peer
        )

    def reduce_third(k, ref):
        arrived(r_xs.at[k], s_red.at[k, 3], r_red.at[k, 3])
        ref[mine, :, x, top_rows, :] = ref[mine, :, x, top_rows, :] + r_xs[k]
        arrived(r_ys.at[k], s_red.at[k, 4], r_red.at[k, 4])
        ref[mine, :, x, low_rows, :] = ref[mine, :, x, low_rows, :] + r_ys[k]
        for step in range(1, NZ):
            push(
                ref.at[mine, z_at(step), x],
                r_z.at[k, step - 1],
                s_rz.at[k, step],
                r_rz.at[k, step],
                z_peer(step),
            )

    def reduce_last(k, ref, result):
        total = ref[mine, z, x].astype(F32)
        for step in range(1, NZ):
            arrived(r_z.at[k, step - 1], s_rz.at[k, step], r_rz.at[k, step])
            total = total + r_z[k, step - 1].astype(F32)
        result[...] = total

    add_core(0, g_d)
    reduce_first(0, g_d)
    add_core(1, g_i)
    reduce_first(1, g_i)
    forward_result(0)

    xhat = xh1[...]
    normed_grad = acc[...]
    gs[0, 0:1, :] = col_sum(normed_grad * xhat)
    gs[0, 3:4, :] = col_sum(normed_grad)
    first_grad = norm_back(normed_grad, xhat, rs1[...], par_row(0))
    gs[0, 2:3, :] = col_sum(first_grad)
    acc[...] = first_grad
    bl[...] = first_grad.astype(BF16)
    bl_t[...] = bl[...].T
    low_t[...] = xs[...].T
    finish(PILOT)
    reduce_second(0, g_d)

    g_a = w_d

    def back_attention(i, carry):
        m = block_of(i)
        outer(bl_t, ctx.at[m], g_a, m, qkv_cols, width)
        context_grad = nn(bl[...], square(w_a, m, qkv_cols, width)).astype(BF16)
        part = qkv[m]
        for h in range(heads_here):
            lo = h * HEAD_DIM
            q = part[:, lo : lo + HEAD_DIM]
            k = part[:, head_cols + lo : head_cols + lo + HEAD_DIM]
            v = part[:, 2 * head_cols + lo : 2 * head_cols + lo + HEAD_DIM]
            d_ctx = context_grad[:, lo : lo + HEAD_DIM]
            weight = prob[m * heads_here + h]
            d_value = tn(weight.astype(BF16), d_ctx)
            d_prob = nt(d_ctx, v)
            spread = jnp.sum(weight * d_prob, -1, keepdims=True)
            d_score = (weight * (d_prob - spread)).astype(BF16)
            qg[:, lo : lo + HEAD_DIM] = (nn(d_score, k) * scale).astype(BF16)
            qg[:, head_cols + lo : head_cols + lo + HEAD_DIM] = (tn(d_score, q) * scale).astype(BF16)
            qg[:, 2 * head_cols + lo : 2 * head_cols + lo + HEAD_DIM] = d_value.astype(BF16)
        gs[0, pl.ds(QKV_ROW + m, 1), :qkv_cols] = col_sum(qg[...].astype(F32))
        outer(low_t, qg, g_a, m, 0, qkv_cols)
        acc[...] += nt(qg[...], square(w_a, m, 0, qkv_cols))

        @pl.when(i < NY)
        def _():
            to_partner(g_a, 2, i).start()

        return carry

    for chunk, copy in sends:
        if chunk == DOWN:
            copy.wait_send()
    lax.fori_loop(0, GROUP, back_attention, 0)
    small_stage(1, gs, gs_in, 0)
    own[2] = acc[...].astype(BF16)
    send_result(2)
    small_add(1, gs, gs_in, 0)
    small_stage(1, gs, gs_in, 1)
    add_core(2, g_a)
    reduce_first(2, g_a)
    reduce_second(1, g_i)
    small_add(1, gs, gs_in, 1)
    small_stage(1, gs, gs_in, 2)

    acc[...] = jnp.zeros_like(acc)

    def steer(m, carry):
        acc[...] += nt(hid[m], square(w_p, m, 0, width))
        return carry

    lax.fori_loop(0, GROUP, steer, 0)
    tangent = acc[...]
    xhat = xh2[...]
    along = rs2[...] * (tangent - row_mean(tangent) - xhat * row_mean(tangent * xhat))
    own[1] = (par_row(1) * along).astype(BF16)
    send_result(1)
    small_add(1, gs, gs_in, 2)
    small_stage(1, gs, gs_in, 3)
    reduce_third(0, g_d)
    forward_result(2)
    reduce_third(1, g_i)
    reduce_second(2, g_a)
    forward_result(1)
    small_sum[...] = small_last(1, gs, gs_in)
    reduce_last(0, g_d, grad_d)
    reduce_last(1, g_i, grad_i)
    reduce_third(2, g_a)
    reduce_last(2, g_a, grad_a)
    for index in range(3):
        finish_result(index)
    for k, ref in enumerate((g_d, g_i, g_a)):
        for i in range(NY):
            to_partner(ref, k, i).wait_send()
    for chunk, copy in sends:
        if chunk != DOWN:
            copy.wait_send()


def run_layer(inner, lens, tok, cot, shards, small):
    width = tok.shape[1]
    rows = tok.shape[0] // GROUP
    block = width // BLOCKS
    head_cols = width // GROUP
    qkv_cols = 3 * head_cols
    heads = width // HEAD_DIM
    anywhere = pl.BlockSpec(memory_space=pl.ANY)
    vmem = pl.BlockSpec(memory_space=pltpu.VMEM)
    weight = pltpu.VMEM((GROUP, NZ, NX, block, width), BF16)
    act = pltpu.VMEM((rows, width), F32)
    act_low = pltpu.VMEM((rows, width), BF16)
    column = pltpu.VMEM((rows, 1), F32)
    dma = pltpu.SemaphoreType.DMA
    grads = 3
    scratch = (
        [weight] * 6
        + [
            pltpu.VMEM((grads, NY, NZ, NX, block, width), BF16),
            pltpu.VMEM((grads, NZ, NX, BWD_ROWS, width), BF16),
            pltpu.VMEM((grads, NY, NZ, block - BWD_ROWS, width), BF16),
            pltpu.VMEM((grads, NZ, BWD_ROWS, width), BF16),
            pltpu.VMEM((grads, NZ, block - BWD_ROWS, width), BF16),
            pltpu.VMEM((grads, NZ - 1, block, width), BF16),
            pltpu.VMEM((5, SMALL_ROWS, width), F32),
            pltpu.VMEM((6, SMALL_ROWS, width), F32),
            pltpu.VMEM((4, SMALL_ROWS, width), F32),
            pltpu.VMEM((6, SMALL_ROWS, width), F32),
            act_low,
            act_low,
            pltpu.VMEM((GROUP, rows, qkv_cols), BF16),
            pltpu.VMEM((heads, rows, rows), F32),
            pltpu.VMEM((GROUP, rows, head_cols), BF16),
            act,
            act,
            column,
            act_low,
            pltpu.VMEM((width, rows), BF16),
            pltpu.VMEM((GROUP, rows, width), BF16),
            pltpu.VMEM((GROUP, rows, width), F32),
            act,
            column,
            act,
            act_low,
            pltpu.VMEM((width, rows), BF16),
            pltpu.VMEM((rows, qkv_cols), BF16),
            pltpu.VMEM((3, rows, width), BF16),
        ]
        + [dma((7,))]
        + [dma((4, NZ))] * 12
        + [dma((grads, NY))] * 2
        + [dma((grads, 5))] * 2
        + [dma((grads, NZ))] * 2
        + [dma((2, 6))] * 2
        + [dma((3, 3))] * 2
        + [dma((3,))]
    )
    whole = jax.ShapeDtypeStruct(tok.shape, BF16)
    piece = jax.ShapeDtypeStruct((block, width), F32)
    return pl.pallas_call(
        functools.partial(layer_kernel, inner),
        out_shape=(
            whole,
            whole,
            whole,
            piece,
            piece,
            piece,
            jax.ShapeDtypeStruct((SMALL_ROWS, width), F32),
        ),
        in_specs=[pl.BlockSpec(memory_space=pltpu.SMEM)] + [anywhere] * 7,
        out_specs=(anywhere,) * 3 + (vmem,) * 4,
        scratch_shapes=scratch,
        compiler_params=pltpu.CompilerParams(
            collective_id=0, has_side_effects=True, vmem_limit_bytes=67043328
        ),
        name="layer",
    )(lens, tok, cot, *shards, small)


def local(
    tokens, cotangent, lengths, w_qkv, qv_bias, w_out, w_in, in_bias, w_down, pilot, gains, shifts
):
    n_dp = lax.axis_size("dp")
    inner = n_dp // BLOCKS
    groups = [[b * inner + i for i in range(inner)] for b in range(BLOCKS)]
    dp = lax.axis_index("dp")
    mp = lax.axis_index("mp")
    width = tokens.shape[1]
    head_cols = w_out.shape[0]
    local_rows = w_qkv.shape[0]
    shards = (
        jnp.concatenate([w_qkv.reshape(local_rows, 3 * head_cols), w_out.T], 1),
        w_in,
        w_down.T,
        pilot.T,
    )

    spot = jnp.arange(width, dtype=jnp.int32)
    share = gains.shape[1]

    def spread(values, period, offset):
        per = values.shape[1]
        tiled = jnp.tile(values, (1, period // per))
        tiled = jnp.pad(tiled, ((0, 0), (offset, width - offset - period)))
        place = (spot - offset) // per == dp
        return jnp.where(place & (spot >= offset) & (spot < offset + period), tiled, 0)

    head = (mp == 0).astype(F32)
    vectors = spread(jnp.concatenate([gains, shifts], 0).astype(F32), width, 0) * head
    at_mp = (jnp.arange(GROUP) == mp).astype(F32)[:, None]
    hidden_bias = spread(in_bias.astype(F32), width, 0) * at_mp
    pair = qv_bias.reshape(2, -1).astype(F32)
    qkv_bias = (
        spread(pair[0:1], head_cols, 0) + spread(pair[1:2], head_cols, 2 * head_cols)
    ) * at_mp
    small = jnp.concatenate(
        [
            vectors,
            hidden_bias,
            qkv_bias,
            jnp.zeros((SMALL_ROWS - QKV_ROW - GROUP, width), F32),
        ],
        0,
    )
    if inner > 1:
        shards = tuple(
            lax.all_gather(item, "dp", axis=0, tiled=True, axis_index_groups=groups)
            for item in shards
        )
        small = lax.psum(small, "dp", axis_index_groups=groups)

    out, along, input_grad, grad_a, grad_i, grad_d, sums = run_layer(
        inner, lengths, tokens, cotangent, shards, small
    )
    if inner > 1:
        grad_a, grad_i, grad_d = (
            lax.psum_scatter(
                item, "dp", scatter_dimension=0, tiled=True, axis_index_groups=groups
            )
            for item in (grad_a, grad_i, grad_d)
        )
        sums = lax.psum(sums, "dp", axis_index_groups=groups)

    columns = lax.dynamic_slice_in_dim(sums, dp * share, share, 1)
    bias_share = qv_bias.shape[2]
    bias_row = lax.dynamic_slice_in_dim(sums, QKV_ROW + mp, 1, 0)
    grad_qvb = jnp.stack(
        [
            lax.dynamic_slice_in_dim(bias_row, dp * bias_share, bias_share, 1),
            lax.dynamic_slice_in_dim(
                bias_row, 2 * head_cols + dp * bias_share, bias_share, 1
            ),
        ]
    )
    return (
        out,
        input_grad.astype(F32),
        along.astype(F32),
        grad_a[:, : 3 * head_cols].reshape(local_rows, 3, head_cols),
        grad_qvb,
        grad_a[:, 3 * head_cols :].T,
        grad_i,
        lax.dynamic_slice_in_dim(columns, BIAS_ROW + mp, 1, 0),
        grad_d.T,
        columns[0:2],
        columns[2:6],
    )


def solution(mesh):
    in_specs = (
        P("dp", None),
        P("dp", None),
        P("dp"),
        P("dp", None, "mp"),
        P(None, "mp", "dp"),
        P("mp", "dp"),
        P("dp", "mp"),
        P("mp", "dp"),
        P("mp", "dp"),
        P("mp", "dp"),
        P(None, "dp"),
        P(None, "dp"),
    )
    out_specs = (
        P("dp", None),
        P("dp", None),
        P("dp", None),
        P("dp", None, "mp"),
        P(None, "mp", "dp"),
        P("mp", "dp"),
        P("dp", "mp"),
        P("mp", "dp"),
        P("mp", "dp"),
        P(None, "dp"),
        P(None, "dp"),
    )
    return jax.shard_map(local, mesh=mesh, in_specs=in_specs, out_specs=out_specs, check_vma=False)
```

```python
import functools
import math

import jax
import jax.numpy as jnp
from jax import lax
from jax.experimental import pallas as pl
from jax.experimental.pallas import tpu as pltpu
from jax.sharding import PartitionSpec as P

HEAD_DIM = 64
SEQ_LEN = 256
EPSILON = 1e-06
NZ, NX, NY, NC = 4, 2, 2, 2
BLOCKS = NZ * NX
GROUP = NY * NC
SMALL_ROWS = 16
BIAS_ROW = 6
QKV_ROW = BIAS_ROW + GROUP
FWD_ROWS = 48
BWD_ROWS = 48
F32 = jnp.float32
BF16 = jnp.bfloat16
QKV, IN, DOWN, PILOT = range(4)


def nt(a, b):
    return lax.dot_general(a, b, (((1,), (1,)), ((), ())), preferred_element_type=F32)


def tn(a, b):
    return lax.dot_general(a, b, (((0,), (0,)), ((), ())), preferred_element_type=F32)


def nn(a, b):
    return jnp.dot(a, b, preferred_element_type=F32)


def row_mean(v):
    return jnp.mean(v, -1, keepdims=True)


def col_sum(v):
    return jnp.sum(v, 0, keepdims=True)


def layer_kernel(
    inner,
    lens,
    tok,
    cot,
    shard_a,
    shard_i,
    shard_d,
    shard_p,
    small,
    out_o,
    along_o,
    ig_o,
    grad_a,
    grad_i,
    grad_d,
    small_sum,
    w_a,
    w_i,
    w_d,
    w_p,
    g_i,
    g_d,
    r_core,
    r_yf,
    r_xf,
    r_xs,
    r_ys,
    r_z,
    par,
    par_in,
    gs,
    gs_in,
    xs,
    cots,
    qkv,
    prob,
    ctx,
    acc,
    xh1,
    rs1,
    low,
    low_t,
    hid,
    gder,
    xh2,
    rs2,
    sgrad,
    bl,
    bl_t,
    qg,
    own,
    s_load,
    s_z,
    r_zs,
    s_x,
    r_x,
    s_y,
    r_y,
    s_dx,
    r_dx,
    s_dy,
    r_dy,
    s_c,
    r_c,
    s_rc,
    r_rc,
    s_red,
    r_red,
    s_rz,
    r_rz,
    s_sm,
    r_sm,
    s_out,
    r_out,
    s_own,
):
    weights = (w_a, w_i, w_d, w_p)
    shards = (shard_a, shard_i, shard_d, shard_p)
    width = xs.shape[1]
    block = w_a.shape[3]
    head_cols = ctx.shape[2]
    qkv_cols = 3 * head_cols
    heads_here = head_cols // HEAD_DIM
    rows = xs.shape[0]
    scale = HEAD_DIM ** (-0.5)

    dp = lax.axis_index("dp")
    mp = lax.axis_index("mp")
    spot = dp // inner
    rest = dp - spot * inner
    z, x = spot // NX, spot % NX
    y, c = mp // NC, mp % NC
    far_y, far_x, far_c = 1 - y, 1 - x, 1 - c
    mine = mp
    over_y = far_y * NC + c
    x_peer = {"dp": (z * NX + far_x) * inner + rest, "mp": mp}
    y_peer = {"dp": dp, "mp": over_y}
    c_peer = {"dp": dp, "mp": y * NC + far_c}

    def z_at(step):
        return (z + step) % NZ

    def z_from(step):
        return (z + NZ - step) % NZ

    def z_peer(step):
        return {"dp": (z_at(step) * NX + x) * inner + rest, "mp": mp}

    sends = []

    def remote(src, dst, send, recv, peer):
        return pltpu.make_async_remote_copy(
            src_ref=src,
            dst_ref=dst,
            send_sem=send,
            recv_sem=recv,
            device_id=peer,
            device_id_type=pl.DeviceIdType.MESH,
        )

    def push(src, dst, send, recv, peer, chunk=None):
        copy = remote(src, dst, send, recv, peer)
        copy.start()
        sends.append((chunk, copy))

    def arrived(dst, send, recv):
        remote(dst, dst, send, recv, c_peer).wait_recv()

    barrier = pltpu.get_barrier_semaphore()
    peers = [x_peer, y_peer, c_peer] + [z_peer(step) for step in range(1, NZ)]
    for peer in peers:
        pl.semaphore_signal(barrier, inc=1, device_id=peer, device_id_type=pl.DeviceIdType.MESH)
    pl.semaphore_wait(barrier, len(peers))

    loads = []
    for k in range(4):
        loads.append(
            pltpu.make_async_copy(shards[k], weights[k].at[mine, z, x], s_load.at[k])
        )
    my_rows = pl.ds(mp * rows, rows)
    loads.append(pltpu.make_async_copy(tok.at[my_rows], xs, s_load.at[4]))
    loads.append(pltpu.make_async_copy(cot.at[my_rows], cots, s_load.at[5]))

    def send_z(k):
        for step in range(1, NZ):
            push(
                shards[k],
                weights[k].at[mine, z, x],
                s_z.at[k, step],
                r_zs.at[k, step],
                z_peer(step),
                k,
            )

    def send_own(k):
        for sem_s, sem_r, peer in ((s_x, r_x, x_peer), (s_y, r_y, y_peer)):
            push(shards[k], weights[k].at[mine, z, x], sem_s.at[k, 0], sem_r.at[k, 0], peer, k)

    def forward_z(k, step):
        src = weights[k].at[mine, z_from(step), x]
        arrived(src, s_z.at[k, step], r_zs.at[k, step])
        push(src, src, s_x.at[k, step], r_x.at[k, step], x_peer, k)
        push(src, src, s_y.at[k, step], r_y.at[k, step], y_peer, k)

    first = pl.ds(0, FWD_ROWS)
    second = pl.ds(FWD_ROWS, block - FWD_ROWS)

    def forward_diagonal(k, step):
        from_x = weights[k].at[mine, z_from(step), far_x]
        arrived(from_x, s_x.at[k, step], r_x.at[k, step])
        part = weights[k].at[mine, z_from(step), far_x, first]
        push(part, part, s_dy.at[k, step], r_dy.at[k, step], y_peer, k)
        from_y = weights[k].at[over_y, z_from(step), x]
        arrived(from_y, s_y.at[k, step], r_y.at[k, step])
        part = weights[k].at[over_y, z_from(step), x, second]
        push(part, part, s_dx.at[k, step], r_dx.at[k, step], x_peer, k)

    def to_core(k, index, block_index, column):
        src = weights[k].at[block_index, :, column]
        push(src, src, s_c.at[k, index], r_c.at[k, index], c_peer, k)

    def finish(k):
        for step in range(NZ):
            arrived(
                weights[k].at[over_y, z_from(step), far_x, first],
                s_dy.at[k, step],
                r_dy.at[k, step],
            )
            arrived(
                weights[k].at[over_y, z_from(step), far_x, second],
                s_dx.at[k, step],
                r_dx.at[k, step],
            )
        to_core(k, 3, over_y, far_x)
        for index, (block_index, column) in enumerate(
            (
                (y * NC + far_c, x),
                (y * NC + far_c, far_x),
                (far_y * NC + far_c, x),
                (far_y * NC + far_c, far_x),
            )
        ):
            arrived(
                weights[k].at[block_index, :, column], s_c.at[k, index], r_c.at[k, index]
            )

    def small_stage(which, buf, buf_in, stage):
        if stage < 3:
            peer = (c_peer, y_peer, x_peer)[stage]
            push(buf.at[stage], buf_in.at[stage], s_sm.at[which, stage], r_sm.at[which, stage], peer)
        else:
            for step in range(1, NZ):
                push(
                    buf.at[3],
                    buf_in.at[2 + step],
                    s_sm.at[which, 2 + step],
                    r_sm.at[which, 2 + step],
                    z_peer(step),
                )

    def small_add(which, buf, buf_in, stage):
        arrived(buf_in.at[stage], s_sm.at[which, stage], r_sm.at[which, stage])
        buf[stage + 1] = buf[stage] + buf_in[stage]

    def small_last(which, buf, buf_in):
        for step in range(1, NZ):
            arrived(buf_in.at[2 + step], s_sm.at[which, 2 + step], r_sm.at[which, 2 + step])
        total = jnp.zeros(buf.shape[1:], F32)
        for place in range(NZ):
            term = buf[3]
            for step in range(1, NZ):
                term = jnp.where(z_from(step) == place, buf_in[2 + step], term)
            total = total + term
        return total

    load_small = pltpu.make_async_copy(small, par.at[0], s_load.at[6])
    load_small.start()
    send_z(QKV)
    for copy in loads:
        copy.start()
    send_own(QKV)
    load_small.wait()
    small_stage(0, par, par_in, 0)
    send_z(IN)
    small_add(0, par, par_in, 0)
    small_stage(0, par, par_in, 1)
    forward_z(QKV, 1)
    small_add(0, par, par_in, 1)
    small_stage(0, par, par_in, 2)
    forward_z(QKV, 3)
    small_add(0, par, par_in, 2)
    small_stage(0, par, par_in, 3)
    forward_z(QKV, 2)
    send_z(DOWN)
    send_z(PILOT)
    for copy in loads:
        copy.wait()
    to_core(QKV, 0, mine, x)
    send_own(IN)
    forward_diagonal(QKV, 0)
    forward_diagonal(QKV, 1)
    forward_z(IN, 1)
    forward_diagonal(QKV, 3)
    forward_z(IN, 3)
    forward_diagonal(QKV, 2)
    to_core(QKV, 1, mine, far_x)
    to_core(QKV, 2, over_y, x)
    forward_z(IN, 2)
    to_core(IN, 0, mine, x)
    par[4] = small_last(0, par, par_in)
    finish(QKV)

    length = lens[mp]
    key_keep = lax.broadcasted_iota(jnp.int32, (rows, rows), 1) < length
    row_keep = (lax.broadcasted_iota(jnp.int32, (rows, 1), 0) < length).astype(F32)

    def par_row(index):
        return par[4, index : index + 1, :]

    def square(ref, m, start, stop):
        value = ref[m, :, :, :, start:stop]
        return value.reshape(width, stop - start)

    def project(m, carry):
        bias = par[4, pl.ds(QKV_ROW + m, 1), :qkv_cols]
        qkv[m] = (nn(xs[...], square(w_a, m, 0, qkv_cols)) + bias).astype(BF16)
        return carry

    lax.fori_loop(0, GROUP, project, 0)

    def attend(m, carry):
        part = qkv[m]
        for h in range(heads_here):
            lo = h * HEAD_DIM
            q = part[:, lo : lo + HEAD_DIM]
            k = part[:, head_cols + lo : head_cols + lo + HEAD_DIM]
            v = part[:, 2 * head_cols + lo : 2 * head_cols + lo + HEAD_DIM]
            score = jnp.where(key_keep, nt(q, k) * scale, -1000000000.0)
            expo = jnp.exp(score - jnp.max(score, -1, keepdims=True))
            weight = expo / jnp.sum(expo, -1, keepdims=True)
            prob[m * heads_here + h] = weight
            ctx[m, :, lo : lo + HEAD_DIM] = nn(weight.astype(BF16), v).astype(BF16)
        return carry

    def next_chunk(k, part):
        if part == 0:
            if k < PILOT:
                send_own(k + 1)
            forward_diagonal(k, 0)
            forward_diagonal(k, 1)
            if k < PILOT:
                forward_z(k + 1, 1)
            return
        forward_diagonal(k, 3)
        if k < PILOT:
            forward_z(k + 1, 3)
        forward_diagonal(k, 2)
        to_core(k, 1, mine, far_x)
        to_core(k, 2, over_y, x)
        if k < PILOT:
            forward_z(k + 1, 2)
            to_core(k + 1, 0, mine, x)

    next_chunk(IN, 0)
    lax.fori_loop(0, GROUP, attend, 0)
    next_chunk(IN, 1)

    acc[...] = jnp.zeros_like(acc)

    def attended(m, carry):
        acc[...] += nt(ctx[m], square(w_a, m, qkv_cols, width))
        return carry

    lax.fori_loop(0, GROUP, attended, 0)
    opening = xs[...].astype(F32) + acc[...] + par_row(2)
    centered = opening - row_mean(opening)
    rstd = lax.rsqrt(row_mean(centered * centered) + EPSILON)
    rs1[...] = rstd
    xhat = centered * rstd
    xh1[...] = xhat
    normed_low = (xhat * par_row(0) + par_row(3)).astype(BF16)
    low[...] = normed_low
    finish(IN)
    next_chunk(DOWN, 0)

    def expand(m, carry):
        pre = nn(low[...], square(w_i, m, 0, width)) + par[4, pl.ds(BIAS_ROW + m, 1), :]
        gate = 0.5 + 0.5 * lax.erf(pre * math.sqrt(0.5))
        hid[m] = (pre * gate).astype(BF16)
        gder[m] = gate + pre * (jnp.exp(-0.5 * pre * pre) * (1.0 / math.sqrt(2.0 * math.pi)))
        return carry

    lax.fori_loop(0, GROUP, expand, 0)
    low_t[...] = low[...].T
    next_chunk(DOWN, 1)
    finish(DOWN)

    acc[...] = xh1[...] * par_row(0) + par_row(3) + par_row(4)

    def contract(m, carry):
        acc[...] += nt(hid[m], square(w_d, m, 0, width))
        return carry

    lax.fori_loop(0, GROUP, contract, 0)
    next_chunk(PILOT, 0)

    stream = acc[...]
    centered = stream - row_mean(stream)
    rstd = lax.rsqrt(row_mean(centered * centered) + EPSILON)
    rs2[...] = rstd
    xhat = centered * rstd
    xh2[...] = xhat
    own[0] = (xhat * par_row(1) + par_row(5)).astype(BF16)

    outs = (out_o, along_o, ig_o)

    def send_result(index):
        dst = outs[index].at[my_rows]
        pltpu.make_async_copy(own.at[index], dst, s_own.at[index]).start()
        push(own.at[index], dst, s_out.at[index, 0], r_out.at[index, 0], y_peer)
        push(own.at[index], dst, s_out.at[index, 1], r_out.at[index, 1], c_peer)

    def forward_result(index):
        part = outs[index].at[pl.ds(over_y * rows, rows)]
        arrived(part, s_out.at[index, 0], r_out.at[index, 0])
        push(part, part, s_out.at[index, 2], r_out.at[index, 2], c_peer)

    def finish_result(index):
        pltpu.make_async_copy(own.at[index], outs[index].at[my_rows], s_own.at[index]).wait()
        near = outs[index].at[pl.ds((y * NC + far_c) * rows, rows)]
        arrived(near, s_out.at[index, 1], r_out.at[index, 1])
        far = outs[index].at[pl.ds((far_y * NC + far_c) * rows, rows)]
        arrived(far, s_out.at[index, 2], r_out.at[index, 2])

    send_result(0)

    gs[0] = jnp.zeros(gs.shape[1:], F32)

    def norm_back(grad, xhat, rstd, gain):
        hat = grad * gain
        return rstd * (hat - row_mean(hat) - xhat * row_mean(hat * xhat))

    masked = cots[...].astype(F32) * row_keep
    xhat = xh2[...]
    gs[0, 1:2, :] = col_sum(masked * xhat)
    gs[0, 5:6, :] = col_sum(masked)
    stream_grad = norm_back(masked, xhat, rs2[...], par_row(1))
    gs[0, 4:5, :] = col_sum(stream_grad)
    sgrad[...] = stream_grad
    bl[...] = stream_grad.astype(BF16)
    bl_t[...] = bl[...].T
    acc[...] = stream_grad

    def block_of(i):
        return i * NC + far_c if i < NY else (i - NY) * NC + c

    slab = NX * block

    def outer(left_t, right, ref, m, start, stop):
        def one(zz, carry):
            top = pl.multiple_of(zz * slab, slab)
            value = nn(left_t[pl.ds(top, slab), :], right[...])
            ref[m, zz, :, :, start:stop] = value.astype(BF16).reshape(NX, block, stop - start)
            return carry

        lax.fori_loop(0, NZ, one, 0)

    def to_partner(ref, k, i):
        src = ref.at[i * NC + far_c]
        copy = remote(src, r_core.at[k, i], s_rc.at[k, i], r_rc.at[k, i], c_peer)
        return copy

    pre_low = own.at[1]

    def back_ff(i):
        m = block_of(i)
        outer(bl_t, hid.at[m], g_d, m, 0, width)
        grad = nn(bl[...], square(w_d, m, 0, width)) * gder[m]
        pre_low[...] = grad.astype(BF16)
        gs[0, pl.ds(BIAS_ROW + m, 1), :] = col_sum(pre_low[...].astype(F32))
        outer(low_t, pre_low, g_i, m, 0, width)
        acc[...] += nt(pre_low[...], square(w_i, m, 0, width))

        if i < NY:
            to_partner(g_d, 0, i).start()
            to_partner(g_i, 1, i).start()

    for i in range(GROUP):
        back_ff(i)
        if i == 0:
            next_chunk(PILOT, 1)

    top_rows = pl.ds(0, BWD_ROWS)
    low_rows = pl.ds(BWD_ROWS, block - BWD_ROWS)

    def add_core(k, ref):
        for yy in range(NY):
            m = yy * NC + c
            to_partner(ref, k, yy).wait_recv()

            def one(zz, carry):
                ref[m, zz] = ref[m, zz] + r_core[k, yy, zz]
                return carry

            lax.fori_loop(0, NZ, one, 0)

    def reduce_first(k, ref):
        push(
            ref.at[over_y, :, :, top_rows], r_yf.at[k], s_red.at[k, 0], r_red.at[k, 0], y_peer
        )
        for yy in range(NY):
            push(
                ref.at[yy * NC + c, :, far_x, low_rows],
                r_xf.at[k, yy],
                s_red.at[k, 1 + yy],
                r_red.at[k, 1 + yy],
                x_peer,
            )

    def reduce_second(k, ref):
        arrived(r_yf.at[k], s_red.at[k, 0], r_red.at[k, 0])
        ref[mine, :, :, top_rows, :] = ref[mine, :, :, top_rows, :] + r_yf[k]
        push(
            ref.at[mine, :, far_x, top_rows], r_xs.at[k], s_red.at[k, 3], r_red.at[k, 3], x_peer
        )
        for yy in range(NY):
            m = yy * NC + c
            arrived(r_xf.at[k, yy], s_red.at[k, 1 + yy], r_red.at[k, 1 + yy])
            ref[m, :, x, low_rows, :] = ref[m, :, x, low_rows, :] + r_xf[k, yy]
        push(
            ref.at[over_y, :, x, low_rows], r_ys.at[k], s_red.at[k, 4], r_red.at[k, 4], y_peer
        )

    def reduce_third(k, ref):
        arrived(r_xs.at[k], s_red.at[k, 3], r_red.at[k, 3])
        ref[mine, :, x, top_rows, :] = ref[mine, :, x, top_rows, :] + r_xs[k]
        arrived(r_ys.at[k], s_red.at[k, 4], r_red.at[k, 4])
        ref[mine, :, x, low_rows, :] = ref[mine, :, x, low_rows, :] + r_ys[k]
        for step in range(1, NZ):
            push(
                ref.at[mine, z_at(step), x],
                r_z.at[k, step - 1],
                s_rz.at[k, step],
                r_rz.at[k, step],
                z_peer(step),
            )

    def reduce_last(k, ref, result):
        total = ref[mine, z, x].astype(F32)
        for step in range(1, NZ):
            arrived(r_z.at[k, step - 1], s_rz.at[k, step], r_rz.at[k, step])
            total = total + r_z[k, step - 1].astype(F32)
        result[...] = total

    add_core(0, g_d)
    reduce_first(0, g_d)
    add_core(1, g_i)
    reduce_first(1, g_i)
    forward_result(0)

    xhat = xh1[...]
    normed_grad = acc[...]
    gs[0, 0:1, :] = col_sum(normed_grad * xhat)
    gs[0, 3:4, :] = col_sum(normed_grad)
    first_grad = norm_back(normed_grad, xhat, rs1[...], par_row(0))
    gs[0, 2:3, :] = col_sum(first_grad)
    acc[...] = first_grad
    bl[...] = first_grad.astype(BF16)
    bl_t[...] = bl[...].T
    low_t[...] = xs[...].T
    g_a = w_d

    def back_attention(i):
        m = block_of(i)
        outer(bl_t, ctx.at[m], g_a, m, qkv_cols, width)
        context_grad = nn(bl[...], square(w_a, m, qkv_cols, width)).astype(BF16)
        part = qkv[m]
        for h in range(heads_here):
            lo = h * HEAD_DIM
            q = part[:, lo : lo + HEAD_DIM]
            k = part[:, head_cols + lo : head_cols + lo + HEAD_DIM]
            v = part[:, 2 * head_cols + lo : 2 * head_cols + lo + HEAD_DIM]
            d_ctx = context_grad[:, lo : lo + HEAD_DIM]
            weight = prob[m * heads_here + h]
            d_value = tn(weight.astype(BF16), d_ctx)
            d_prob = nt(d_ctx, v)
            spread = jnp.sum(weight * d_prob, -1, keepdims=True)
            d_score = (weight * (d_prob - spread)).astype(BF16)
            qg[:, lo : lo + HEAD_DIM] = (nn(d_score, k) * scale).astype(BF16)
            qg[:, head_cols + lo : head_cols + lo + HEAD_DIM] = (tn(d_score, q) * scale).astype(BF16)
            qg[:, 2 * head_cols + lo : 2 * head_cols + lo + HEAD_DIM] = d_value.astype(BF16)
        gs[0, pl.ds(QKV_ROW + m, 1), :qkv_cols] = col_sum(qg[...].astype(F32))
        outer(low_t, qg, g_a, m, 0, qkv_cols)
        acc[...] += nt(qg[...], square(w_a, m, 0, qkv_cols))

        if i < NY:
            to_partner(g_a, 2, i).start()

    for chunk, copy in sends:
        if chunk == DOWN:
            copy.wait_send()
    for i in range(GROUP):
        back_attention(i)
        if i == 2:
            finish(PILOT)
            reduce_second(0, g_d)
    own[2] = acc[...].astype(BF16)
    add_core(2, g_a)
    reduce_first(2, g_a)
    send_result(2)
    small_stage(1, gs, gs_in, 0)
    reduce_second(1, g_i)
    small_add(1, gs, gs_in, 0)
    small_stage(1, gs, gs_in, 1)

    acc[...] = jnp.zeros_like(acc)

    def steer(m, carry):
        acc[...] += nt(hid[m], square(w_p, m, 0, width))
        return carry

    lax.fori_loop(0, GROUP, steer, 0)
    tangent = acc[...]
    xhat = xh2[...]
    along = rs2[...] * (tangent - row_mean(tangent) - xhat * row_mean(tangent * xhat))
    own[1] = (par_row(1) * along).astype(BF16)
    send_result(1)
    reduce_third(0, g_d)
    small_add(1, gs, gs_in, 1)
    small_stage(1, gs, gs_in, 2)
    reduce_second(2, g_a)
    reduce_third(1, g_i)
    small_add(1, gs, gs_in, 2)
    small_stage(1, gs, gs_in, 3)
    reduce_last(0, g_d, grad_d)
    forward_result(2)
    reduce_third(2, g_a)
    forward_result(1)
    reduce_last(1, g_i, grad_i)
    small_sum[...] = small_last(1, gs, gs_in)
    reduce_last(2, g_a, grad_a)
    for index in range(3):
        finish_result(index)
    for k, ref in enumerate((g_d, g_i, g_a)):
        for i in range(NY):
            to_partner(ref, k, i).wait_send()
    for chunk, copy in sends:
        if chunk != DOWN:
            copy.wait_send()


def run_layer(inner, lens, tok, cot, shards, small):
    width = tok.shape[1]
    rows = tok.shape[0] // GROUP
    block = width // BLOCKS
    head_cols = width // GROUP
    qkv_cols = 3 * head_cols
    heads = width // HEAD_DIM
    anywhere = pl.BlockSpec(memory_space=pl.ANY)
    vmem = pl.BlockSpec(memory_space=pltpu.VMEM)
    weight = pltpu.VMEM((GROUP, NZ, NX, block, width), BF16)
    act = pltpu.VMEM((rows, width), F32)
    act_low = pltpu.VMEM((rows, width), BF16)
    column = pltpu.VMEM((rows, 1), F32)
    dma = pltpu.SemaphoreType.DMA
    grads = 3
    scratch = (
        [weight] * 6
        + [
            pltpu.VMEM((grads, NY, NZ, NX, block, width), BF16),
            pltpu.VMEM((grads, NZ, NX, BWD_ROWS, width), BF16),
            pltpu.VMEM((grads, NY, NZ, block - BWD_ROWS, width), BF16),
            pltpu.VMEM((grads, NZ, BWD_ROWS, width), BF16),
            pltpu.VMEM((grads, NZ, block - BWD_ROWS, width), BF16),
            pltpu.VMEM((grads, NZ - 1, block, width), BF16),
            pltpu.VMEM((5, SMALL_ROWS, width), F32),
            pltpu.VMEM((6, SMALL_ROWS, width), F32),
            pltpu.VMEM((4, SMALL_ROWS, width), F32),
            pltpu.VMEM((6, SMALL_ROWS, width), F32),
            act_low,
            act_low,
            pltpu.VMEM((GROUP, rows, qkv_cols), BF16),
            pltpu.VMEM((heads, rows, rows), F32),
            pltpu.VMEM((GROUP, rows, head_cols), BF16),
            act,
            act,
            column,
            act_low,
            pltpu.VMEM((width, rows), BF16),
            pltpu.VMEM((GROUP, rows, width), BF16),
            pltpu.VMEM((GROUP, rows, width), F32),
            act,
            column,
            act,
            act_low,
            pltpu.VMEM((width, rows), BF16),
            pltpu.VMEM((rows, qkv_cols), BF16),
            pltpu.VMEM((3, rows, width), BF16),
        ]
        + [dma((7,))]
        + [dma((4, NZ))] * 12
        + [dma((grads, NY))] * 2
        + [dma((grads, 5))] * 2
        + [dma((grads, NZ))] * 2
        + [dma((2, 6))] * 2
        + [dma((3, 3))] * 2
        + [dma((3,))]
    )
    whole = jax.ShapeDtypeStruct(tok.shape, BF16)
    piece = jax.ShapeDtypeStruct((block, width), F32)
    return pl.pallas_call(
        functools.partial(layer_kernel, inner),
        out_shape=(
            whole,
            whole,
            whole,
            piece,
            piece,
            piece,
            jax.ShapeDtypeStruct((SMALL_ROWS, width), F32),
        ),
        in_specs=[pl.BlockSpec(memory_space=pltpu.SMEM)] + [anywhere] * 7,
        out_specs=(anywhere,) * 3 + (vmem,) * 4,
        scratch_shapes=scratch,
        compiler_params=pltpu.CompilerParams(
            collective_id=0, has_side_effects=True, vmem_limit_bytes=67043328
        ),
        name="layer",
    )(lens, tok, cot, *shards, small)


def local(
    tokens, cotangent, lengths, w_qkv, qv_bias, w_out, w_in, in_bias, w_down, pilot, gains, shifts
):
    n_dp = lax.axis_size("dp")
    inner = n_dp // BLOCKS
    groups = [[b * inner + i for i in range(inner)] for b in range(BLOCKS)]
    dp = lax.axis_index("dp")
    mp = lax.axis_index("mp")
    width = tokens.shape[1]
    head_cols = w_out.shape[0]
    local_rows = w_qkv.shape[0]
    shards = (
        jnp.concatenate([w_qkv.reshape(local_rows, 3 * head_cols), w_out.T], 1),
        w_in,
        w_down.T,
        pilot.T,
    )

    spot = jnp.arange(width, dtype=jnp.int32)
    share = gains.shape[1]

    def spread(values, period, offset):
        per = values.shape[1]
        tiled = jnp.tile(values, (1, period // per))
        tiled = jnp.pad(tiled, ((0, 0), (offset, width - offset - period)))
        place = (spot - offset) // per == dp
        return jnp.where(place & (spot >= offset) & (spot < offset + period), tiled, 0)

    head = (mp == 0).astype(F32)
    vectors = spread(jnp.concatenate([gains, shifts], 0).astype(F32), width, 0) * head
    at_mp = (jnp.arange(GROUP) == mp).astype(F32)[:, None]
    hidden_bias = spread(in_bias.astype(F32), width, 0) * at_mp
    pair = qv_bias.reshape(2, -1).astype(F32)
    qkv_bias = (
        spread(pair[0:1], head_cols, 0) + spread(pair[1:2], head_cols, 2 * head_cols)
    ) * at_mp
    small = jnp.concatenate(
        [
            vectors,
            hidden_bias,
            qkv_bias,
            jnp.zeros((SMALL_ROWS - QKV_ROW - GROUP, width), F32),
        ],
        0,
    )
    if inner > 1:
        shards = tuple(
            lax.all_gather(item, "dp", axis=0, tiled=True, axis_index_groups=groups)
            for item in shards
        )
        small = lax.psum(small, "dp", axis_index_groups=groups)

    out, along, input_grad, grad_a, grad_i, grad_d, sums = run_layer(
        inner, lengths, tokens, cotangent, shards, small
    )
    if inner > 1:
        grad_a, grad_i, grad_d = (
            lax.psum_scatter(
                item, "dp", scatter_dimension=0, tiled=True, axis_index_groups=groups
            )
            for item in (grad_a, grad_i, grad_d)
        )
        sums = lax.psum(sums, "dp", axis_index_groups=groups)

    columns = lax.dynamic_slice_in_dim(sums, dp * share, share, 1)
    bias_share = qv_bias.shape[2]
    bias_row = lax.dynamic_slice_in_dim(sums, QKV_ROW + mp, 1, 0)
    grad_qvb = jnp.stack(
        [
            lax.dynamic_slice_in_dim(bias_row, dp * bias_share, bias_share, 1),
            lax.dynamic_slice_in_dim(
                bias_row, 2 * head_cols + dp * bias_share, bias_share, 1
            ),
        ]
    )
    return (
        out,
        input_grad.astype(F32),
        along.astype(F32),
        grad_a[:, : 3 * head_cols].reshape(local_rows, 3, head_cols),
        grad_qvb,
        grad_a[:, 3 * head_cols :].T,
        grad_i,
        lax.dynamic_slice_in_dim(columns, BIAS_ROW + mp, 1, 0),
        grad_d.T,
        columns[0:2],
        columns[2:6],
    )


def solution(mesh):
    in_specs = (
        P("dp", None),
        P("dp", None),
        P("dp"),
        P("dp", None, "mp"),
        P(None, "mp", "dp"),
        P("mp", "dp"),
        P("dp", "mp"),
        P("mp", "dp"),
        P("mp", "dp"),
        P("mp", "dp"),
        P(None, "dp"),
        P(None, "dp"),
    )
    out_specs = (
        P("dp", None),
        P("dp", None),
        P("dp", None),
        P("dp", None, "mp"),
        P(None, "mp", "dp"),
        P("mp", "dp"),
        P("dp", "mp"),
        P("mp", "dp"),
        P("mp", "dp"),
        P(None, "dp"),
        P(None, "dp"),
    )
    return jax.shard_map(local, mesh=mesh, in_specs=in_specs, out_specs=out_specs, check_vma=False)
```

```python
import functools
import math

import jax
import jax.numpy as jnp
from jax import lax
from jax.experimental import pallas as pl
from jax.experimental.pallas import tpu as pltpu
from jax.sharding import PartitionSpec as P

HEAD_DIM = 64
SEQ_LEN = 256
EPSILON = 1e-06
NZ, NX, NY, NC = 4, 2, 2, 2
BLOCKS = NZ * NX
GROUP = NY * NC
SMALL_ROWS = 16
BIAS_ROW = 6
QKV_ROW = BIAS_ROW + GROUP
FWD_ROWS = 48
BWD_ROWS = 48
F32 = jnp.float32
BF16 = jnp.bfloat16
QKV, IN, DOWN, PILOT = range(4)


def nt(a, b):
    return lax.dot_general(a, b, (((1,), (1,)), ((), ())), preferred_element_type=F32)


def tn(a, b):
    return lax.dot_general(a, b, (((0,), (0,)), ((), ())), preferred_element_type=F32)


def nn(a, b):
    return jnp.dot(a, b, preferred_element_type=F32)


def row_mean(v):
    return jnp.mean(v, -1, keepdims=True)


def col_sum(v):
    return jnp.sum(v, 0, keepdims=True)


def layer_kernel(
    inner,
    lens,
    tok,
    cot,
    shard_a,
    shard_i,
    shard_d,
    shard_p,
    small,
    out_o,
    along_o,
    ig_o,
    grad_a,
    grad_i,
    grad_d,
    small_sum,
    w_a,
    w_i,
    w_d,
    w_p,
    g_i,
    g_d,
    r_core,
    r_yf,
    r_xf,
    r_xs,
    r_ys,
    r_z,
    par,
    par_in,
    gs,
    gs_in,
    xs,
    cots,
    qkv,
    prob,
    ctx,
    acc,
    xh1,
    rs1,
    low,
    low_t,
    hid,
    gder,
    xh2,
    rs2,
    sgrad,
    bl,
    bl_t,
    qg,
    own,
    s_load,
    s_z,
    r_zs,
    s_x,
    r_x,
    s_y,
    r_y,
    s_dx,
    r_dx,
    s_dy,
    r_dy,
    s_c,
    r_c,
    s_rc,
    r_rc,
    s_red,
    r_red,
    s_rz,
    r_rz,
    s_sm,
    r_sm,
    s_out,
    r_out,
    s_own,
):
    weights = (w_a, w_i, w_d, w_p)
    shards = (shard_a, shard_i, shard_d, shard_p)
    width = xs.shape[1]
    block = w_a.shape[3]
    head_cols = ctx.shape[2]
    qkv_cols = 3 * head_cols
    heads_here = head_cols // HEAD_DIM
    rows = xs.shape[0]
    scale = HEAD_DIM ** (-0.5)

    dp = lax.axis_index("dp")
    mp = lax.axis_index("mp")
    spot = dp // inner
    rest = dp - spot * inner
    z, x = spot // NX, spot % NX
    y, c = mp // NC, mp % NC
    far_y, far_x, far_c = 1 - y, 1 - x, 1 - c
    mine = mp
    over_y = far_y * NC + c
    x_peer = {"dp": (z * NX + far_x) * inner + rest, "mp": mp}
    y_peer = {"dp": dp, "mp": over_y}
    c_peer = {"dp": dp, "mp": y * NC + far_c}

    def z_at(step):
        return (z + step) % NZ

    def z_from(step):
        return (z + NZ - step) % NZ

    def z_peer(step):
        return {"dp": (z_at(step) * NX + x) * inner + rest, "mp": mp}

    sends = []

    def remote(src, dst, send, recv, peer):
        return pltpu.make_async_remote_copy(
            src_ref=src,
            dst_ref=dst,
            send_sem=send,
            recv_sem=recv,
            device_id=peer,
            device_id_type=pl.DeviceIdType.MESH,
        )

    def push(src, dst, send, recv, peer, chunk=None):
        copy = remote(src, dst, send, recv, peer)
        copy.start()
        sends.append((chunk, copy))

    def arrived(dst, send, recv):
        remote(dst, dst, send, recv, c_peer).wait_recv()

    barrier = pltpu.get_barrier_semaphore()
    peers = [x_peer, y_peer, c_peer] + [z_peer(step) for step in range(1, NZ)]
    for peer in peers:
        pl.semaphore_signal(barrier, inc=1, device_id=peer, device_id_type=pl.DeviceIdType.MESH)
    pl.semaphore_wait(barrier, len(peers))

    loads = []
    for k in range(4):
        loads.append(
            pltpu.make_async_copy(shards[k], weights[k].at[mine, z, x], s_load.at[k])
        )
    my_rows = pl.ds(mp * rows, rows)
    loads.append(pltpu.make_async_copy(tok.at[my_rows], xs, s_load.at[4]))
    loads.append(pltpu.make_async_copy(cot.at[my_rows], cots, s_load.at[5]))

    def send_z(k):
        for step in range(1, NZ):
            push(
                shards[k],
                weights[k].at[mine, z, x],
                s_z.at[k, step],
                r_zs.at[k, step],
                z_peer(step),
                k,
            )

    def send_own(k):
        for sem_s, sem_r, peer in ((s_x, r_x, x_peer), (s_y, r_y, y_peer)):
            push(shards[k], weights[k].at[mine, z, x], sem_s.at[k, 0], sem_r.at[k, 0], peer, k)

    def forward_z(k, step):
        src = weights[k].at[mine, z_from(step), x]
        arrived(src, s_z.at[k, step], r_zs.at[k, step])
        push(src, src, s_x.at[k, step], r_x.at[k, step], x_peer, k)
        push(src, src, s_y.at[k, step], r_y.at[k, step], y_peer, k)

    first = pl.ds(0, FWD_ROWS)
    second = pl.ds(FWD_ROWS, block - FWD_ROWS)

    def forward_diagonal(k, step):
        from_x = weights[k].at[mine, z_from(step), far_x]
        arrived(from_x, s_x.at[k, step], r_x.at[k, step])
        part = weights[k].at[mine, z_from(step), far_x, first]
        push(part, part, s_dy.at[k, step], r_dy.at[k, step], y_peer, k)
        from_y = weights[k].at[over_y, z_from(step), x]
        arrived(from_y, s_y.at[k, step], r_y.at[k, step])
        part = weights[k].at[over_y, z_from(step), x, second]
        push(part, part, s_dx.at[k, step], r_dx.at[k, step], x_peer, k)

    def to_core(k, index, block_index, column):
        src = weights[k].at[block_index, :, column]
        push(src, src, s_c.at[k, index], r_c.at[k, index], c_peer, k)

    def columns_to_core(k):
        to_core(k, 1, mine, far_x)
        to_core(k, 2, over_y, x)

    def finish(k):
        for step in range(NZ):
            arrived(
                weights[k].at[over_y, z_from(step), far_x, first],
                s_dy.at[k, step],
                r_dy.at[k, step],
            )
            arrived(
                weights[k].at[over_y, z_from(step), far_x, second],
                s_dx.at[k, step],
                r_dx.at[k, step],
            )
        to_core(k, 3, over_y, far_x)
        for index, (block_index, column) in enumerate(
            (
                (y * NC + far_c, x),
                (y * NC + far_c, far_x),
                (far_y * NC + far_c, x),
                (far_y * NC + far_c, far_x),
            )
        ):
            arrived(
                weights[k].at[block_index, :, column], s_c.at[k, index], r_c.at[k, index]
            )

    def small_stage(which, buf, buf_in, stage):
        if stage < 3:
            peer = (c_peer, y_peer, x_peer)[stage]
            push(buf.at[stage], buf_in.at[stage], s_sm.at[which, stage], r_sm.at[which, stage], peer)
        else:
            for step in range(1, NZ):
                push(
                    buf.at[3],
                    buf_in.at[2 + step],
                    s_sm.at[which, 2 + step],
                    r_sm.at[which, 2 + step],
                    z_peer(step),
                )

    def small_add(which, buf, buf_in, stage):
        arrived(buf_in.at[stage], s_sm.at[which, stage], r_sm.at[which, stage])
        buf[stage + 1] = buf[stage] + buf_in[stage]

    def small_last(which, buf, buf_in):
        for step in range(1, NZ):
            arrived(buf_in.at[2 + step], s_sm.at[which, 2 + step], r_sm.at[which, 2 + step])
        total = jnp.zeros(buf.shape[1:], F32)
        for place in range(NZ):
            term = buf[3]
            for step in range(1, NZ):
                term = jnp.where(z_from(step) == place, buf_in[2 + step], term)
            total = total + term
        return total

    load_small = pltpu.make_async_copy(small, par.at[0], s_load.at[6])
    load_small.start()
    send_z(QKV)
    for copy in loads:
        copy.start()
    send_own(QKV)
    load_small.wait()
    small_stage(0, par, par_in, 0)
    send_own(IN)
    send_z(IN)
    small_add(0, par, par_in, 0)
    small_stage(0, par, par_in, 1)
    forward_z(QKV, 1)
    small_add(0, par, par_in, 1)
    small_stage(0, par, par_in, 2)
    forward_diagonal(QKV, 0)
    forward_z(QKV, 3)
    small_add(0, par, par_in, 2)
    small_stage(0, par, par_in, 3)
    forward_diagonal(QKV, 1)
    forward_z(QKV, 2)
    send_z(DOWN)
    send_z(PILOT)
    for copy in loads:
        copy.wait()
    to_core(QKV, 0, mine, x)
    send_own(DOWN)
    forward_diagonal(QKV, 3)
    forward_z(IN, 1)
    forward_diagonal(QKV, 2)
    columns_to_core(QKV)
    forward_z(IN, 3)
    forward_diagonal(IN, 0)
    forward_z(IN, 2)
    to_core(IN, 0, mine, x)
    par[4] = small_last(0, par, par_in)
    finish(QKV)

    length = lens[mp]
    key_keep = lax.broadcasted_iota(jnp.int32, (rows, rows), 1) < length
    row_keep = (lax.broadcasted_iota(jnp.int32, (rows, 1), 0) < length).astype(F32)

    def par_row(index):
        return par[4, index : index + 1, :]

    def square(ref, m, start, stop):
        value = ref[m, :, :, :, start:stop]
        return value.reshape(width, stop - start)

    def project(m, carry):
        bias = par[4, pl.ds(QKV_ROW + m, 1), :qkv_cols]
        qkv[m] = (nn(xs[...], square(w_a, m, 0, qkv_cols)) + bias).astype(BF16)
        return carry

    lax.fori_loop(0, GROUP, project, 0)

    def attend(m, carry):
        part = qkv[m]
        for h in range(heads_here):
            lo = h * HEAD_DIM
            q = part[:, lo : lo + HEAD_DIM]
            k = part[:, head_cols + lo : head_cols + lo + HEAD_DIM]
            v = part[:, 2 * head_cols + lo : 2 * head_cols + lo + HEAD_DIM]
            score = jnp.where(key_keep, nt(q, k) * scale, -1000000000.0)
            expo = jnp.exp(score - jnp.max(score, -1, keepdims=True))
            weight = expo / jnp.sum(expo, -1, keepdims=True)
            prob[m * heads_here + h] = weight
            ctx[m, :, lo : lo + HEAD_DIM] = nn(weight.astype(BF16), v).astype(BF16)
        return carry

    forward_diagonal(IN, 1)
    send_own(PILOT)
    forward_diagonal(IN, 3)
    forward_z(DOWN, 1)
    lax.fori_loop(0, NY, attend, 0)
    forward_diagonal(IN, 2)
    columns_to_core(IN)
    forward_z(DOWN, 3)
    forward_diagonal(DOWN, 0)
    lax.fori_loop(NY, GROUP, attend, 0)

    acc[...] = jnp.zeros_like(acc)

    def attended(m, carry):
        acc[...] += nt(ctx[m], square(w_a, m, qkv_cols, width))
        return carry

    lax.fori_loop(0, GROUP, attended, 0)
    opening = xs[...].astype(F32) + acc[...] + par_row(2)
    centered = opening - row_mean(opening)
    rstd = lax.rsqrt(row_mean(centered * centered) + EPSILON)
    rs1[...] = rstd
    xhat = centered * rstd
    xh1[...] = xhat
    normed_low = (xhat * par_row(0) + par_row(3)).astype(BF16)
    low[...] = normed_low
    forward_z(DOWN, 2)
    to_core(DOWN, 0, mine, x)
    forward_diagonal(DOWN, 1)
    finish(IN)
    forward_diagonal(DOWN, 3)
    forward_z(PILOT, 1)

    def expand(m, carry):
        pre = nn(low[...], square(w_i, m, 0, width)) + par[4, pl.ds(BIAS_ROW + m, 1), :]
        gate = 0.5 + 0.5 * lax.erf(pre * math.sqrt(0.5))
        hid[m] = (pre * gate).astype(BF16)
        gder[m] = gate + pre * (jnp.exp(-0.5 * pre * pre) * (1.0 / math.sqrt(2.0 * math.pi)))
        return carry

    lax.fori_loop(0, GROUP, expand, 0)
    low_t[...] = low[...].T
    forward_diagonal(DOWN, 2)
    columns_to_core(DOWN)
    forward_z(PILOT, 3)
    forward_diagonal(PILOT, 0)
    forward_z(PILOT, 2)
    to_core(PILOT, 0, mine, x)
    finish(DOWN)
    forward_diagonal(PILOT, 1)

    acc[...] = xh1[...] * par_row(0) + par_row(3) + par_row(4)

    def contract(m, carry):
        acc[...] += nt(hid[m], square(w_d, m, 0, width))
        return carry

    lax.fori_loop(0, GROUP, contract, 0)
    stream = acc[...]
    centered = stream - row_mean(stream)
    rstd = lax.rsqrt(row_mean(centered * centered) + EPSILON)
    rs2[...] = rstd
    xhat = centered * rstd
    xh2[...] = xhat
    own[0] = (xhat * par_row(1) + par_row(5)).astype(BF16)

    outs = (out_o, along_o, ig_o)

    def send_result(index):
        dst = outs[index].at[my_rows]
        pltpu.make_async_copy(own.at[index], dst, s_own.at[index]).start()
        push(own.at[index], dst, s_out.at[index, 0], r_out.at[index, 0], y_peer)
        push(own.at[index], dst, s_out.at[index, 1], r_out.at[index, 1], c_peer)

    def forward_result(index):
        part = outs[index].at[pl.ds(over_y * rows, rows)]
        arrived(part, s_out.at[index, 0], r_out.at[index, 0])
        push(part, part, s_out.at[index, 2], r_out.at[index, 2], c_peer)

    def finish_result(index):
        pltpu.make_async_copy(own.at[index], outs[index].at[my_rows], s_own.at[index]).wait()
        near = outs[index].at[pl.ds((y * NC + far_c) * rows, rows)]
        arrived(near, s_out.at[index, 1], r_out.at[index, 1])
        far = outs[index].at[pl.ds((far_y * NC + far_c) * rows, rows)]
        arrived(far, s_out.at[index, 2], r_out.at[index, 2])

    send_result(0)
    forward_diagonal(PILOT, 3)

    gs[0] = jnp.zeros(gs.shape[1:], F32)

    def norm_back(grad, xhat, rstd, gain):
        hat = grad * gain
        return rstd * (hat - row_mean(hat) - xhat * row_mean(hat * xhat))

    masked = cots[...].astype(F32) * row_keep
    xhat = xh2[...]
    gs[0, 1:2, :] = col_sum(masked * xhat)
    gs[0, 5:6, :] = col_sum(masked)
    stream_grad = norm_back(masked, xhat, rs2[...], par_row(1))
    gs[0, 4:5, :] = col_sum(stream_grad)
    sgrad[...] = stream_grad
    bl[...] = stream_grad.astype(BF16)
    bl_t[...] = bl[...].T
    acc[...] = stream_grad

    def block_of(i):
        return i * NC + far_c if i < NY else (i - NY) * NC + c

    slab = NX * block

    def outer(left_t, right, ref, m, start, stop):
        def one(zz, carry):
            top = pl.multiple_of(zz * slab, slab)
            value = nn(left_t[pl.ds(top, slab), :], right[...])
            ref[m, zz, :, :, start:stop] = value.astype(BF16).reshape(NX, block, stop - start)
            return carry

        lax.fori_loop(0, NZ, one, 0)

    def to_partner(ref, k, i):
        src = ref.at[i * NC + far_c]
        copy = remote(src, r_core.at[k, i], s_rc.at[k, i], r_rc.at[k, i], c_peer)
        return copy

    pre_low = own.at[1]

    def back_ff(i):
        m = block_of(i)
        outer(bl_t, hid.at[m], g_d, m, 0, width)
        grad = nn(bl[...], square(w_d, m, 0, width)) * gder[m]
        pre_low[...] = grad.astype(BF16)
        gs[0, pl.ds(BIAS_ROW + m, 1), :] = col_sum(pre_low[...].astype(F32))
        outer(low_t, pre_low, g_i, m, 0, width)
        acc[...] += nt(pre_low[...], square(w_i, m, 0, width))

        if i < NY:
            to_partner(g_d, 0, i).start()
            to_partner(g_i, 1, i).start()

    for i in range(GROUP):
        back_ff(i)
        if i == 0:
            forward_diagonal(PILOT, 2)
            columns_to_core(PILOT)

    top_rows = pl.ds(0, BWD_ROWS)
    low_rows = pl.ds(BWD_ROWS, block - BWD_ROWS)

    def add_core(k, ref):
        for yy in range(NY):
            m = yy * NC + c
            to_partner(ref, k, yy).wait_recv()

            def one(zz, carry):
                ref[m, zz] = ref[m, zz] + r_core[k, yy, zz]
                return carry

            lax.fori_loop(0, NZ, one, 0)

    def reduce_first(k, ref):
        push(
            ref.at[over_y, :, :, top_rows], r_yf.at[k], s_red.at[k, 0], r_red.at[k, 0], y_peer
        )
        for yy in range(NY):
            push(
                ref.at[yy * NC + c, :, far_x, low_rows],
                r_xf.at[k, yy],
                s_red.at[k, 1 + yy],
                r_red.at[k, 1 + yy],
                x_peer,
            )

    def reduce_second(k, ref):
        arrived(r_yf.at[k], s_red.at[k, 0], r_red.at[k, 0])
        ref[mine, :, :, top_rows, :] = ref[mine, :, :, top_rows, :] + r_yf[k]
        push(
            ref.at[mine, :, far_x, top_rows], r_xs.at[k], s_red.at[k, 3], r_red.at[k, 3], x_peer
        )
        for yy in range(NY):
            m = yy * NC + c
            arrived(r_xf.at[k, yy], s_red.at[k, 1 + yy], r_red.at[k, 1 + yy])
            ref[m, :, x, low_rows, :] = ref[m, :, x, low_rows, :] + r_xf[k, yy]
        push(
            ref.at[over_y, :, x, low_rows], r_ys.at[k], s_red.at[k, 4], r_red.at[k, 4], y_peer
        )

    def reduce_third(k, ref):
        arrived(r_xs.at[k], s_red.at[k, 3], r_red.at[k, 3])
        ref[mine, :, x, top_rows, :] = ref[mine, :, x, top_rows, :] + r_xs[k]
        arrived(r_ys.at[k], s_red.at[k, 4], r_red.at[k, 4])
        ref[mine, :, x, low_rows, :] = ref[mine, :, x, low_rows, :] + r_ys[k]
        for step in range(1, NZ):
            push(
                ref.at[mine, z_at(step), x],
                r_z.at[k, step - 1],
                s_rz.at[k, step],
                r_rz.at[k, step],
                z_peer(step),
            )

    def reduce_last(k, ref, result):
        total = ref[mine, z, x].astype(F32)
        for step in range(1, NZ):
            arrived(r_z.at[k, step - 1], s_rz.at[k, step], r_rz.at[k, step])
            total = total + r_z[k, step - 1].astype(F32)
        result[...] = total

    add_core(0, g_d)
    reduce_first(0, g_d)
    add_core(1, g_i)
    reduce_first(1, g_i)
    forward_result(0)

    xhat = xh1[...]
    normed_grad = acc[...]
    gs[0, 0:1, :] = col_sum(normed_grad * xhat)
    gs[0, 3:4, :] = col_sum(normed_grad)
    first_grad = norm_back(normed_grad, xhat, rs1[...], par_row(0))
    gs[0, 2:3, :] = col_sum(first_grad)
    acc[...] = first_grad
    bl[...] = first_grad.astype(BF16)
    bl_t[...] = bl[...].T
    low_t[...] = xs[...].T
    g_a = w_d

    def back_attention(i):
        m = block_of(i)
        outer(bl_t, ctx.at[m], g_a, m, qkv_cols, width)
        context_grad = nn(bl[...], square(w_a, m, qkv_cols, width)).astype(BF16)
        part = qkv[m]
        for h in range(heads_here):
            lo = h * HEAD_DIM
            q = part[:, lo : lo + HEAD_DIM]
            k = part[:, head_cols + lo : head_cols + lo + HEAD_DIM]
            v = part[:, 2 * head_cols + lo : 2 * head_cols + lo + HEAD_DIM]
            d_ctx = context_grad[:, lo : lo + HEAD_DIM]
            weight = prob[m * heads_here + h]
            d_value = tn(weight.astype(BF16), d_ctx)
            d_prob = nt(d_ctx, v)
            spread = jnp.sum(weight * d_prob, -1, keepdims=True)
            d_score = (weight * (d_prob - spread)).astype(BF16)
            qg[:, lo : lo + HEAD_DIM] = (nn(d_score, k) * scale).astype(BF16)
            qg[:, head_cols + lo : head_cols + lo + HEAD_DIM] = (tn(d_score, q) * scale).astype(BF16)
            qg[:, 2 * head_cols + lo : 2 * head_cols + lo + HEAD_DIM] = d_value.astype(BF16)
        gs[0, pl.ds(QKV_ROW + m, 1), :qkv_cols] = col_sum(qg[...].astype(F32))
        outer(low_t, qg, g_a, m, 0, qkv_cols)
        acc[...] += nt(qg[...], square(w_a, m, 0, qkv_cols))

        if i < NY:
            to_partner(g_a, 2, i).start()

    for chunk, copy in sends:
        if chunk == DOWN:
            copy.wait_send()
    for i in range(GROUP):
        back_attention(i)
        if i == 2:
            finish(PILOT)
            reduce_second(0, g_d)
    own[2] = acc[...].astype(BF16)
    add_core(2, g_a)
    reduce_second(1, g_i)
    reduce_first(2, g_a)
    send_result(2)
    small_stage(1, gs, gs_in, 0)
    reduce_third(0, g_d)
    small_add(1, gs, gs_in, 0)
    small_stage(1, gs, gs_in, 1)

    acc[...] = jnp.zeros_like(acc)

    def steer(m, carry):
        acc[...] += nt(hid[m], square(w_p, m, 0, width))
        return carry

    lax.fori_loop(0, GROUP, steer, 0)
    tangent = acc[...]
    xhat = xh2[...]
    along = rs2[...] * (tangent - row_mean(tangent) - xhat * row_mean(tangent * xhat))
    own[1] = (par_row(1) * along).astype(BF16)
    send_result(1)
    reduce_third(1, g_i)
    small_add(1, gs, gs_in, 1)
    small_stage(1, gs, gs_in, 2)
    reduce_second(2, g_a)
    reduce_last(0, g_d, grad_d)
    forward_result(2)
    small_add(1, gs, gs_in, 2)
    small_stage(1, gs, gs_in, 3)
    reduce_third(2, g_a)
    forward_result(1)
    reduce_last(1, g_i, grad_i)
    small_sum[...] = small_last(1, gs, gs_in)
    reduce_last(2, g_a, grad_a)
    for index in range(3):
        finish_result(index)
    for k, ref in enumerate((g_d, g_i, g_a)):
        for i in range(NY):
            to_partner(ref, k, i).wait_send()
    for chunk, copy in sends:
        if chunk != DOWN:
            copy.wait_send()


def run_layer(inner, lens, tok, cot, shards, small):
    width = tok.shape[1]
    rows = tok.shape[0] // GROUP
    block = width // BLOCKS
    head_cols = width // GROUP
    qkv_cols = 3 * head_cols
    heads = width // HEAD_DIM
    anywhere = pl.BlockSpec(memory_space=pl.ANY)
    vmem = pl.BlockSpec(memory_space=pltpu.VMEM)
    weight = pltpu.VMEM((GROUP, NZ, NX, block, width), BF16)
    act = pltpu.VMEM((rows, width), F32)
    act_low = pltpu.VMEM((rows, width), BF16)
    column = pltpu.VMEM((rows, 1), F32)
    dma = pltpu.SemaphoreType.DMA
    grads = 3
    scratch = (
        [weight] * 6
        + [
            pltpu.VMEM((grads, NY, NZ, NX, block, width), BF16),
            pltpu.VMEM((grads, NZ, NX, BWD_ROWS, width), BF16),
            pltpu.VMEM((grads, NY, NZ, block - BWD_ROWS, width), BF16),
            pltpu.VMEM((grads, NZ, BWD_ROWS, width), BF16),
            pltpu.VMEM((grads, NZ, block - BWD_ROWS, width), BF16),
            pltpu.VMEM((grads, NZ - 1, block, width), BF16),
            pltpu.VMEM((5, SMALL_ROWS, width), F32),
            pltpu.VMEM((6, SMALL_ROWS, width), F32),
            pltpu.VMEM((4, SMALL_ROWS, width), F32),
            pltpu.VMEM((6, SMALL_ROWS, width), F32),
            act_low,
            act_low,
            pltpu.VMEM((GROUP, rows, qkv_cols), BF16),
            pltpu.VMEM((heads, rows, rows), F32),
            pltpu.VMEM((GROUP, rows, head_cols), BF16),
            act,
            act,
            column,
            act_low,
            pltpu.VMEM((width, rows), BF16),
            pltpu.VMEM((GROUP, rows, width), BF16),
            pltpu.VMEM((GROUP, rows, width), F32),
            act,
            column,
            act,
            act_low,
            pltpu.VMEM((width, rows), BF16),
            pltpu.VMEM((rows, qkv_cols), BF16),
            pltpu.VMEM((3, rows, width), BF16),
        ]
        + [dma((7,))]
        + [dma((4, NZ))] * 12
        + [dma((grads, NY))] * 2
        + [dma((grads, 5))] * 2
        + [dma((grads, NZ))] * 2
        + [dma((2, 6))] * 2
        + [dma((3, 3))] * 2
        + [dma((3,))]
    )
    whole = jax.ShapeDtypeStruct(tok.shape, BF16)
    piece = jax.ShapeDtypeStruct((block, width), F32)
    return pl.pallas_call(
        functools.partial(layer_kernel, inner),
        out_shape=(
            whole,
            whole,
            whole,
            piece,
            piece,
            piece,
            jax.ShapeDtypeStruct((SMALL_ROWS, width), F32),
        ),
        in_specs=[pl.BlockSpec(memory_space=pltpu.SMEM)] + [anywhere] * 7,
        out_specs=(anywhere,) * 3 + (vmem,) * 4,
        scratch_shapes=scratch,
        compiler_params=pltpu.CompilerParams(
            collective_id=0, has_side_effects=True, vmem_limit_bytes=67043328
        ),
        name="layer",
    )(lens, tok, cot, *shards, small)


def local(
    tokens, cotangent, lengths, w_qkv, qv_bias, w_out, w_in, in_bias, w_down, pilot, gains, shifts
):
    n_dp = lax.axis_size("dp")
    inner = n_dp // BLOCKS
    groups = [[b * inner + i for i in range(inner)] for b in range(BLOCKS)]
    dp = lax.axis_index("dp")
    mp = lax.axis_index("mp")
    width = tokens.shape[1]
    head_cols = w_out.shape[0]
    local_rows = w_qkv.shape[0]
    shards = (
        jnp.concatenate([w_qkv.reshape(local_rows, 3 * head_cols), w_out.T], 1),
        w_in,
        w_down.T,
        pilot.T,
    )

    spot = jnp.arange(width, dtype=jnp.int32)
    share = gains.shape[1]

    def spread(values, period, offset):
        per = values.shape[1]
        tiled = jnp.tile(values, (1, period // per))
        tiled = jnp.pad(tiled, ((0, 0), (offset, width - offset - period)))
        place = (spot - offset) // per == dp
        return jnp.where(place & (spot >= offset) & (spot < offset + period), tiled, 0)

    head = (mp == 0).astype(F32)
    vectors = spread(jnp.concatenate([gains, shifts], 0).astype(F32), width, 0) * head
    at_mp = (jnp.arange(GROUP) == mp).astype(F32)[:, None]
    hidden_bias = spread(in_bias.astype(F32), width, 0) * at_mp
    pair = qv_bias.reshape(2, -1).astype(F32)
    qkv_bias = (
        spread(pair[0:1], head_cols, 0) + spread(pair[1:2], head_cols, 2 * head_cols)
    ) * at_mp
    small = jnp.concatenate(
        [
            vectors,
            hidden_bias,
            qkv_bias,
            jnp.zeros((SMALL_ROWS - QKV_ROW - GROUP, width), F32),
        ],
        0,
    )
    if inner > 1:
        shards = tuple(
            lax.all_gather(item, "dp", axis=0, tiled=True, axis_index_groups=groups)
            for item in shards
        )
        small = lax.psum(small, "dp", axis_index_groups=groups)

    out, along, input_grad, grad_a, grad_i, grad_d, sums = run_layer(
        inner, lengths, tokens, cotangent, shards, small
    )
    if inner > 1:
        grad_a, grad_i, grad_d = (
            lax.psum_scatter(
                item, "dp", scatter_dimension=0, tiled=True, axis_index_groups=groups
            )
            for item in (grad_a, grad_i, grad_d)
        )
        sums = lax.psum(sums, "dp", axis_index_groups=groups)

    columns = lax.dynamic_slice_in_dim(sums, dp * share, share, 1)
    bias_share = qv_bias.shape[2]
    bias_row = lax.dynamic_slice_in_dim(sums, QKV_ROW + mp, 1, 0)
    grad_qvb = jnp.stack(
        [
            lax.dynamic_slice_in_dim(bias_row, dp * bias_share, bias_share, 1),
            lax.dynamic_slice_in_dim(
                bias_row, 2 * head_cols + dp * bias_share, bias_share, 1
            ),
        ]
    )
    return (
        out,
        input_grad.astype(F32),
        along.astype(F32),
        grad_a[:, : 3 * head_cols].reshape(local_rows, 3, head_cols),
        grad_qvb,
        grad_a[:, 3 * head_cols :].T,
        grad_i,
        lax.dynamic_slice_in_dim(columns, BIAS_ROW + mp, 1, 0),
        grad_d.T,
        columns[0:2],
        columns[2:6],
    )


def solution(mesh):
    in_specs = (
        P("dp", None),
        P("dp", None),
        P("dp"),
        P("dp", None, "mp"),
        P(None, "mp", "dp"),
        P("mp", "dp"),
        P("dp", "mp"),
        P("mp", "dp"),
        P("mp", "dp"),
        P("mp", "dp"),
        P(None, "dp"),
        P(None, "dp"),
    )
    out_specs = (
        P("dp", None),
        P("dp", None),
        P("dp", None),
        P("dp", None, "mp"),
        P(None, "mp", "dp"),
        P("mp", "dp"),
        P("dp", "mp"),
        P("mp", "dp"),
        P("mp", "dp"),
        P(None, "dp"),
        P(None, "dp"),
    )
    return jax.shard_map(local, mesh=mesh, in_specs=in_specs, out_specs=out_specs, check_vma=False)
```

```python
import functools
import math

import jax
import jax.numpy as jnp
from jax import lax
from jax.experimental import pallas as pl
from jax.experimental.pallas import tpu as pltpu
from jax.sharding import PartitionSpec as P

HEAD_DIM = 64
SEQ_LEN = 256
EPSILON = 1e-06
NZ, NX, NY, NC = 4, 2, 2, 2
BLOCKS = NZ * NX
GROUP = NY * NC
SMALL_ROWS = 16
BIAS_ROW = 6
QKV_ROW = BIAS_ROW + GROUP
FWD_ROWS = 48
BWD_ROWS = 48
F32 = jnp.float32
BF16 = jnp.bfloat16
QKV, IN, DOWN, PILOT = range(4)


def nt(a, b):
    return lax.dot_general(a, b, (((1,), (1,)), ((), ())), preferred_element_type=F32)


def tn(a, b):
    return lax.dot_general(a, b, (((0,), (0,)), ((), ())), preferred_element_type=F32)


def nn(a, b):
    return jnp.dot(a, b, preferred_element_type=F32)


def row_mean(v):
    return jnp.mean(v, -1, keepdims=True)


def col_sum(v):
    return jnp.sum(v, 0, keepdims=True)


def layer_kernel(
    inner,
    lens,
    tok,
    cot,
    shard_a,
    shard_i,
    shard_d,
    shard_p,
    small,
    out_o,
    along_o,
    ig_o,
    grad_a,
    grad_i,
    grad_d,
    small_sum,
    w_a,
    w_i,
    w_d,
    w_p,
    g_i,
    g_d,
    r_core,
    r_yf,
    r_xf,
    r_xs,
    r_ys,
    r_z,
    par,
    par_in,
    gs,
    gs_in,
    xs,
    cots,
    qkv,
    prob,
    ctx,
    acc,
    xh1,
    rs1,
    low,
    low_t,
    hid,
    gder,
    xh2,
    rs2,
    sgrad,
    bl,
    bl_t,
    qg,
    own,
    s_load,
    s_z,
    r_zs,
    s_x,
    r_x,
    s_y,
    r_y,
    s_dx,
    r_dx,
    s_dy,
    r_dy,
    s_c,
    r_c,
    s_rc,
    r_rc,
    s_red,
    r_red,
    s_rz,
    r_rz,
    s_sm,
    r_sm,
    s_out,
    r_out,
    s_own,
):
    weights = (w_a, w_i, w_d, w_p)
    shards = (shard_a, shard_i, shard_d, shard_p)
    width = xs.shape[1]
    block = w_a.shape[3]
    head_cols = ctx.shape[2]
    qkv_cols = 3 * head_cols
    heads_here = head_cols // HEAD_DIM
    rows = xs.shape[0]
    scale = HEAD_DIM ** (-0.5)

    dp = lax.axis_index("dp")
    mp = lax.axis_index("mp")
    spot = dp // inner
    rest = dp - spot * inner
    z, x = spot // NX, spot % NX
    y, c = mp // NC, mp % NC
    far_y, far_x, far_c = 1 - y, 1 - x, 1 - c
    mine = mp
    over_y = far_y * NC + c
    x_peer = {"dp": (z * NX + far_x) * inner + rest, "mp": mp}
    y_peer = {"dp": dp, "mp": over_y}
    c_peer = {"dp": dp, "mp": y * NC + far_c}

    def z_at(step):
        return (z + step) % NZ

    def z_from(step):
        return (z + NZ - step) % NZ

    def z_peer(step):
        return {"dp": (z_at(step) * NX + x) * inner + rest, "mp": mp}

    sends = []

    def remote(src, dst, send, recv, peer):
        return pltpu.make_async_remote_copy(
            src_ref=src,
            dst_ref=dst,
            send_sem=send,
            recv_sem=recv,
            device_id=peer,
            device_id_type=pl.DeviceIdType.MESH,
        )

    def push(src, dst, send, recv, peer, chunk=None):
        copy = remote(src, dst, send, recv, peer)
        copy.start()
        sends.append((chunk, copy))

    def arrived(dst, send, recv):
        remote(dst, dst, send, recv, c_peer).wait_recv()

    barrier = pltpu.get_barrier_semaphore()
    peers = [x_peer, y_peer, c_peer] + [z_peer(step) for step in range(1, NZ)]
    for peer in peers:
        pl.semaphore_signal(barrier, inc=1, device_id=peer, device_id_type=pl.DeviceIdType.MESH)
    pl.semaphore_wait(barrier, len(peers))

    loads = []
    for k in range(4):
        loads.append(
            pltpu.make_async_copy(shards[k], weights[k].at[mine, z, x], s_load.at[k])
        )
    my_rows = pl.ds(mp * rows, rows)
    loads.append(pltpu.make_async_copy(tok.at[my_rows], xs, s_load.at[4]))
    loads.append(pltpu.make_async_copy(cot.at[my_rows], cots, s_load.at[5]))

    def send_z(k):
        for step in range(1, NZ):
            push(
                shards[k],
                weights[k].at[mine, z, x],
                s_z.at[k, step],
                r_zs.at[k, step],
                z_peer(step),
                k,
            )

    def send_own(k):
        for sem_s, sem_r, peer in ((s_x, r_x, x_peer), (s_y, r_y, y_peer)):
            push(shards[k], weights[k].at[mine, z, x], sem_s.at[k, 0], sem_r.at[k, 0], peer, k)

    def forward_z(k, step):
        src = weights[k].at[mine, z_from(step), x]
        arrived(src, s_z.at[k, step], r_zs.at[k, step])
        push(src, src, s_x.at[k, step], r_x.at[k, step], x_peer, k)
        push(src, src, s_y.at[k, step], r_y.at[k, step], y_peer, k)

    first = pl.ds(0, FWD_ROWS)
    second = pl.ds(FWD_ROWS, block - FWD_ROWS)

    def forward_diagonal(k, step):
        from_x = weights[k].at[mine, z_from(step), far_x]
        arrived(from_x, s_x.at[k, step], r_x.at[k, step])
        part = weights[k].at[mine, z_from(step), far_x, first]
        push(part, part, s_dy.at[k, step], r_dy.at[k, step], y_peer, k)
        from_y = weights[k].at[over_y, z_from(step), x]
        arrived(from_y, s_y.at[k, step], r_y.at[k, step])
        part = weights[k].at[over_y, z_from(step), x, second]
        push(part, part, s_dx.at[k, step], r_dx.at[k, step], x_peer, k)

    def to_core(k, index, block_index, column):
        src = weights[k].at[block_index, :, column]
        push(src, src, s_c.at[k, index], r_c.at[k, index], c_peer, k)

    def side_z(k):
        for step in range(1, NZ):
            src = weights[k].at[mine, z, far_x]
            push(src, src, s_x.at[k, step], r_x.at[k, step], z_peer(step), k)
            src = weights[k].at[over_y, z, x]
            push(src, src, s_y.at[k, step], r_y.at[k, step], z_peer(step), k)

    def corner_z(k):
        arrived(weights[k].at[over_y, z, far_x, first], s_dy.at[k, 0], r_dy.at[k, 0])
        arrived(weights[k].at[over_y, z, far_x, second], s_dx.at[k, 0], r_dx.at[k, 0])
        src = weights[k].at[over_y, z, far_x]
        for step in range(1, NZ):
            push(src, src, s_dx.at[k, step], r_dx.at[k, step], z_peer(step), k)

    def finish_z(k):
        for step in range(1, NZ):
            at = z_from(step)
            arrived(weights[k].at[mine, at, x], s_z.at[k, step], r_zs.at[k, step])
            arrived(weights[k].at[mine, at, far_x], s_x.at[k, step], r_x.at[k, step])
            arrived(weights[k].at[over_y, at, x], s_y.at[k, step], r_y.at[k, step])
            arrived(weights[k].at[over_y, at, far_x], s_dx.at[k, step], r_dx.at[k, step])
        to_core(k, 0, mine, x)
        columns_to_core(k)
        exchange_core(k)

    def columns_to_core(k):
        to_core(k, 1, mine, far_x)
        to_core(k, 2, over_y, x)

    def finish(k):
        for step in range(NZ):
            arrived(
                weights[k].at[over_y, z_from(step), far_x, first],
                s_dy.at[k, step],
                r_dy.at[k, step],
            )
            arrived(
                weights[k].at[over_y, z_from(step), far_x, second],
                s_dx.at[k, step],
                r_dx.at[k, step],
            )
        exchange_core(k)

    def exchange_core(k):
        to_core(k, 3, over_y, far_x)
        for index, (block_index, column) in enumerate(
            (
                (y * NC + far_c, x),
                (y * NC + far_c, far_x),
                (far_y * NC + far_c, x),
                (far_y * NC + far_c, far_x),
            )
        ):
            arrived(
                weights[k].at[block_index, :, column], s_c.at[k, index], r_c.at[k, index]
            )

    def small_stage(which, buf, buf_in, stage):
        if stage < 3:
            peer = (c_peer, y_peer, x_peer)[stage]
            push(buf.at[stage], buf_in.at[stage], s_sm.at[which, stage], r_sm.at[which, stage], peer)
        else:
            for step in range(1, NZ):
                push(
                    buf.at[3],
                    buf_in.at[2 + step],
                    s_sm.at[which, 2 + step],
                    r_sm.at[which, 2 + step],
                    z_peer(step),
                )

    def small_add(which, buf, buf_in, stage):
        arrived(buf_in.at[stage], s_sm.at[which, stage], r_sm.at[which, stage])
        buf[stage + 1] = buf[stage] + buf_in[stage]

    def small_last(which, buf, buf_in):
        for step in range(1, NZ):
            arrived(buf_in.at[2 + step], s_sm.at[which, 2 + step], r_sm.at[which, 2 + step])
        total = jnp.zeros(buf.shape[1:], F32)
        for place in range(NZ):
            term = buf[3]
            for step in range(1, NZ):
                term = jnp.where(z_from(step) == place, buf_in[2 + step], term)
            total = total + term
        return total

    load_small = pltpu.make_async_copy(small, par.at[0], s_load.at[6])
    load_small.start()
    send_z(QKV)
    for copy in loads:
        copy.start()
    send_own(QKV)
    load_small.wait()
    small_stage(0, par, par_in, 0)
    send_own(IN)
    small_add(0, par, par_in, 0)
    small_stage(0, par, par_in, 1)
    send_own(DOWN)
    forward_z(QKV, 1)
    small_add(0, par, par_in, 1)
    small_stage(0, par, par_in, 2)
    send_own(PILOT)
    forward_diagonal(QKV, 0)
    forward_z(QKV, 3)
    small_add(0, par, par_in, 2)
    small_stage(0, par, par_in, 3)
    forward_diagonal(QKV, 1)
    forward_z(QKV, 2)
    send_z(IN)
    for copy in loads:
        copy.wait()
    to_core(QKV, 0, mine, x)
    forward_diagonal(QKV, 3)
    forward_z(IN, 1)
    forward_diagonal(QKV, 2)
    columns_to_core(QKV)
    forward_z(IN, 3)
    forward_diagonal(IN, 0)
    forward_z(IN, 2)
    to_core(IN, 0, mine, x)
    send_z(DOWN)
    par[4] = small_last(0, par, par_in)
    finish(QKV)

    length = lens[mp]
    key_keep = lax.broadcasted_iota(jnp.int32, (rows, rows), 1) < length
    row_keep = (lax.broadcasted_iota(jnp.int32, (rows, 1), 0) < length).astype(F32)

    def par_row(index):
        return par[4, index : index + 1, :]

    def square(ref, m, start, stop):
        value = ref[m, :, :, :, start:stop]
        return value.reshape(width, stop - start)

    def project(m, carry):
        bias = par[4, pl.ds(QKV_ROW + m, 1), :qkv_cols]
        qkv[m] = (nn(xs[...], square(w_a, m, 0, qkv_cols)) + bias).astype(BF16)
        return carry

    lax.fori_loop(0, GROUP, project, 0)

    def attend(m, carry):
        part = qkv[m]
        for h in range(heads_here):
            lo = h * HEAD_DIM
            q = part[:, lo : lo + HEAD_DIM]
            k = part[:, head_cols + lo : head_cols + lo + HEAD_DIM]
            v = part[:, 2 * head_cols + lo : 2 * head_cols + lo + HEAD_DIM]
            score = jnp.where(key_keep, nt(q, k) * scale, -1000000000.0)
            expo = jnp.exp(score - jnp.max(score, -1, keepdims=True))
            weight = expo / jnp.sum(expo, -1, keepdims=True)
            prob[m * heads_here + h] = weight
            ctx[m, :, lo : lo + HEAD_DIM] = nn(weight.astype(BF16), v).astype(BF16)
        return carry

    forward_diagonal(IN, 1)
    forward_diagonal(IN, 3)
    forward_z(DOWN, 1)
    forward_diagonal(PILOT, 0)
    lax.fori_loop(0, NY, attend, 0)
    forward_diagonal(IN, 2)
    columns_to_core(IN)
    forward_z(DOWN, 3)
    send_z(PILOT)
    side_z(PILOT)
    forward_diagonal(DOWN, 0)
    lax.fori_loop(NY, GROUP, attend, 0)

    acc[...] = jnp.zeros_like(acc)

    def attended(m, carry):
        acc[...] += nt(ctx[m], square(w_a, m, qkv_cols, width))
        return carry

    lax.fori_loop(0, GROUP, attended, 0)
    opening = xs[...].astype(F32) + acc[...] + par_row(2)
    centered = opening - row_mean(opening)
    rstd = lax.rsqrt(row_mean(centered * centered) + EPSILON)
    rs1[...] = rstd
    xhat = centered * rstd
    xh1[...] = xhat
    normed_low = (xhat * par_row(0) + par_row(3)).astype(BF16)
    low[...] = normed_low
    forward_z(DOWN, 2)
    to_core(DOWN, 0, mine, x)
    forward_diagonal(DOWN, 1)
    finish(IN)
    forward_diagonal(DOWN, 3)
    corner_z(PILOT)

    def expand(m, carry):
        pre = nn(low[...], square(w_i, m, 0, width)) + par[4, pl.ds(BIAS_ROW + m, 1), :]
        gate = 0.5 + 0.5 * lax.erf(pre * math.sqrt(0.5))
        hid[m] = (pre * gate).astype(BF16)
        gder[m] = gate + pre * (jnp.exp(-0.5 * pre * pre) * (1.0 / math.sqrt(2.0 * math.pi)))
        return carry

    lax.fori_loop(0, GROUP, expand, 0)
    low_t[...] = low[...].T
    forward_diagonal(DOWN, 2)
    columns_to_core(DOWN)
    finish(DOWN)

    acc[...] = xh1[...] * par_row(0) + par_row(3) + par_row(4)

    def contract(m, carry):
        acc[...] += nt(hid[m], square(w_d, m, 0, width))
        return carry

    lax.fori_loop(0, GROUP, contract, 0)
    stream = acc[...]
    centered = stream - row_mean(stream)
    rstd = lax.rsqrt(row_mean(centered * centered) + EPSILON)
    rs2[...] = rstd
    xhat = centered * rstd
    xh2[...] = xhat
    own[0] = (xhat * par_row(1) + par_row(5)).astype(BF16)

    outs = (out_o, along_o, ig_o)

    def send_result(index):
        dst = outs[index].at[my_rows]
        pltpu.make_async_copy(own.at[index], dst, s_own.at[index]).start()
        push(own.at[index], dst, s_out.at[index, 0], r_out.at[index, 0], y_peer)
        push(own.at[index], dst, s_out.at[index, 1], r_out.at[index, 1], c_peer)

    def forward_result(index):
        part = outs[index].at[pl.ds(over_y * rows, rows)]
        arrived(part, s_out.at[index, 0], r_out.at[index, 0])
        push(part, part, s_out.at[index, 2], r_out.at[index, 2], c_peer)

    def finish_result(index):
        pltpu.make_async_copy(own.at[index], outs[index].at[my_rows], s_own.at[index]).wait()
        near = outs[index].at[pl.ds((y * NC + far_c) * rows, rows)]
        arrived(near, s_out.at[index, 1], r_out.at[index, 1])
        far = outs[index].at[pl.ds((far_y * NC + far_c) * rows, rows)]
        arrived(far, s_out.at[index, 2], r_out.at[index, 2])

    send_result(0)

    gs[0] = jnp.zeros(gs.shape[1:], F32)

    def norm_back(grad, xhat, rstd, gain):
        hat = grad * gain
        return rstd * (hat - row_mean(hat) - xhat * row_mean(hat * xhat))

    masked = cots[...].astype(F32) * row_keep
    xhat = xh2[...]
    gs[0, 1:2, :] = col_sum(masked * xhat)
    gs[0, 5:6, :] = col_sum(masked)
    stream_grad = norm_back(masked, xhat, rs2[...], par_row(1))
    gs[0, 4:5, :] = col_sum(stream_grad)
    sgrad[...] = stream_grad
    bl[...] = stream_grad.astype(BF16)
    bl_t[...] = bl[...].T
    acc[...] = stream_grad

    def block_of(i):
        return i * NC + far_c if i < NY else (i - NY) * NC + c

    slab = NX * block

    def outer(left_t, right, ref, m, start, stop):
        def one(zz, carry):
            top = pl.multiple_of(zz * slab, slab)
            value = nn(left_t[pl.ds(top, slab), :], right[...])
            ref[m, zz, :, :, start:stop] = value.astype(BF16).reshape(NX, block, stop - start)
            return carry

        lax.fori_loop(0, NZ, one, 0)

    def to_partner(ref, k, i):
        src = ref.at[i * NC + far_c]
        copy = remote(src, r_core.at[k, i], s_rc.at[k, i], r_rc.at[k, i], c_peer)
        return copy

    pre_low = own.at[1]

    def back_ff(i):
        m = block_of(i)
        grad = nn(bl[...], square(w_d, m, 0, width)) * gder[m]
        pre_low[...] = grad.astype(BF16)
        gs[0, pl.ds(BIAS_ROW + m, 1), :] = col_sum(pre_low[...].astype(F32))
        outer(low_t, pre_low, g_i, m, 0, width)
        acc[...] += nt(pre_low[...], square(w_i, m, 0, width))

        if i < NY:
            to_partner(g_i, 1, i).start()


    top_rows = pl.ds(0, BWD_ROWS)
    low_rows = pl.ds(BWD_ROWS, block - BWD_ROWS)

    def add_core(k, ref):
        for yy in range(NY):
            m = yy * NC + c
            to_partner(ref, k, yy).wait_recv()

            def one(zz, carry):
                ref[m, zz] = ref[m, zz] + r_core[k, yy, zz]
                return carry

            lax.fori_loop(0, NZ, one, 0)

    def reduce_first(k, ref):
        push(
            ref.at[over_y, :, :, top_rows], r_yf.at[k], s_red.at[k, 0], r_red.at[k, 0], y_peer
        )
        for yy in range(NY):
            push(
                ref.at[yy * NC + c, :, far_x, low_rows],
                r_xf.at[k, yy],
                s_red.at[k, 1 + yy],
                r_red.at[k, 1 + yy],
                x_peer,
            )

    def reduce_second(k, ref):
        arrived(r_yf.at[k], s_red.at[k, 0], r_red.at[k, 0])
        ref[mine, :, :, top_rows, :] = ref[mine, :, :, top_rows, :] + r_yf[k]
        push(
            ref.at[mine, :, far_x, top_rows], r_xs.at[k], s_red.at[k, 3], r_red.at[k, 3], x_peer
        )
        for yy in range(NY):
            m = yy * NC + c
            arrived(r_xf.at[k, yy], s_red.at[k, 1 + yy], r_red.at[k, 1 + yy])
            ref[m, :, x, low_rows, :] = ref[m, :, x, low_rows, :] + r_xf[k, yy]
        push(
            ref.at[over_y, :, x, low_rows], r_ys.at[k], s_red.at[k, 4], r_red.at[k, 4], y_peer
        )

    def reduce_third(k, ref):
        arrived(r_xs.at[k], s_red.at[k, 3], r_red.at[k, 3])
        ref[mine, :, x, top_rows, :] = ref[mine, :, x, top_rows, :] + r_xs[k]
        arrived(r_ys.at[k], s_red.at[k, 4], r_red.at[k, 4])
        ref[mine, :, x, low_rows, :] = ref[mine, :, x, low_rows, :] + r_ys[k]
        for step in range(1, NZ):
            push(
                ref.at[mine, z_at(step), x],
                r_z.at[k, step - 1],
                s_rz.at[k, step],
                r_rz.at[k, step],
                z_peer(step),
            )

    def reduce_last(k, ref, result):
        total = ref[mine, z, x].astype(F32)
        for step in range(1, NZ):
            arrived(r_z.at[k, step - 1], s_rz.at[k, step], r_rz.at[k, step])
            total = total + r_z[k, step - 1].astype(F32)
        result[...] = total

    for i in range(GROUP):
        outer(bl_t, hid.at[block_of(i)], g_d, block_of(i), 0, width)
        if i < NY:
            to_partner(g_d, 0, i).start()
    add_core(0, g_d)
    reduce_first(0, g_d)
    for i in range(GROUP):
        back_ff(i)
    add_core(1, g_i)
    reduce_first(1, g_i)
    forward_result(0)

    xhat = xh1[...]
    normed_grad = acc[...]
    gs[0, 0:1, :] = col_sum(normed_grad * xhat)
    gs[0, 3:4, :] = col_sum(normed_grad)
    first_grad = norm_back(normed_grad, xhat, rs1[...], par_row(0))
    gs[0, 2:3, :] = col_sum(first_grad)
    acc[...] = first_grad
    bl[...] = first_grad.astype(BF16)
    bl_t[...] = bl[...].T
    low_t[...] = xs[...].T
    g_a = w_d

    def back_attention(i):
        m = block_of(i)
        outer(bl_t, ctx.at[m], g_a, m, qkv_cols, width)
        context_grad = nn(bl[...], square(w_a, m, qkv_cols, width)).astype(BF16)
        part = qkv[m]
        for h in range(heads_here):
            lo = h * HEAD_DIM
            q = part[:, lo : lo + HEAD_DIM]
            k = part[:, head_cols + lo : head_cols + lo + HEAD_DIM]
            v = part[:, 2 * head_cols + lo : 2 * head_cols + lo + HEAD_DIM]
            d_ctx = context_grad[:, lo : lo + HEAD_DIM]
            weight = prob[m * heads_here + h]
            d_value = tn(weight.astype(BF16), d_ctx)
            d_prob = nt(d_ctx, v)
            spread = jnp.sum(weight * d_prob, -1, keepdims=True)
            d_score = (weight * (d_prob - spread)).astype(BF16)
            qg[:, lo : lo + HEAD_DIM] = (nn(d_score, k) * scale).astype(BF16)
            qg[:, head_cols + lo : head_cols + lo + HEAD_DIM] = (tn(d_score, q) * scale).astype(BF16)
            qg[:, 2 * head_cols + lo : 2 * head_cols + lo + HEAD_DIM] = d_value.astype(BF16)
        gs[0, pl.ds(QKV_ROW + m, 1), :qkv_cols] = col_sum(qg[...].astype(F32))
        outer(low_t, qg, g_a, m, 0, qkv_cols)
        acc[...] += nt(qg[...], square(w_a, m, 0, qkv_cols))

        if i < NY:
            to_partner(g_a, 2, i).start()

    for chunk, copy in sends:
        if chunk == DOWN:
            copy.wait_send()
    for i in range(GROUP):
        back_attention(i)
        if i == 2:
            reduce_second(0, g_d)
    own[2] = acc[...].astype(BF16)
    small_stage(1, gs, gs_in, 0)
    add_core(2, g_a)
    reduce_second(1, g_i)
    reduce_first(2, g_a)
    small_add(1, gs, gs_in, 0)
    small_stage(1, gs, gs_in, 1)
    reduce_third(0, g_d)
    finish_z(PILOT)
    acc[...] = jnp.zeros_like(acc)

    def steer(m, carry):
        acc[...] += nt(hid[m], square(w_p, m, 0, width))
        return carry

    lax.fori_loop(0, GROUP, steer, 0)
    tangent = acc[...]
    xhat = xh2[...]
    along = rs2[...] * (tangent - row_mean(tangent) - xhat * row_mean(tangent * xhat))
    own[1] = (par_row(1) * along).astype(BF16)
    reduce_third(1, g_i)
    reduce_second(2, g_a)
    small_add(1, gs, gs_in, 1)
    small_stage(1, gs, gs_in, 2)
    send_result(2)
    send_result(1)
    reduce_last(0, g_d, grad_d)
    small_add(1, gs, gs_in, 2)
    small_stage(1, gs, gs_in, 3)
    reduce_third(2, g_a)
    reduce_last(1, g_i, grad_i)
    forward_result(2)
    forward_result(1)
    small_sum[...] = small_last(1, gs, gs_in)
    reduce_last(2, g_a, grad_a)
    for index in range(3):
        finish_result(index)
    for k, ref in enumerate((g_d, g_i, g_a)):
        for i in range(NY):
            to_partner(ref, k, i).wait_send()
    for chunk, copy in sends:
        if chunk != DOWN:
            copy.wait_send()


def run_layer(inner, lens, tok, cot, shards, small):
    width = tok.shape[1]
    rows = tok.shape[0] // GROUP
    block = width // BLOCKS
    head_cols = width // GROUP
    qkv_cols = 3 * head_cols
    heads = width // HEAD_DIM
    anywhere = pl.BlockSpec(memory_space=pl.ANY)
    vmem = pl.BlockSpec(memory_space=pltpu.VMEM)
    weight = pltpu.VMEM((GROUP, NZ, NX, block, width), BF16)
    act = pltpu.VMEM((rows, width), F32)
    act_low = pltpu.VMEM((rows, width), BF16)
    column = pltpu.VMEM((rows, 1), F32)
    dma = pltpu.SemaphoreType.DMA
    grads = 3
    scratch = (
        [weight] * 6
        + [
            pltpu.VMEM((grads, NY, NZ, NX, block, width), BF16),
            pltpu.VMEM((grads, NZ, NX, BWD_ROWS, width), BF16),
            pltpu.VMEM((grads, NY, NZ, block - BWD_ROWS, width), BF16),
            pltpu.VMEM((grads, NZ, BWD_ROWS, width), BF16),
            pltpu.VMEM((grads, NZ, block - BWD_ROWS, width), BF16),
            pltpu.VMEM((grads, NZ - 1, block, width), BF16),
            pltpu.VMEM((5, SMALL_ROWS, width), F32),
            pltpu.VMEM((6, SMALL_ROWS, width), F32),
            pltpu.VMEM((4, SMALL_ROWS, width), F32),
            pltpu.VMEM((6, SMALL_ROWS, width), F32),
            act_low,
            act_low,
            pltpu.VMEM((GROUP, rows, qkv_cols), BF16),
            pltpu.VMEM((heads, rows, rows), F32),
            pltpu.VMEM((GROUP, rows, head_cols), BF16),
            act,
            act,
            column,
            act_low,
            pltpu.VMEM((width, rows), BF16),
            pltpu.VMEM((GROUP, rows, width), BF16),
            pltpu.VMEM((GROUP, rows, width), F32),
            act,
            column,
            act,
            act_low,
            pltpu.VMEM((width, rows), BF16),
            pltpu.VMEM((rows, qkv_cols), BF16),
            pltpu.VMEM((3, rows, width), BF16),
        ]
        + [dma((7,))]
        + [dma((4, NZ))] * 12
        + [dma((grads, NY))] * 2
        + [dma((grads, 5))] * 2
        + [dma((grads, NZ))] * 2
        + [dma((2, 6))] * 2
        + [dma((3, 3))] * 2
        + [dma((3,))]
    )
    whole = jax.ShapeDtypeStruct(tok.shape, BF16)
    piece = jax.ShapeDtypeStruct((block, width), F32)
    return pl.pallas_call(
        functools.partial(layer_kernel, inner),
        out_shape=(
            whole,
            whole,
            whole,
            piece,
            piece,
            piece,
            jax.ShapeDtypeStruct((SMALL_ROWS, width), F32),
        ),
        in_specs=[pl.BlockSpec(memory_space=pltpu.SMEM)] + [anywhere] * 7,
        out_specs=(anywhere,) * 3 + (vmem,) * 4,
        scratch_shapes=scratch,
        compiler_params=pltpu.CompilerParams(
            collective_id=0, has_side_effects=True, vmem_limit_bytes=67043328
        ),
        name="layer",
    )(lens, tok, cot, *shards, small)


def local(
    tokens, cotangent, lengths, w_qkv, qv_bias, w_out, w_in, in_bias, w_down, pilot, gains, shifts
):
    n_dp = lax.axis_size("dp")
    inner = n_dp // BLOCKS
    groups = [[b * inner + i for i in range(inner)] for b in range(BLOCKS)]
    dp = lax.axis_index("dp")
    mp = lax.axis_index("mp")
    width = tokens.shape[1]
    head_cols = w_out.shape[0]
    local_rows = w_qkv.shape[0]
    shards = (
        jnp.concatenate([w_qkv.reshape(local_rows, 3 * head_cols), w_out.T], 1),
        w_in,
        w_down.T,
        pilot.T,
    )

    spot = jnp.arange(width, dtype=jnp.int32)
    share = gains.shape[1]

    def spread(values, period, offset):
        per = values.shape[1]
        tiled = jnp.tile(values, (1, period // per))
        tiled = jnp.pad(tiled, ((0, 0), (offset, width - offset - period)))
        place = (spot - offset) // per == dp
        return jnp.where(place & (spot >= offset) & (spot < offset + period), tiled, 0)

    head = (mp == 0).astype(F32)
    vectors = spread(jnp.concatenate([gains, shifts], 0).astype(F32), width, 0) * head
    at_mp = (jnp.arange(GROUP) == mp).astype(F32)[:, None]
    hidden_bias = spread(in_bias.astype(F32), width, 0) * at_mp
    pair = qv_bias.reshape(2, -1).astype(F32)
    qkv_bias = (
        spread(pair[0:1], head_cols, 0) + spread(pair[1:2], head_cols, 2 * head_cols)
    ) * at_mp
    small = jnp.concatenate(
        [
            vectors,
            hidden_bias,
            qkv_bias,
            jnp.zeros((SMALL_ROWS - QKV_ROW - GROUP, width), F32),
        ],
        0,
    )
    if inner > 1:
        shards = tuple(
            lax.all_gather(item, "dp", axis=0, tiled=True, axis_index_groups=groups)
            for item in shards
        )
        small = lax.psum(small, "dp", axis_index_groups=groups)

    out, along, input_grad, grad_a, grad_i, grad_d, sums = run_layer(
        inner, lengths, tokens, cotangent, shards, small
    )
    if inner > 1:
        grad_a, grad_i, grad_d = (
            lax.psum_scatter(
                item, "dp", scatter_dimension=0, tiled=True, axis_index_groups=groups
            )
            for item in (grad_a, grad_i, grad_d)
        )
        sums = lax.psum(sums, "dp", axis_index_groups=groups)

    columns = lax.dynamic_slice_in_dim(sums, dp * share, share, 1)
    bias_share = qv_bias.shape[2]
    bias_row = lax.dynamic_slice_in_dim(sums, QKV_ROW + mp, 1, 0)
    grad_qvb = jnp.stack(
        [
            lax.dynamic_slice_in_dim(bias_row, dp * bias_share, bias_share, 1),
            lax.dynamic_slice_in_dim(
                bias_row, 2 * head_cols + dp * bias_share, bias_share, 1
            ),
        ]
    )
    return (
        out,
        input_grad.astype(F32),
        along.astype(F32),
        grad_a[:, : 3 * head_cols].reshape(local_rows, 3, head_cols),
        grad_qvb,
        grad_a[:, 3 * head_cols :].T,
        grad_i,
        lax.dynamic_slice_in_dim(columns, BIAS_ROW + mp, 1, 0),
        grad_d.T,
        columns[0:2],
        columns[2:6],
    )


def solution(mesh):
    in_specs = (
        P("dp", None),
        P("dp", None),
        P("dp"),
        P("dp", None, "mp"),
        P(None, "mp", "dp"),
        P("mp", "dp"),
        P("dp", "mp"),
        P("mp", "dp"),
        P("mp", "dp"),
        P("mp", "dp"),
        P(None, "dp"),
        P(None, "dp"),
    )
    out_specs = (
        P("dp", None),
        P("dp", None),
        P("dp", None),
        P("dp", None, "mp"),
        P(None, "mp", "dp"),
        P("mp", "dp"),
        P("dp", "mp"),
        P("mp", "dp"),
        P("mp", "dp"),
        P(None, "dp"),
        P(None, "dp"),
    )
    return jax.shard_map(local, mesh=mesh, in_specs=in_specs, out_specs=out_specs, check_vma=False)
```

```python
import functools
import math

import jax
import jax.numpy as jnp
from jax import lax
from jax.experimental import pallas as pl
from jax.experimental.pallas import tpu as pltpu
from jax.sharding import PartitionSpec as P

HEAD_DIM = 64
SEQ_LEN = 256
EPSILON = 1e-06
NZ, NX, NY, NC = 4, 2, 2, 2
BLOCKS = NZ * NX
GROUP = NY * NC
SMALL_ROWS = 16
BIAS_ROW = 6
QKV_ROW = BIAS_ROW + GROUP
FWD_ROWS = 48
BWD_ROWS = 48
F32 = jnp.float32
BF16 = jnp.bfloat16
QKV, IN, DOWN, PILOT = range(4)


def nt(a, b):
    return lax.dot_general(a, b, (((1,), (1,)), ((), ())), preferred_element_type=F32)


def tn(a, b):
    return lax.dot_general(a, b, (((0,), (0,)), ((), ())), preferred_element_type=F32)


def nn(a, b):
    return jnp.dot(a, b, preferred_element_type=F32)


def one_hot(rows, columns, offset, dtype=BF16):
    row = lax.broadcasted_iota(jnp.int32, (rows, columns), 0)
    column = lax.broadcasted_iota(jnp.int32, (rows, columns), 1)
    return (row + offset == column).astype(F32).astype(dtype)


def row_mean(v):
    return jnp.mean(v, -1, keepdims=True)


def col_sum(v):
    return jnp.sum(v, 0, keepdims=True)


def layer_kernel(
    inner,
    lens,
    tok,
    cot,
    shard_i,
    shard_d,
    shard_p,
    w_qkv,
    w_out,
    gains,
    shifts,
    in_bias,
    qv_bias,
    out_o,
    along_o,
    ig_o,
    grad_a,
    grad_i,
    grad_d,
    small_sum,
    w_a,
    w_i,
    w_d,
    w_p,
    g_i,
    g_d,
    r_core,
    r_yf,
    r_xf,
    r_xs,
    r_ys,
    r_z,
    par,
    par_in,
    gs,
    gs_in,
    xs,
    cots,
    qkv,
    prob,
    ctx,
    acc,
    xh1,
    rs1,
    low,
    low_t,
    hid,
    gder,
    xh2,
    rs2,
    sgrad,
    bl,
    bl_t,
    qg,
    own,
    s_load,
    s_z,
    r_zs,
    s_x,
    r_x,
    s_y,
    r_y,
    s_dx,
    r_dx,
    s_dy,
    r_dy,
    s_c,
    r_c,
    s_rc,
    r_rc,
    s_red,
    r_red,
    s_rz,
    r_rz,
    s_sm,
    r_sm,
    s_out,
    r_out,
    s_own,
):
    weights = (w_a, w_i, w_d, w_p)
    width = xs.shape[1]
    block = w_a.shape[3]
    head_cols = ctx.shape[2]
    qkv_cols = 3 * head_cols
    heads_here = head_cols // HEAD_DIM
    rows = xs.shape[0]
    scale = HEAD_DIM ** (-0.5)

    dp = lax.axis_index("dp")
    mp = lax.axis_index("mp")
    spot = dp // inner
    rest = dp - spot * inner
    z, x = spot // NX, spot % NX
    y, c = mp // NC, mp % NC
    far_y, far_x, far_c = 1 - y, 1 - x, 1 - c
    mine = mp
    shards = (w_a.at[mine, z, x], shard_i, shard_d, shard_p)
    over_y = far_y * NC + c
    x_peer = {"dp": (z * NX + far_x) * inner + rest, "mp": mp}
    y_peer = {"dp": dp, "mp": over_y}
    c_peer = {"dp": dp, "mp": y * NC + far_c}

    def z_at(step):
        return (z + step) % NZ

    def z_from(step):
        return (z + NZ - step) % NZ

    def z_peer(step):
        return {"dp": (z_at(step) * NX + x) * inner + rest, "mp": mp}

    sends = []

    def remote(src, dst, send, recv, peer):
        return pltpu.make_async_remote_copy(
            src_ref=src,
            dst_ref=dst,
            send_sem=send,
            recv_sem=recv,
            device_id=peer,
            device_id_type=pl.DeviceIdType.MESH,
        )

    def push(src, dst, send, recv, peer, chunk=None):
        copy = remote(src, dst, send, recv, peer)
        copy.start()
        sends.append((chunk, copy))

    def arrived(dst, send, recv):
        remote(dst, dst, send, recv, c_peer).wait_recv()

    barrier = pltpu.get_barrier_semaphore()
    peers = [x_peer, y_peer, c_peer] + [z_peer(step) for step in range(1, NZ)]
    for peer in peers:
        pl.semaphore_signal(barrier, inc=1, device_id=peer, device_id_type=pl.DeviceIdType.MESH)

    for part in range(3):
        w_a[mine, z, x, :, part * head_cols : (part + 1) * head_cols] = w_qkv[part]
    w_a[mine, z, x, :, qkv_cols:] = nt(one_hot(block, block, 0), w_out[...]).astype(BF16)
    share = gains.shape[1]
    bias_share = qv_bias.shape[1]
    par[0] = jnp.zeros(par.shape[1:], F32)
    everyone = one_hot(share, width, spot * share)
    first_only = one_hot(share, width, jnp.where(mp == 0, spot * share, -width))
    par[0, 0:2, :] = nn(gains[...], first_only)
    par[0, 2:6, :] = nn(shifts[...], first_only)
    par[0, pl.ds(BIAS_ROW + mp, 1), :] = nn(in_bias[...], everyone)
    par[0, pl.ds(QKV_ROW + mp, 1), :] = nn(
        qv_bias[0:1, :], one_hot(bias_share, width, spot * bias_share)
    ) + nn(qv_bias[1:2, :], one_hot(bias_share, width, 2 * head_cols + spot * bias_share))

    pl.semaphore_wait(barrier, len(peers))

    loads = []
    for k in range(1, 4):
        loads.append(
            pltpu.make_async_copy(shards[k], weights[k].at[mine, z, x], s_load.at[k])
        )
    my_rows = pl.ds(mp * rows, rows)
    loads.append(pltpu.make_async_copy(tok.at[my_rows], xs, s_load.at[4]))
    loads.append(pltpu.make_async_copy(cot.at[my_rows], cots, s_load.at[5]))

    def send_z(k):
        for step in range(1, NZ):
            push(
                shards[k],
                weights[k].at[mine, z, x],
                s_z.at[k, step],
                r_zs.at[k, step],
                z_peer(step),
                k,
            )

    def send_own(k):
        for sem_s, sem_r, peer in ((s_x, r_x, x_peer), (s_y, r_y, y_peer)):
            push(shards[k], weights[k].at[mine, z, x], sem_s.at[k, 0], sem_r.at[k, 0], peer, k)

    def forward_z(k, step):
        src = weights[k].at[mine, z_from(step), x]
        arrived(src, s_z.at[k, step], r_zs.at[k, step])
        push(src, src, s_x.at[k, step], r_x.at[k, step], x_peer, k)
        push(src, src, s_y.at[k, step], r_y.at[k, step], y_peer, k)

    first = pl.ds(0, FWD_ROWS)
    second = pl.ds(FWD_ROWS, block - FWD_ROWS)

    def forward_diagonal(k, step):
        from_x = weights[k].at[mine, z_from(step), far_x]
        arrived(from_x, s_x.at[k, step], r_x.at[k, step])
        part = weights[k].at[mine, z_from(step), far_x, first]
        push(part, part, s_dy.at[k, step], r_dy.at[k, step], y_peer, k)
        from_y = weights[k].at[over_y, z_from(step), x]
        arrived(from_y, s_y.at[k, step], r_y.at[k, step])
        part = weights[k].at[over_y, z_from(step), x, second]
        push(part, part, s_dx.at[k, step], r_dx.at[k, step], x_peer, k)

    def to_core(k, index, block_index, column):
        src = weights[k].at[block_index, :, column]
        push(src, src, s_c.at[k, index], r_c.at[k, index], c_peer, k)

    def side_z(k):
        for step in range(1, NZ):
            src = weights[k].at[mine, z, far_x]
            push(src, src, s_x.at[k, step], r_x.at[k, step], z_peer(step), k)
            src = weights[k].at[over_y, z, x]
            push(src, src, s_y.at[k, step], r_y.at[k, step], z_peer(step), k)

    def corner_z(k):
        arrived(weights[k].at[over_y, z, far_x, first], s_dy.at[k, 0], r_dy.at[k, 0])
        arrived(weights[k].at[over_y, z, far_x, second], s_dx.at[k, 0], r_dx.at[k, 0])
        src = weights[k].at[over_y, z, far_x]
        for step in range(1, NZ):
            push(src, src, s_dx.at[k, step], r_dx.at[k, step], z_peer(step), k)

    def finish_z(k):
        for step in range(1, NZ):
            at = z_from(step)
            arrived(weights[k].at[mine, at, x], s_z.at[k, step], r_zs.at[k, step])
            arrived(weights[k].at[mine, at, far_x], s_x.at[k, step], r_x.at[k, step])
            arrived(weights[k].at[over_y, at, x], s_y.at[k, step], r_y.at[k, step])
            arrived(weights[k].at[over_y, at, far_x], s_dx.at[k, step], r_dx.at[k, step])
        to_core(k, 0, mine, x)
        columns_to_core(k)
        exchange_core(k)

    def columns_to_core(k):
        to_core(k, 1, mine, far_x)
        to_core(k, 2, over_y, x)

    def finish(k):
        for step in range(NZ):
            arrived(
                weights[k].at[over_y, z_from(step), far_x, first],
                s_dy.at[k, step],
                r_dy.at[k, step],
            )
            arrived(
                weights[k].at[over_y, z_from(step), far_x, second],
                s_dx.at[k, step],
                r_dx.at[k, step],
            )
        exchange_core(k)

    def exchange_core(k):
        to_core(k, 3, over_y, far_x)
        for index, (block_index, column) in enumerate(
            (
                (y * NC + far_c, x),
                (y * NC + far_c, far_x),
                (far_y * NC + far_c, x),
                (far_y * NC + far_c, far_x),
            )
        ):
            arrived(
                weights[k].at[block_index, :, column], s_c.at[k, index], r_c.at[k, index]
            )

    def small_stage(which, buf, buf_in, stage):
        if stage < 3:
            peer = (c_peer, y_peer, x_peer)[stage]
            push(buf.at[stage], buf_in.at[stage], s_sm.at[which, stage], r_sm.at[which, stage], peer)
        else:
            for step in range(1, NZ):
                push(
                    buf.at[3],
                    buf_in.at[2 + step],
                    s_sm.at[which, 2 + step],
                    r_sm.at[which, 2 + step],
                    z_peer(step),
                )

    def small_add(which, buf, buf_in, stage):
        arrived(buf_in.at[stage], s_sm.at[which, stage], r_sm.at[which, stage])
        buf[stage + 1] = buf[stage] + buf_in[stage]

    def small_last(which, buf, buf_in):
        for step in range(1, NZ):
            arrived(buf_in.at[2 + step], s_sm.at[which, 2 + step], r_sm.at[which, 2 + step])
        total = jnp.zeros(buf.shape[1:], F32)
        for place in range(NZ):
            term = buf[3]
            for step in range(1, NZ):
                term = jnp.where(z_from(step) == place, buf_in[2 + step], term)
            total = total + term
        return total

    send_z(QKV)
    for copy in loads:
        copy.start()
    send_own(QKV)
    small_stage(0, par, par_in, 0)
    send_own(IN)
    small_add(0, par, par_in, 0)
    small_stage(0, par, par_in, 1)
    send_own(DOWN)
    forward_z(QKV, 1)
    small_add(0, par, par_in, 1)
    small_stage(0, par, par_in, 2)
    send_own(PILOT)
    forward_diagonal(QKV, 0)
    forward_z(QKV, 3)
    small_add(0, par, par_in, 2)
    small_stage(0, par, par_in, 3)
    forward_diagonal(QKV, 1)
    forward_z(QKV, 2)
    send_z(IN)
    for copy in loads:
        copy.wait()
    to_core(QKV, 0, mine, x)
    forward_diagonal(QKV, 3)
    forward_z(IN, 1)
    forward_diagonal(QKV, 2)
    columns_to_core(QKV)
    forward_z(IN, 3)
    forward_diagonal(IN, 0)
    forward_z(IN, 2)
    to_core(IN, 0, mine, x)
    send_z(DOWN)
    par[4] = small_last(0, par, par_in)
    finish(QKV)

    length = lens[mp]
    key_keep = lax.broadcasted_iota(jnp.int32, (rows, rows), 1) < length
    row_keep = (lax.broadcasted_iota(jnp.int32, (rows, 1), 0) < length).astype(F32)

    def par_row(index):
        return par[4, index : index + 1, :]

    def square(ref, m, start, stop):
        value = ref[m, :, :, :, start:stop]
        return value.reshape(width, stop - start)

    def project(m, carry):
        bias = par[4, pl.ds(QKV_ROW + m, 1), :qkv_cols]
        qkv[m] = (nn(xs[...], square(w_a, m, 0, qkv_cols)) + bias).astype(BF16)
        return carry

    lax.fori_loop(0, GROUP, project, 0)

    def attend(m, carry):
        part = qkv[m]
        for h in range(heads_here):
            lo = h * HEAD_DIM
            q = part[:, lo : lo + HEAD_DIM]
            k = part[:, head_cols + lo : head_cols + lo + HEAD_DIM]
            v = part[:, 2 * head_cols + lo : 2 * head_cols + lo + HEAD_DIM]
            score = jnp.where(key_keep, nt(q, k) * scale, -1000000000.0)
            expo = jnp.exp(score - jnp.max(score, -1, keepdims=True))
            weight = expo / jnp.sum(expo, -1, keepdims=True)
            prob[m * heads_here + h] = weight
            ctx[m, :, lo : lo + HEAD_DIM] = nn(weight.astype(BF16), v).astype(BF16)
        return carry

    forward_diagonal(IN, 1)
    forward_diagonal(IN, 3)
    forward_z(DOWN, 1)
    forward_diagonal(PILOT, 0)
    lax.fori_loop(0, NY, attend, 0)
    forward_diagonal(IN, 2)
    columns_to_core(IN)
    forward_z(DOWN, 3)
    send_z(PILOT)
    side_z(PILOT)
    forward_diagonal(DOWN, 0)
    lax.fori_loop(NY, GROUP, attend, 0)

    acc[...] = jnp.zeros_like(acc)

    def attended(m, carry):
        acc[...] += nt(ctx[m], square(w_a, m, qkv_cols, width))
        return carry

    lax.fori_loop(0, GROUP, attended, 0)
    opening = xs[...].astype(F32) + acc[...] + par_row(2)
    centered = opening - row_mean(opening)
    rstd = lax.rsqrt(row_mean(centered * centered) + EPSILON)
    rs1[...] = rstd
    xhat = centered * rstd
    xh1[...] = xhat
    normed_low = (xhat * par_row(0) + par_row(3)).astype(BF16)
    low[...] = normed_low
    forward_z(DOWN, 2)
    to_core(DOWN, 0, mine, x)
    forward_diagonal(DOWN, 1)
    finish(IN)
    forward_diagonal(DOWN, 3)
    corner_z(PILOT)

    def expand(m, carry):
        pre = nn(low[...], square(w_i, m, 0, width)) + par[4, pl.ds(BIAS_ROW + m, 1), :]
        gate = 0.5 + 0.5 * lax.erf(pre * math.sqrt(0.5))
        hid[m] = (pre * gate).astype(BF16)
        gder[m] = gate + pre * (jnp.exp(-0.5 * pre * pre) * (1.0 / math.sqrt(2.0 * math.pi)))
        return carry

    lax.fori_loop(0, GROUP, expand, 0)
    low_t[...] = low[...].T
    forward_diagonal(DOWN, 2)
    columns_to_core(DOWN)
    finish(DOWN)

    acc[...] = xh1[...] * par_row(0) + par_row(3) + par_row(4)

    def contract(m, carry):
        acc[...] += nt(hid[m], square(w_d, m, 0, width))
        return carry

    lax.fori_loop(0, GROUP, contract, 0)
    stream = acc[...]
    centered = stream - row_mean(stream)
    rstd = lax.rsqrt(row_mean(centered * centered) + EPSILON)
    rs2[...] = rstd
    xhat = centered * rstd
    xh2[...] = xhat
    own[0] = (xhat * par_row(1) + par_row(5)).astype(BF16)

    outs = (out_o, along_o, ig_o)

    def send_result(index):
        dst = outs[index].at[my_rows]
        pltpu.make_async_copy(own.at[index], dst, s_own.at[index]).start()
        push(own.at[index], dst, s_out.at[index, 0], r_out.at[index, 0], y_peer)
        push(own.at[index], dst, s_out.at[index, 1], r_out.at[index, 1], c_peer)

    def forward_result(index):
        part = outs[index].at[pl.ds(over_y * rows, rows)]
        arrived(part, s_out.at[index, 0], r_out.at[index, 0])
        push(part, part, s_out.at[index, 2], r_out.at[index, 2], c_peer)

    def finish_result(index):
        pltpu.make_async_copy(own.at[index], outs[index].at[my_rows], s_own.at[index]).wait()
        near = outs[index].at[pl.ds((y * NC + far_c) * rows, rows)]
        arrived(near, s_out.at[index, 1], r_out.at[index, 1])
        far = outs[index].at[pl.ds((far_y * NC + far_c) * rows, rows)]
        arrived(far, s_out.at[index, 2], r_out.at[index, 2])

    send_result(0)

    gs[0] = jnp.zeros(gs.shape[1:], F32)

    def norm_back(grad, xhat, rstd, gain):
        hat = grad * gain
        return rstd * (hat - row_mean(hat) - xhat * row_mean(hat * xhat))

    masked = cots[...].astype(F32) * row_keep
    xhat = xh2[...]
    gs[0, 1:2, :] = col_sum(masked * xhat)
    gs[0, 5:6, :] = col_sum(masked)
    stream_grad = norm_back(masked, xhat, rs2[...], par_row(1))
    gs[0, 4:5, :] = col_sum(stream_grad)
    sgrad[...] = stream_grad
    bl[...] = stream_grad.astype(BF16)
    bl_t[...] = bl[...].T
    acc[...] = stream_grad

    def block_of(i):
        return i * NC + far_c if i < NY else (i - NY) * NC + c

    slab = NX * block

    def outer(left_t, right, ref, m, start, stop):
        def one(zz, carry):
            top = pl.multiple_of(zz * slab, slab)
            value = nn(left_t[pl.ds(top, slab), :], right[...])
            ref[m, zz, :, :, start:stop] = value.astype(BF16).reshape(NX, block, stop - start)
            return carry

        lax.fori_loop(0, NZ, one, 0)

    def to_partner(ref, k, i):
        src = ref.at[i * NC + far_c]
        copy = remote(src, r_core.at[k, i], s_rc.at[k, i], r_rc.at[k, i], c_peer)
        return copy

    pre_low = own.at[1]

    def back_ff(i):
        m = block_of(i)
        grad = nn(bl[...], square(w_d, m, 0, width)) * gder[m]
        pre_low[...] = grad.astype(BF16)
        gs[0, pl.ds(BIAS_ROW + m, 1), :] = col_sum(pre_low[...].astype(F32))
        outer(low_t, pre_low, g_i, m, 0, width)
        acc[...] += nt(pre_low[...], square(w_i, m, 0, width))

        if i < NY:
            to_partner(g_i, 1, i).start()


    top_rows = pl.ds(0, BWD_ROWS)
    low_rows = pl.ds(BWD_ROWS, block - BWD_ROWS)

    def add_core(k, ref):
        for yy in range(NY):
            m = yy * NC + c
            to_partner(ref, k, yy).wait_recv()

            def one(zz, carry):
                ref[m, zz] = ref[m, zz] + r_core[k, yy, zz]
                return carry

            lax.fori_loop(0, NZ, one, 0)

    def reduce_first(k, ref):
        push(
            ref.at[over_y, :, :, top_rows], r_yf.at[k], s_red.at[k, 0], r_red.at[k, 0], y_peer
        )
        for yy in range(NY):
            push(
                ref.at[yy * NC + c, :, far_x, low_rows],
                r_xf.at[k, yy],
                s_red.at[k, 1 + yy],
                r_red.at[k, 1 + yy],
                x_peer,
            )

    def reduce_second(k, ref):
        arrived(r_yf.at[k], s_red.at[k, 0], r_red.at[k, 0])
        ref[mine, :, :, top_rows, :] = ref[mine, :, :, top_rows, :] + r_yf[k]
        push(
            ref.at[mine, :, far_x, top_rows], r_xs.at[k], s_red.at[k, 3], r_red.at[k, 3], x_peer
        )
        for yy in range(NY):
            m = yy * NC + c
            arrived(r_xf.at[k, yy], s_red.at[k, 1 + yy], r_red.at[k, 1 + yy])
            ref[m, :, x, low_rows, :] = ref[m, :, x, low_rows, :] + r_xf[k, yy]
        push(
            ref.at[over_y, :, x, low_rows], r_ys.at[k], s_red.at[k, 4], r_red.at[k, 4], y_peer
        )

    def reduce_third(k, ref):
        arrived(r_xs.at[k], s_red.at[k, 3], r_red.at[k, 3])
        ref[mine, :, x, top_rows, :] = ref[mine, :, x, top_rows, :] + r_xs[k]
        arrived(r_ys.at[k], s_red.at[k, 4], r_red.at[k, 4])
        ref[mine, :, x, low_rows, :] = ref[mine, :, x, low_rows, :] + r_ys[k]
        for step in range(1, NZ):
            push(
                ref.at[mine, z_at(step), x],
                r_z.at[k, step - 1],
                s_rz.at[k, step],
                r_rz.at[k, step],
                z_peer(step),
            )

    def reduce_last(k, ref, result):
        total = ref[mine, z, x].astype(F32)
        for step in range(1, NZ):
            arrived(r_z.at[k, step - 1], s_rz.at[k, step], r_rz.at[k, step])
            total = total + r_z[k, step - 1].astype(F32)
        result[...] = total

    for i in range(GROUP):
        outer(bl_t, hid.at[block_of(i)], g_d, block_of(i), 0, width)
        if i < NY:
            to_partner(g_d, 0, i).start()
    add_core(0, g_d)
    reduce_first(0, g_d)
    for i in range(GROUP):
        back_ff(i)
    add_core(1, g_i)
    reduce_first(1, g_i)
    forward_result(0)

    xhat = xh1[...]
    normed_grad = acc[...]
    gs[0, 0:1, :] = col_sum(normed_grad * xhat)
    gs[0, 3:4, :] = col_sum(normed_grad)
    first_grad = norm_back(normed_grad, xhat, rs1[...], par_row(0))
    gs[0, 2:3, :] = col_sum(first_grad)
    acc[...] = first_grad
    bl[...] = first_grad.astype(BF16)
    bl_t[...] = bl[...].T
    low_t[...] = xs[...].T
    g_a = w_d

    def back_attention(i):
        m = block_of(i)
        outer(bl_t, ctx.at[m], g_a, m, qkv_cols, width)
        context_grad = nn(bl[...], square(w_a, m, qkv_cols, width)).astype(BF16)
        part = qkv[m]
        for h in range(heads_here):
            lo = h * HEAD_DIM
            q = part[:, lo : lo + HEAD_DIM]
            k = part[:, head_cols + lo : head_cols + lo + HEAD_DIM]
            v = part[:, 2 * head_cols + lo : 2 * head_cols + lo + HEAD_DIM]
            d_ctx = context_grad[:, lo : lo + HEAD_DIM]
            weight = prob[m * heads_here + h]
            d_value = tn(weight.astype(BF16), d_ctx)
            d_prob = nt(d_ctx, v)
            spread = jnp.sum(weight * d_prob, -1, keepdims=True)
            d_score = (weight * (d_prob - spread)).astype(BF16)
            qg[:, lo : lo + HEAD_DIM] = (nn(d_score, k) * scale).astype(BF16)
            qg[:, head_cols + lo : head_cols + lo + HEAD_DIM] = (tn(d_score, q) * scale).astype(BF16)
            qg[:, 2 * head_cols + lo : 2 * head_cols + lo + HEAD_DIM] = d_value.astype(BF16)
        gs[0, pl.ds(QKV_ROW + m, 1), :qkv_cols] = col_sum(qg[...].astype(F32))
        outer(low_t, qg, g_a, m, 0, qkv_cols)
        acc[...] += nt(qg[...], square(w_a, m, 0, qkv_cols))

        if i < NY:
            to_partner(g_a, 2, i).start()

    for chunk, copy in sends:
        if chunk == DOWN:
            copy.wait_send()
    for i in range(GROUP):
        back_attention(i)
        if i == 2:
            reduce_second(0, g_d)
    own[2] = acc[...].astype(BF16)
    small_stage(1, gs, gs_in, 0)
    add_core(2, g_a)
    reduce_second(1, g_i)
    reduce_first(2, g_a)
    small_add(1, gs, gs_in, 0)
    small_stage(1, gs, gs_in, 1)
    reduce_third(0, g_d)
    finish_z(PILOT)
    acc[...] = jnp.zeros_like(acc)

    def steer(m, carry):
        acc[...] += nt(hid[m], square(w_p, m, 0, width))
        return carry

    lax.fori_loop(0, GROUP, steer, 0)
    tangent = acc[...]
    xhat = xh2[...]
    along = rs2[...] * (tangent - row_mean(tangent) - xhat * row_mean(tangent * xhat))
    own[1] = (par_row(1) * along).astype(BF16)
    reduce_third(1, g_i)
    reduce_second(2, g_a)
    small_add(1, gs, gs_in, 1)
    small_stage(1, gs, gs_in, 2)
    send_result(2)
    send_result(1)
    reduce_last(0, g_d, grad_d)
    small_add(1, gs, gs_in, 2)
    small_stage(1, gs, gs_in, 3)
    reduce_third(2, g_a)
    reduce_last(1, g_i, grad_i)
    forward_result(2)
    forward_result(1)
    small_sum[...] = small_last(1, gs, gs_in)
    reduce_last(2, g_a, grad_a)
    for index in range(3):
        finish_result(index)
    for k, ref in enumerate((g_d, g_i, g_a)):
        for i in range(NY):
            to_partner(ref, k, i).wait_send()
    for chunk, copy in sends:
        if chunk != DOWN:
            copy.wait_send()


def run_layer(inner, lens, tok, cot, shards, projections, small):
    width = tok.shape[1]
    rows = tok.shape[0] // GROUP
    block = width // BLOCKS
    head_cols = width // GROUP
    qkv_cols = 3 * head_cols
    heads = width // HEAD_DIM
    anywhere = pl.BlockSpec(memory_space=pl.ANY)
    vmem = pl.BlockSpec(memory_space=pltpu.VMEM)
    weight = pltpu.VMEM((GROUP, NZ, NX, block, width), BF16)
    act = pltpu.VMEM((rows, width), F32)
    act_low = pltpu.VMEM((rows, width), BF16)
    column = pltpu.VMEM((rows, 1), F32)
    dma = pltpu.SemaphoreType.DMA
    grads = 3
    scratch = (
        [weight] * 6
        + [
            pltpu.VMEM((grads, NY, NZ, NX, block, width), BF16),
            pltpu.VMEM((grads, NZ, NX, BWD_ROWS, width), BF16),
            pltpu.VMEM((grads, NY, NZ, block - BWD_ROWS, width), BF16),
            pltpu.VMEM((grads, NZ, BWD_ROWS, width), BF16),
            pltpu.VMEM((grads, NZ, block - BWD_ROWS, width), BF16),
            pltpu.VMEM((grads, NZ - 1, block, width), BF16),
            pltpu.VMEM((5, SMALL_ROWS, width), F32),
            pltpu.VMEM((6, SMALL_ROWS, width), F32),
            pltpu.VMEM((4, SMALL_ROWS, width), F32),
            pltpu.VMEM((6, SMALL_ROWS, width), F32),
            act_low,
            act_low,
            pltpu.VMEM((GROUP, rows, qkv_cols), BF16),
            pltpu.VMEM((heads, rows, rows), F32),
            pltpu.VMEM((GROUP, rows, head_cols), BF16),
            act,
            act,
            column,
            act_low,
            pltpu.VMEM((width, rows), BF16),
            pltpu.VMEM((GROUP, rows, width), BF16),
            pltpu.VMEM((GROUP, rows, width), F32),
            act,
            column,
            act,
            act_low,
            pltpu.VMEM((width, rows), BF16),
            pltpu.VMEM((rows, qkv_cols), BF16),
            pltpu.VMEM((3, rows, width), BF16),
        ]
        + [dma((7,))]
        + [dma((4, NZ))] * 12
        + [dma((grads, NY))] * 2
        + [dma((grads, 5))] * 2
        + [dma((grads, NZ))] * 2
        + [dma((2, 6))] * 2
        + [dma((3, 3))] * 2
        + [dma((3,))]
    )
    whole = jax.ShapeDtypeStruct(tok.shape, BF16)
    piece = jax.ShapeDtypeStruct((block, width), F32)
    return pl.pallas_call(
        functools.partial(layer_kernel, inner),
        out_shape=(
            whole,
            whole,
            whole,
            piece,
            piece,
            piece,
            jax.ShapeDtypeStruct((SMALL_ROWS, width), F32),
        ),
        in_specs=[pl.BlockSpec(memory_space=pltpu.SMEM)] + [anywhere] * 5 + [vmem] * 6,
        out_specs=(anywhere,) * 3 + (vmem,) * 4,
        scratch_shapes=scratch,
        compiler_params=pltpu.CompilerParams(
            collective_id=0, has_side_effects=True, vmem_limit_bytes=67043328
        ),
        name="layer",
    )(lens, tok, cot, *shards, *projections, *small)


def finish_kernel(
    out,
    input_grad,
    along,
    grad_a,
    grad_i,
    grad_d,
    sums,
    out_o,
    input_grad_o,
    along_o,
    grad_qkv_o,
    grad_out_o,
    grad_i_o,
    grad_d_o,
    grad_gains_o,
    grad_shifts_o,
    grad_in_bias_o,
    grad_qvb_o,
):
    out_o[...] = out[...]
    input_grad_o[...] = input_grad[...].astype(F32)
    along_o[...] = along[...].astype(F32)

    @pl.when(pl.program_id(0) == 0)
    def _():
        dp = lax.axis_index("dp")
        mp = lax.axis_index("mp")
        rows, width = grad_a.shape
        head_cols = grad_out_o.shape[0]
        exact = lax.Precision.HIGHEST

        def pick(values, share, offset):
            places = one_hot(share, width, offset, F32)
            return lax.dot_general(
                values,
                places,
                (((1,), (1,)), ((), ())),
                precision=exact,
                preferred_element_type=F32,
            )

        for part in range(3):
            grad_qkv_o[part] = grad_a[:, part * head_cols : (part + 1) * head_cols]
        grad_out_o[...] = lax.dot_general(
            grad_a[:, 3 * head_cols :],
            one_hot(rows, rows, 0, F32),
            (((0,), (0,)), ((), ())),
            precision=exact,
            preferred_element_type=F32,
        )
        grad_i_o[...] = grad_i[...]
        grad_d_o[...] = grad_d[...]
        share = grad_gains_o.shape[1]
        bias_share = grad_qvb_o.shape[1]
        norms = pick(sums[0:8, :], share, dp * share)
        grad_gains_o[...] = norms[0:2]
        grad_shifts_o[...] = norms[2:6]
        grad_in_bias_o[...] = pick(sums[pl.ds(BIAS_ROW + mp, 1), :], share, dp * share)
        row = sums[pl.ds(QKV_ROW + mp, 1), :]
        grad_qvb_o[0:1, :] = pick(row, bias_share, dp * bias_share)
        grad_qvb_o[1:2, :] = pick(row, bias_share, 2 * head_cols + dp * bias_share)


def run_finish(
    out, input_grad, along, grad_a, grad_i, grad_d, sums, head_cols, share, bias_share
):
    steps = 4
    rows, width = out.shape
    local_rows = grad_a.shape[0]

    def whole(*shape):
        return pl.BlockSpec(shape, lambda i: (0,) * len(shape))

    slab = pl.BlockSpec((rows // steps, width), lambda i: (i, 0))
    shapes = (
        (3, local_rows, head_cols),
        (head_cols, local_rows),
        (local_rows, width),
        (local_rows, width),
        (2, share),
        (4, share),
        (1, share),
        (2, bias_share),
    )
    return pl.pallas_call(
        finish_kernel,
        grid=(steps,),
        out_shape=(
            jax.ShapeDtypeStruct(out.shape, BF16),
            jax.ShapeDtypeStruct(out.shape, F32),
            jax.ShapeDtypeStruct(out.shape, F32),
        )
        + tuple(jax.ShapeDtypeStruct(shape, F32) for shape in shapes),
        in_specs=[slab] * 3 + [whole(local_rows, width)] * 3 + [whole(*sums.shape)],
        out_specs=(slab,) * 3 + tuple(whole(*shape) for shape in shapes),
        name="finish",
    )(out, input_grad, along, grad_a, grad_i, grad_d, sums)


def local(
    tokens, cotangent, lengths, w_qkv, qv_bias, w_out, w_in, in_bias, w_down, pilot, gains, shifts
):
    n_dp = lax.axis_size("dp")
    inner = n_dp // BLOCKS
    groups = [[b * inner + i for i in range(inner)] for b in range(BLOCKS)]
    head_cols = w_out.shape[0]
    local_rows = w_qkv.shape[0]
    shards = (w_in, w_down.T, pilot.T)
    projections = (w_qkv.transpose(1, 0, 2), w_out)
    small = (gains, shifts, in_bias, qv_bias.reshape(2, -1))
    if inner > 1:

        def joined(item, axis):
            return lax.all_gather(item, "dp", axis=axis, tiled=True, axis_index_groups=groups)

        shards = tuple(joined(item, 0) for item in shards)
        projections = tuple(joined(item, 1) for item in projections)
        small = tuple(joined(item, 1) for item in small)

    out, along, input_grad, grad_a, grad_i, grad_d, sums = run_layer(
        inner, lengths, tokens, cotangent, shards, projections, small
    )
    if inner > 1:
        grad_a, grad_i, grad_d = (
            lax.psum_scatter(
                item, "dp", scatter_dimension=0, tiled=True, axis_index_groups=groups
            )
            for item in (grad_a, grad_i, grad_d)
        )
        sums = lax.psum(sums, "dp", axis_index_groups=groups)
    (
        out,
        input_grad,
        along,
        grad_qkv,
        grad_out,
        grad_i,
        grad_d,
        grad_gains,
        grad_shifts,
        grad_in_bias,
        grad_qvb,
    ) = run_finish(
        out, input_grad, along, grad_a, grad_i, grad_d, sums, head_cols, gains.shape[1], qv_bias.shape[2]
    )
    return (
        out,
        input_grad,
        along,
        grad_qkv.transpose(1, 0, 2),
        grad_qvb.reshape(qv_bias.shape),
        grad_out,
        grad_i,
        grad_in_bias,
        grad_d.T,
        grad_gains,
        grad_shifts,
    )


def solution(mesh):
    in_specs = (
        P("dp", None),
        P("dp", None),
        P("dp"),
        P("dp", None, "mp"),
        P(None, "mp", "dp"),
        P("mp", "dp"),
        P("dp", "mp"),
        P("mp", "dp"),
        P("mp", "dp"),
        P("mp", "dp"),
        P(None, "dp"),
        P(None, "dp"),
    )
    out_specs = (
        P("dp", None),
        P("dp", None),
        P("dp", None),
        P("dp", None, "mp"),
        P(None, "mp", "dp"),
        P("mp", "dp"),
        P("dp", "mp"),
        P("mp", "dp"),
        P("mp", "dp"),
        P(None, "dp"),
        P(None, "dp"),
    )
    return jax.shard_map(local, mesh=mesh, in_specs=in_specs, out_specs=out_specs, check_vma=False)
```

```python
import functools
import math

import jax
import jax.numpy as jnp
from jax import lax
from jax.experimental import pallas as pl
from jax.experimental.pallas import tpu as pltpu
from jax.sharding import PartitionSpec as P

HEAD_DIM = 64
SEQ_LEN = 256
EPSILON = 1e-06
NZ, NX, NY, NC = 4, 2, 2, 2
BLOCKS = NZ * NX
GROUP = NY * NC
SMALL_ROWS = 16
BIAS_ROW = 6
QKV_ROW = BIAS_ROW + GROUP
FWD_ROWS = 48
BWD_ROWS = 48
DEEP_ROWS = 32
F32 = jnp.float32
BF16 = jnp.bfloat16
QKV, IN, DOWN, PILOT = range(4)


def nt(a, b):
    return lax.dot_general(a, b, (((1,), (1,)), ((), ())), preferred_element_type=F32)


def tn(a, b):
    return lax.dot_general(a, b, (((0,), (0,)), ((), ())), preferred_element_type=F32)


def nn(a, b):
    return jnp.dot(a, b, preferred_element_type=F32)


def one_hot(rows, columns, offset, dtype=BF16):
    row = lax.broadcasted_iota(jnp.int32, (rows, columns), 0)
    column = lax.broadcasted_iota(jnp.int32, (rows, columns), 1)
    return (row + offset == column).astype(F32).astype(dtype)


def row_mean(v):
    return jnp.mean(v, -1, keepdims=True)


def col_sum(v):
    return jnp.sum(v, 0, keepdims=True)


def layer_kernel(
    inner,
    lens,
    tok,
    cot,
    shard_i,
    shard_d,
    shard_p,
    w_qkv,
    w_out,
    gains,
    shifts,
    in_bias,
    qv_bias,
    out_o,
    along_o,
    ig_o,
    grad_a,
    grad_i,
    grad_d,
    small_sum,
    w_a,
    w_i,
    w_d,
    w_p,
    g_i,
    g_d,
    r_core,
    r_yf,
    r_xf,
    r_xs,
    r_ys,
    r_z,
    r_deep,
    r_plane,
    par,
    par_in,
    gs,
    gs_in,
    xs,
    cots,
    qkv,
    prob,
    ctx,
    acc,
    xh1,
    rs1,
    low,
    low_t,
    hid,
    gder,
    xh2,
    rs2,
    sgrad,
    bl,
    bl_t,
    qg,
    own,
    s_load,
    s_z,
    r_zs,
    s_x,
    r_x,
    s_y,
    r_y,
    s_dx,
    r_dx,
    s_dy,
    r_dy,
    s_c,
    r_c,
    s_rc,
    r_rc,
    s_red,
    r_red,
    s_rz,
    r_rz,
    s_deep,
    r_deeps,
    s_plane,
    r_planes,
    s_sm,
    r_sm,
    s_out,
    r_out,
    s_own,
):
    weights = (w_a, w_i, w_d, w_p)
    width = xs.shape[1]
    block = w_a.shape[3]
    head_cols = ctx.shape[2]
    qkv_cols = 3 * head_cols
    heads_here = head_cols // HEAD_DIM
    rows = xs.shape[0]
    scale = HEAD_DIM ** (-0.5)

    dp = lax.axis_index("dp")
    mp = lax.axis_index("mp")
    spot = dp // inner
    rest = dp - spot * inner
    z, x = spot // NX, spot % NX
    y, c = mp // NC, mp % NC
    far_y, far_x, far_c = 1 - y, 1 - x, 1 - c
    mine = mp
    shards = (w_a.at[mine, z, x], shard_i, shard_d, shard_p)
    over_y = far_y * NC + c
    x_peer = {"dp": (z * NX + far_x) * inner + rest, "mp": mp}
    y_peer = {"dp": dp, "mp": over_y}
    c_peer = {"dp": dp, "mp": y * NC + far_c}
    corner_peer = {"dp": x_peer["dp"], "mp": over_y}

    def z_at(step):
        return (z + step) % NZ

    def z_from(step):
        return (z + NZ - step) % NZ

    def z_peer(step):
        return {"dp": (z_at(step) * NX + x) * inner + rest, "mp": mp}

    sends = []

    def remote(src, dst, send, recv, peer):
        return pltpu.make_async_remote_copy(
            src_ref=src,
            dst_ref=dst,
            send_sem=send,
            recv_sem=recv,
            device_id=peer,
            device_id_type=pl.DeviceIdType.MESH,
        )

    def push(src, dst, send, recv, peer, chunk=None):
        copy = remote(src, dst, send, recv, peer)
        copy.start()
        sends.append((chunk, copy))

    def arrived(dst, send, recv):
        remote(dst, dst, send, recv, c_peer).wait_recv()

    barrier = pltpu.get_barrier_semaphore()
    peers = [x_peer, y_peer, c_peer, corner_peer] + [z_peer(step) for step in range(1, NZ)]
    for peer in peers:
        pl.semaphore_signal(barrier, inc=1, device_id=peer, device_id_type=pl.DeviceIdType.MESH)

    for part in range(3):
        w_a[mine, z, x, :, part * head_cols : (part + 1) * head_cols] = w_qkv[part]
    w_a[mine, z, x, :, qkv_cols:] = nt(one_hot(block, block, 0), w_out[...]).astype(BF16)
    share = gains.shape[1]
    bias_share = qv_bias.shape[1]
    par[0] = jnp.zeros(par.shape[1:], F32)
    everyone = one_hot(share, width, spot * share)
    first_only = one_hot(share, width, jnp.where(mp == 0, spot * share, -width))
    par[0, 0:2, :] = nn(gains[...], first_only)
    par[0, 2:6, :] = nn(shifts[...], first_only)
    par[0, pl.ds(BIAS_ROW + mp, 1), :] = nn(in_bias[...], everyone)
    par[0, pl.ds(QKV_ROW + mp, 1), :] = nn(
        qv_bias[0:1, :], one_hot(bias_share, width, spot * bias_share)
    ) + nn(qv_bias[1:2, :], one_hot(bias_share, width, 2 * head_cols + spot * bias_share))

    pl.semaphore_wait(barrier, len(peers))

    loads = []
    for k in range(1, 4):
        loads.append(
            pltpu.make_async_copy(shards[k], weights[k].at[mine, z, x], s_load.at[k])
        )
    my_rows = pl.ds(mp * rows, rows)
    loads.append(pltpu.make_async_copy(tok.at[my_rows], xs, s_load.at[4]))
    loads.append(pltpu.make_async_copy(cot.at[my_rows], cots, s_load.at[5]))

    def send_z(k):
        for step in range(1, NZ):
            push(
                shards[k],
                weights[k].at[mine, z, x],
                s_z.at[k, step],
                r_zs.at[k, step],
                z_peer(step),
                k,
            )

    def send_own(k):
        for sem_s, sem_r, peer in ((s_x, r_x, x_peer), (s_y, r_y, y_peer)):
            push(shards[k], weights[k].at[mine, z, x], sem_s.at[k, 0], sem_r.at[k, 0], peer, k)

    def forward_z(k, step):
        src = weights[k].at[mine, z_from(step), x]
        arrived(src, s_z.at[k, step], r_zs.at[k, step])
        push(src, src, s_x.at[k, step], r_x.at[k, step], x_peer, k)
        push(src, src, s_y.at[k, step], r_y.at[k, step], y_peer, k)

    first = pl.ds(0, FWD_ROWS)
    second = pl.ds(FWD_ROWS, block - FWD_ROWS)

    def forward_diagonal(k, step):
        from_x = weights[k].at[mine, z_from(step), far_x]
        arrived(from_x, s_x.at[k, step], r_x.at[k, step])
        part = weights[k].at[mine, z_from(step), far_x, first]
        push(part, part, s_dy.at[k, step], r_dy.at[k, step], y_peer, k)
        from_y = weights[k].at[over_y, z_from(step), x]
        arrived(from_y, s_y.at[k, step], r_y.at[k, step])
        part = weights[k].at[over_y, z_from(step), x, second]
        push(part, part, s_dx.at[k, step], r_dx.at[k, step], x_peer, k)

    def to_core(k, index, block_index, column):
        src = weights[k].at[block_index, :, column]
        push(src, src, s_c.at[k, index], r_c.at[k, index], c_peer, k)

    def side_z(k):
        for step in range(1, NZ):
            src = weights[k].at[mine, z, far_x]
            push(src, src, s_x.at[k, step], r_x.at[k, step], z_peer(step), k)
            src = weights[k].at[over_y, z, x]
            push(src, src, s_y.at[k, step], r_y.at[k, step], z_peer(step), k)

    def corner_z(k):
        arrived(weights[k].at[over_y, z, far_x, first], s_dy.at[k, 0], r_dy.at[k, 0])
        arrived(weights[k].at[over_y, z, far_x, second], s_dx.at[k, 0], r_dx.at[k, 0])
        src = weights[k].at[over_y, z, far_x]
        for step in range(1, NZ):
            push(src, src, s_dx.at[k, step], r_dx.at[k, step], z_peer(step), k)

    def finish_z(k):
        for step in range(1, NZ):
            at = z_from(step)
            arrived(weights[k].at[mine, at, x], s_z.at[k, step], r_zs.at[k, step])
            arrived(weights[k].at[mine, at, far_x], s_x.at[k, step], r_x.at[k, step])
            arrived(weights[k].at[over_y, at, x], s_y.at[k, step], r_y.at[k, step])
            arrived(weights[k].at[over_y, at, far_x], s_dx.at[k, step], r_dx.at[k, step])
        to_core(k, 0, mine, x)
        columns_to_core(k)
        exchange_core(k)

    def columns_to_core(k):
        to_core(k, 1, mine, far_x)
        to_core(k, 2, over_y, x)

    def finish(k):
        for step in range(NZ):
            arrived(
                weights[k].at[over_y, z_from(step), far_x, first],
                s_dy.at[k, step],
                r_dy.at[k, step],
            )
            arrived(
                weights[k].at[over_y, z_from(step), far_x, second],
                s_dx.at[k, step],
                r_dx.at[k, step],
            )

    def exchange_core(k):
        to_core(k, 3, over_y, far_x)
        from_core(k)

    def from_core(k):
        for index, (block_index, column) in enumerate(
            (
                (y * NC + far_c, x),
                (y * NC + far_c, far_x),
                (far_y * NC + far_c, x),
                (far_y * NC + far_c, far_x),
            )
        ):
            arrived(
                weights[k].at[block_index, :, column], s_c.at[k, index], r_c.at[k, index]
            )

    def small_stage(which, buf, buf_in, stage):
        if stage < 3:
            peer = (c_peer, y_peer, x_peer)[stage]
            push(buf.at[stage], buf_in.at[stage], s_sm.at[which, stage], r_sm.at[which, stage], peer)
        else:
            for step in range(1, NZ):
                push(
                    buf.at[3],
                    buf_in.at[2 + step],
                    s_sm.at[which, 2 + step],
                    r_sm.at[which, 2 + step],
                    z_peer(step),
                )

    def small_add(which, buf, buf_in, stage):
        arrived(buf_in.at[stage], s_sm.at[which, stage], r_sm.at[which, stage])
        buf[stage + 1] = buf[stage] + buf_in[stage]

    def small_last(which, buf, buf_in):
        for step in range(1, NZ):
            arrived(buf_in.at[2 + step], s_sm.at[which, 2 + step], r_sm.at[which, 2 + step])
        total = jnp.zeros(buf.shape[1:], F32)
        for place in range(NZ):
            term = buf[3]
            for step in range(1, NZ):
                term = jnp.where(z_from(step) == place, buf_in[2 + step], term)
            total = total + term
        return total

    send_z(QKV)
    for copy in loads:
        copy.start()
    send_own(QKV)
    small_stage(0, par, par_in, 0)
    send_own(IN)
    small_add(0, par, par_in, 0)
    small_stage(0, par, par_in, 1)
    send_own(DOWN)
    forward_z(QKV, 1)
    small_add(0, par, par_in, 1)
    small_stage(0, par, par_in, 2)
    send_own(PILOT)
    forward_diagonal(QKV, 0)
    forward_z(QKV, 3)
    small_add(0, par, par_in, 2)
    small_stage(0, par, par_in, 3)
    forward_diagonal(QKV, 1)
    forward_z(QKV, 2)
    send_z(IN)
    for copy in loads:
        copy.wait()
    to_core(QKV, 0, mine, x)
    forward_diagonal(QKV, 3)
    forward_z(IN, 1)
    forward_diagonal(QKV, 2)
    columns_to_core(QKV)
    forward_z(IN, 3)
    forward_diagonal(IN, 0)
    forward_z(IN, 2)
    to_core(IN, 0, mine, x)
    send_z(DOWN)
    par[4] = small_last(0, par, par_in)
    finish(QKV)
    exchange_core(QKV)

    length = lens[mp]
    key_keep = lax.broadcasted_iota(jnp.int32, (rows, rows), 1) < length
    row_keep = (lax.broadcasted_iota(jnp.int32, (rows, 1), 0) < length).astype(F32)

    def par_row(index):
        return par[4, index : index + 1, :]

    def square(ref, m, start, stop):
        value = ref[m, :, :, :, start:stop]
        return value.reshape(width, stop - start)

    def project(m, carry):
        bias = par[4, pl.ds(QKV_ROW + m, 1), :qkv_cols]
        qkv[m] = (nn(xs[...], square(w_a, m, 0, qkv_cols)) + bias).astype(BF16)
        return carry

    lax.fori_loop(0, GROUP, project, 0)

    def attend(m, carry):
        part = qkv[m]
        for h in range(heads_here):
            lo = h * HEAD_DIM
            q = part[:, lo : lo + HEAD_DIM]
            k = part[:, head_cols + lo : head_cols + lo + HEAD_DIM]
            v = part[:, 2 * head_cols + lo : 2 * head_cols + lo + HEAD_DIM]
            score = jnp.where(key_keep, nt(q, k) * scale, -1000000000.0)
            expo = jnp.exp(score - jnp.max(score, -1, keepdims=True))
            weight = expo / jnp.sum(expo, -1, keepdims=True)
            prob[m * heads_here + h] = weight
            ctx[m, :, lo : lo + HEAD_DIM] = nn(weight.astype(BF16), v).astype(BF16)
        return carry

    forward_diagonal(IN, 1)
    forward_diagonal(IN, 3)
    forward_z(DOWN, 1)
    forward_diagonal(PILOT, 0)
    send_z(PILOT)
    side_z(PILOT)
    lax.fori_loop(0, NY, attend, 0)
    forward_diagonal(IN, 2)
    columns_to_core(IN)
    forward_z(DOWN, 3)
    forward_diagonal(DOWN, 0)
    corner_z(PILOT)
    lax.fori_loop(NY, GROUP, attend, 0)

    acc[...] = jnp.zeros_like(acc)

    def attended(m, carry):
        acc[...] += nt(ctx[m], square(w_a, m, qkv_cols, width))
        return carry

    lax.fori_loop(0, GROUP, attended, 0)
    opening = xs[...].astype(F32) + acc[...] + par_row(2)
    centered = opening - row_mean(opening)
    rstd = lax.rsqrt(row_mean(centered * centered) + EPSILON)
    rs1[...] = rstd
    xhat = centered * rstd
    xh1[...] = xhat
    normed_low = (xhat * par_row(0) + par_row(3)).astype(BF16)
    low[...] = normed_low
    forward_z(DOWN, 2)
    to_core(DOWN, 0, mine, x)
    forward_diagonal(DOWN, 1)
    finish(IN)
    exchange_core(IN)
    forward_diagonal(DOWN, 3)

    def expand(m, carry):
        pre = nn(low[...], square(w_i, m, 0, width)) + par[4, pl.ds(BIAS_ROW + m, 1), :]
        gate = 0.5 + 0.5 * lax.erf(pre * math.sqrt(0.5))
        hid[m] = (pre * gate).astype(BF16)
        gder[m] = gate + pre * (jnp.exp(-0.5 * pre * pre) * (1.0 / math.sqrt(2.0 * math.pi)))
        return carry

    lax.fori_loop(0, GROUP, expand, 0)
    low_t[...] = low[...].T
    forward_diagonal(DOWN, 2)
    columns_to_core(DOWN)
    acc[...] = xh1[...] * par_row(0) + par_row(3) + par_row(4)

    def contract(m):
        acc[...] += nt(hid[m], square(w_d, m, 0, width))

    contract(mine)
    finish(DOWN)
    to_core(DOWN, 3, over_y, far_x)
    contract(over_y)
    from_core(DOWN)
    contract(y * NC + far_c)
    contract(far_y * NC + far_c)
    stream = acc[...]
    centered = stream - row_mean(stream)
    rstd = lax.rsqrt(row_mean(centered * centered) + EPSILON)
    rs2[...] = rstd
    xhat = centered * rstd
    xh2[...] = xhat
    own[0] = (xhat * par_row(1) + par_row(5)).astype(BF16)

    outs = (out_o, along_o, ig_o)

    def send_result(index):
        dst = outs[index].at[my_rows]
        pltpu.make_async_copy(own.at[index], dst, s_own.at[index]).start()
        push(own.at[index], dst, s_out.at[index, 0], r_out.at[index, 0], y_peer)
        push(own.at[index], dst, s_out.at[index, 1], r_out.at[index, 1], c_peer)

    def forward_result(index):
        part = outs[index].at[pl.ds(over_y * rows, rows)]
        arrived(part, s_out.at[index, 0], r_out.at[index, 0])
        push(part, part, s_out.at[index, 2], r_out.at[index, 2], c_peer)

    def finish_result(index):
        pltpu.make_async_copy(own.at[index], outs[index].at[my_rows], s_own.at[index]).wait()
        near = outs[index].at[pl.ds((y * NC + far_c) * rows, rows)]
        arrived(near, s_out.at[index, 1], r_out.at[index, 1])
        far = outs[index].at[pl.ds((far_y * NC + far_c) * rows, rows)]
        arrived(far, s_out.at[index, 2], r_out.at[index, 2])

    send_result(0)

    gs[0] = jnp.zeros(gs.shape[1:], F32)

    def norm_back(grad, xhat, rstd, gain):
        hat = grad * gain
        return rstd * (hat - row_mean(hat) - xhat * row_mean(hat * xhat))

    masked = cots[...].astype(F32) * row_keep
    xhat = xh2[...]
    gs[0, 1:2, :] = col_sum(masked * xhat)
    gs[0, 5:6, :] = col_sum(masked)
    stream_grad = norm_back(masked, xhat, rs2[...], par_row(1))
    gs[0, 4:5, :] = col_sum(stream_grad)
    sgrad[...] = stream_grad
    bl[...] = stream_grad.astype(BF16)
    bl_t[...] = bl[...].T
    acc[...] = stream_grad

    def block_of(i):
        return i * NC + far_c if i < NY else (i - NY) * NC + c

    slab = NX * block

    def outer(left_t, right, ref, m, start, stop):
        def one(zz, carry):
            top = pl.multiple_of(zz * slab, slab)
            value = nn(left_t[pl.ds(top, slab), :], right[...])
            ref[m, zz, :, :, start:stop] = value.astype(BF16).reshape(NX, block, stop - start)
            return carry

        lax.fori_loop(0, NZ, one, 0)

    def to_partner(ref, k, i):
        src = ref.at[i * NC + far_c]
        copy = remote(src, r_core.at[k, i], s_rc.at[k, i], r_rc.at[k, i], c_peer)
        return copy

    pre_low = own.at[1]

    def back_ff(i):
        m = block_of(i)
        grad = nn(bl[...], square(w_d, m, 0, width)) * gder[m]
        pre_low[...] = grad.astype(BF16)
        gs[0, pl.ds(BIAS_ROW + m, 1), :] = col_sum(pre_low[...].astype(F32))
        outer(low_t, pre_low, g_i, m, 0, width)
        acc[...] += nt(pre_low[...], square(w_i, m, 0, width))

        if i < NY:
            to_partner(g_i, 1, i).start()


    def flat_rows(k):
        return block - DEEP_ROWS if k == 0 else block

    def half_rows(k):
        return (block - DEEP_ROWS) // 2 if k == 0 else BWD_ROWS

    def top_rows(k):
        return pl.ds(0, half_rows(k))

    def low_rows(k):
        return pl.ds(half_rows(k), flat_rows(k) - half_rows(k))

    def low_part(k):
        return pl.ds(0, flat_rows(k) - half_rows(k))

    deep = pl.ds(block - DEEP_ROWS, DEEP_ROWS)

    def deep_first(ref):
        for step in range(1, NZ):
            for index, m in enumerate((mine, over_y)):
                push(
                    ref.at[m, z_at(step), :, deep],
                    r_deep.at[step - 1, index],
                    s_deep.at[step, index],
                    r_deeps.at[step, index],
                    z_peer(step),
                )

    def deep_second(ref):
        for index, m in enumerate((mine, over_y)):
            total = ref[m, z, :, deep, :].astype(F32)
            for step in range(1, NZ):
                arrived(r_deep.at[step - 1, index], s_deep.at[step, index], r_deeps.at[step, index])
                total = total + r_deep[step - 1, index].astype(F32)
            ref[m, z, :, deep, :] = total.astype(BF16)
        for index, (m, column, peer) in enumerate(
            ((over_y, x, y_peer), (mine, far_x, x_peer), (over_y, far_x, corner_peer))
        ):
            push(
                ref.at[m, z, column, deep],
                r_plane.at[index],
                s_plane.at[index],
                r_planes.at[index],
                peer,
            )

    def add_core_block(k, ref, yy):
        m = yy * NC + c
        remote(
            ref.at[m], r_core.at[k, yy], s_rc.at[k, yy], r_rc.at[k, yy], c_peer
        ).wait_recv()

        def one(zz, carry):
            ref[m, zz] = ref[m, zz] + r_core[k, yy, zz]
            return carry

        lax.fori_loop(0, NZ, one, 0)

    def first_over_y(k, ref):
        push(
            ref.at[over_y, :, :, top_rows(k)],
            r_yf.at[k, :, :, top_rows(k)],
            s_red.at[k, 0],
            r_red.at[k, 0],
            y_peer,
        )

    def first_over_x(k, ref, yy):
        push(
            ref.at[yy * NC + c, :, far_x, low_rows(k)],
            r_xf.at[k, yy, :, low_part(k)],
            s_red.at[k, 1 + yy],
            r_red.at[k, 1 + yy],
            x_peer,
        )

    def add_core(k, ref):
        for yy in range(NY):
            add_core_block(k, ref, yy)

    def reduce_first(k, ref):
        first_over_y(k, ref)
        for yy in range(NY):
            first_over_x(k, ref, yy)

    def reduce_second(k, ref):
        top, low, part = top_rows(k), low_rows(k), low_part(k)
        arrived(r_yf.at[k, :, :, top], s_red.at[k, 0], r_red.at[k, 0])
        ref[mine, :, :, top, :] = ref[mine, :, :, top, :] + r_yf[k, :, :, top, :]
        push(
            ref.at[mine, :, far_x, top],
            r_xs.at[k, :, top],
            s_red.at[k, 3],
            r_red.at[k, 3],
            x_peer,
        )
        for yy in range(NY):
            m = yy * NC + c
            arrived(r_xf.at[k, yy, :, part], s_red.at[k, 1 + yy], r_red.at[k, 1 + yy])
            ref[m, :, x, low, :] = ref[m, :, x, low, :] + r_xf[k, yy, :, part, :]
        push(
            ref.at[over_y, :, x, low],
            r_ys.at[k, :, part],
            s_red.at[k, 4],
            r_red.at[k, 4],
            y_peer,
        )

    def reduce_third(k, ref):
        top, low, part = top_rows(k), low_rows(k), low_part(k)
        arrived(r_xs.at[k, :, top], s_red.at[k, 3], r_red.at[k, 3])
        ref[mine, :, x, top, :] = ref[mine, :, x, top, :] + r_xs[k, :, top, :]
        arrived(r_ys.at[k, :, part], s_red.at[k, 4], r_red.at[k, 4])
        ref[mine, :, x, low, :] = ref[mine, :, x, low, :] + r_ys[k, :, part, :]
        flat = pl.ds(0, flat_rows(k))
        for step in range(1, NZ):
            push(
                ref.at[mine, z_at(step), x, flat],
                r_z.at[k, step - 1, flat],
                s_rz.at[k, step],
                r_rz.at[k, step],
                z_peer(step),
            )

    def reduce_last(k, ref, result):
        flat = pl.ds(0, flat_rows(k))
        total = ref[mine, z, x, flat, :].astype(F32)
        for step in range(1, NZ):
            arrived(r_z.at[k, step - 1, flat], s_rz.at[k, step], r_rz.at[k, step])
            total = total + r_z[k, step - 1, flat, :].astype(F32)
        result[flat, :] = total
        if k == 0:
            total = ref[mine, z, x, deep, :].astype(F32)
            for index in range(3):
                arrived(r_plane.at[index], s_plane.at[index], r_planes.at[index])
                total = total + r_plane[index].astype(F32)
            result[deep, :] = total

    for i in range(NY):
        outer(bl_t, hid.at[block_of(i)], g_d, block_of(i), 0, width)
        to_partner(g_d, 0, i).start()
    for yy in (far_y, y):
        outer(bl_t, hid.at[yy * NC + c], g_d, yy * NC + c, 0, width)
        add_core_block(0, g_d, yy)
        first_over_x(0, g_d, yy)
        if yy is far_y:
            first_over_y(0, g_d)
    deep_first(g_d)
    for i in range(GROUP):
        back_ff(i)
    add_core(1, g_i)
    reduce_first(1, g_i)
    forward_result(0)

    xhat = xh1[...]
    normed_grad = acc[...]
    gs[0, 0:1, :] = col_sum(normed_grad * xhat)
    gs[0, 3:4, :] = col_sum(normed_grad)
    first_grad = norm_back(normed_grad, xhat, rs1[...], par_row(0))
    gs[0, 2:3, :] = col_sum(first_grad)
    acc[...] = first_grad
    bl[...] = first_grad.astype(BF16)
    bl_t[...] = bl[...].T
    low_t[...] = xs[...].T
    g_a = w_d

    def back_attention(i):
        m = block_of(i)
        outer(bl_t, ctx.at[m], g_a, m, qkv_cols, width)
        context_grad = nn(bl[...], square(w_a, m, qkv_cols, width)).astype(BF16)
        part = qkv[m]
        for h in range(heads_here):
            lo = h * HEAD_DIM
            q = part[:, lo : lo + HEAD_DIM]
            k = part[:, head_cols + lo : head_cols + lo + HEAD_DIM]
            v = part[:, 2 * head_cols + lo : 2 * head_cols + lo + HEAD_DIM]
            d_ctx = context_grad[:, lo : lo + HEAD_DIM]
            weight = prob[m * heads_here + h]
            d_value = tn(weight.astype(BF16), d_ctx)
            d_prob = nt(d_ctx, v)
            spread = jnp.sum(weight * d_prob, -1, keepdims=True)
            d_score = (weight * (d_prob - spread)).astype(BF16)
            qg[:, lo : lo + HEAD_DIM] = (nn(d_score, k) * scale).astype(BF16)
            qg[:, head_cols + lo : head_cols + lo + HEAD_DIM] = (tn(d_score, q) * scale).astype(BF16)
            qg[:, 2 * head_cols + lo : 2 * head_cols + lo + HEAD_DIM] = d_value.astype(BF16)
        gs[0, pl.ds(QKV_ROW + m, 1), :qkv_cols] = col_sum(qg[...].astype(F32))
        outer(low_t, qg, g_a, m, 0, qkv_cols)
        acc[...] += nt(qg[...], square(w_a, m, 0, qkv_cols))

        if i < NY:
            to_partner(g_a, 2, i).start()

    for chunk, copy in sends:
        if chunk == DOWN:
            copy.wait_send()
    for i in range(GROUP):
        back_attention(i)
        if i == 2:
            reduce_second(0, g_d)
    own[2] = acc[...].astype(BF16)
    small_stage(1, gs, gs_in, 0)
    add_core(2, g_a)
    reduce_second(1, g_i)
    reduce_first(2, g_a)
    small_add(1, gs, gs_in, 0)
    small_stage(1, gs, gs_in, 1)
    deep_second(g_d)
    reduce_third(0, g_d)
    finish_z(PILOT)
    acc[...] = jnp.zeros_like(acc)

    def steer(m, carry):
        acc[...] += nt(hid[m], square(w_p, m, 0, width))
        return carry

    lax.fori_loop(0, GROUP, steer, 0)
    tangent = acc[...]
    xhat = xh2[...]
    along = rs2[...] * (tangent - row_mean(tangent) - xhat * row_mean(tangent * xhat))
    own[1] = (par_row(1) * along).astype(BF16)
    reduce_third(1, g_i)
    reduce_second(2, g_a)
    small_add(1, gs, gs_in, 1)
    small_stage(1, gs, gs_in, 2)
    send_result(2)
    send_result(1)
    reduce_last(0, g_d, grad_d)
    small_add(1, gs, gs_in, 2)
    small_stage(1, gs, gs_in, 3)
    reduce_third(2, g_a)
    reduce_last(1, g_i, grad_i)
    forward_result(2)
    forward_result(1)
    small_sum[...] = small_last(1, gs, gs_in)
    reduce_last(2, g_a, grad_a)
    for index in range(3):
        finish_result(index)
    for k, ref in enumerate((g_d, g_i, g_a)):
        for i in range(NY):
            to_partner(ref, k, i).wait_send()
    for chunk, copy in sends:
        if chunk != DOWN:
            copy.wait_send()


def run_layer(inner, lens, tok, cot, shards, projections, small):
    width = tok.shape[1]
    rows = tok.shape[0] // GROUP
    block = width // BLOCKS
    head_cols = width // GROUP
    qkv_cols = 3 * head_cols
    heads = width // HEAD_DIM
    anywhere = pl.BlockSpec(memory_space=pl.ANY)
    vmem = pl.BlockSpec(memory_space=pltpu.VMEM)
    weight = pltpu.VMEM((GROUP, NZ, NX, block, width), BF16)
    act = pltpu.VMEM((rows, width), F32)
    act_low = pltpu.VMEM((rows, width), BF16)
    column = pltpu.VMEM((rows, 1), F32)
    dma = pltpu.SemaphoreType.DMA
    grads = 3
    scratch = (
        [weight] * 6
        + [
            pltpu.VMEM((grads, NY, NZ, NX, block, width), BF16),
            pltpu.VMEM((grads, NZ, NX, BWD_ROWS, width), BF16),
            pltpu.VMEM((grads, NY, NZ, block - BWD_ROWS, width), BF16),
            pltpu.VMEM((grads, NZ, BWD_ROWS, width), BF16),
            pltpu.VMEM((grads, NZ, block - BWD_ROWS, width), BF16),
            pltpu.VMEM((grads, NZ - 1, block, width), BF16),
            pltpu.VMEM((NZ - 1, 2, NX, DEEP_ROWS, width), BF16),
            pltpu.VMEM((3, DEEP_ROWS, width), BF16),
            pltpu.VMEM((5, SMALL_ROWS, width), F32),
            pltpu.VMEM((6, SMALL_ROWS, width), F32),
            pltpu.VMEM((4, SMALL_ROWS, width), F32),
            pltpu.VMEM((6, SMALL_ROWS, width), F32),
            act_low,
            act_low,
            pltpu.VMEM((GROUP, rows, qkv_cols), BF16),
            pltpu.VMEM((heads, rows, rows), F32),
            pltpu.VMEM((GROUP, rows, head_cols), BF16),
            act,
            act,
            column,
            act_low,
            pltpu.VMEM((width, rows), BF16),
            pltpu.VMEM((GROUP, rows, width), BF16),
            pltpu.VMEM((GROUP, rows, width), F32),
            act,
            column,
            act,
            act_low,
            pltpu.VMEM((width, rows), BF16),
            pltpu.VMEM((rows, qkv_cols), BF16),
            pltpu.VMEM((3, rows, width), BF16),
        ]
        + [dma((7,))]
        + [dma((4, NZ))] * 12
        + [dma((grads, NY))] * 2
        + [dma((grads, 5))] * 2
        + [dma((grads, NZ))] * 2
        + [dma((NZ, 2))] * 2
        + [dma((3,))] * 2
        + [dma((2, 6))] * 2
        + [dma((3, 3))] * 2
        + [dma((3,))]
    )
    whole = jax.ShapeDtypeStruct(tok.shape, BF16)
    piece = jax.ShapeDtypeStruct((block, width), F32)
    return pl.pallas_call(
        functools.partial(layer_kernel, inner),
        out_shape=(
            whole,
            whole,
            whole,
            piece,
            piece,
            piece,
            jax.ShapeDtypeStruct((SMALL_ROWS, width), F32),
        ),
        in_specs=[pl.BlockSpec(memory_space=pltpu.SMEM)] + [anywhere] * 5 + [vmem] * 6,
        out_specs=(anywhere,) * 3 + (vmem,) * 4,
        scratch_shapes=scratch,
        compiler_params=pltpu.CompilerParams(
            collective_id=0, has_side_effects=True, vmem_limit_bytes=67043328
        ),
        name="layer",
    )(lens, tok, cot, *shards, *projections, *small)


def finish_kernel(
    out,
    input_grad,
    along,
    grad_a,
    grad_i,
    grad_d,
    sums,
    out_o,
    input_grad_o,
    along_o,
    grad_qkv_o,
    grad_out_o,
    grad_i_o,
    grad_d_o,
    grad_gains_o,
    grad_shifts_o,
    grad_in_bias_o,
    grad_qvb_o,
):
    out_o[...] = out[...]
    input_grad_o[...] = input_grad[...].astype(F32)
    along_o[...] = along[...].astype(F32)

    @pl.when(pl.program_id(0) == 0)
    def _():
        dp = lax.axis_index("dp")
        mp = lax.axis_index("mp")
        rows, width = grad_a.shape
        head_cols = grad_out_o.shape[0]
        exact = lax.Precision.HIGHEST

        def pick(values, share, offset):
            places = one_hot(share, width, offset, F32)
            return lax.dot_general(
                values,
                places,
                (((1,), (1,)), ((), ())),
                precision=exact,
                preferred_element_type=F32,
            )

        for part in range(3):
            grad_qkv_o[part] = grad_a[:, part * head_cols : (part + 1) * head_cols]
        grad_out_o[...] = lax.dot_general(
            grad_a[:, 3 * head_cols :],
            one_hot(rows, rows, 0, F32),
            (((0,), (0,)), ((), ())),
            precision=exact,
            preferred_element_type=F32,
        )
        grad_i_o[...] = grad_i[...]
        grad_d_o[...] = grad_d[...]
        share = grad_gains_o.shape[1]
        bias_share = grad_qvb_o.shape[1]
        norms = pick(sums[0:8, :], share, dp * share)
        grad_gains_o[...] = norms[0:2]
        grad_shifts_o[...] = norms[2:6]
        grad_in_bias_o[...] = pick(sums[pl.ds(BIAS_ROW + mp, 1), :], share, dp * share)
        row = sums[pl.ds(QKV_ROW + mp, 1), :]
        grad_qvb_o[0:1, :] = pick(row, bias_share, dp * bias_share)
        grad_qvb_o[1:2, :] = pick(row, bias_share, 2 * head_cols + dp * bias_share)


def run_finish(
    out, input_grad, along, grad_a, grad_i, grad_d, sums, head_cols, share, bias_share
):
    steps = 2
    rows, width = out.shape
    local_rows = grad_a.shape[0]

    def whole(*shape):
        return pl.BlockSpec(shape, lambda i: (0,) * len(shape))

    slab = pl.BlockSpec((rows // steps, width), lambda i: (i, 0))
    shapes = (
        (3, local_rows, head_cols),
        (head_cols, local_rows),
        (local_rows, width),
        (local_rows, width),
        (2, share),
        (4, share),
        (1, share),
        (2, bias_share),
    )
    return pl.pallas_call(
        finish_kernel,
        grid=(steps,),
        out_shape=(
            jax.ShapeDtypeStruct(out.shape, BF16),
            jax.ShapeDtypeStruct(out.shape, F32),
            jax.ShapeDtypeStruct(out.shape, F32),
        )
        + tuple(jax.ShapeDtypeStruct(shape, F32) for shape in shapes),
        in_specs=[slab] * 3 + [whole(local_rows, width)] * 3 + [whole(*sums.shape)],
        out_specs=(slab,) * 3 + tuple(whole(*shape) for shape in shapes),
        name="finish",
    )(out, input_grad, along, grad_a, grad_i, grad_d, sums)


def local(
    tokens, cotangent, lengths, w_qkv, qv_bias, w_out, w_in, in_bias, w_down, pilot, gains, shifts
):
    n_dp = lax.axis_size("dp")
    inner = n_dp // BLOCKS
    groups = [[b * inner + i for i in range(inner)] for b in range(BLOCKS)]
    head_cols = w_out.shape[0]
    local_rows = w_qkv.shape[0]
    shards = (w_in, w_down.T, pilot.T)
    projections = (w_qkv.transpose(1, 0, 2), w_out)
    small = (gains, shifts, in_bias, qv_bias.reshape(2, -1))
    if inner > 1:

        def joined(item, axis):
            return lax.all_gather(item, "dp", axis=axis, tiled=True, axis_index_groups=groups)

        shards = tuple(joined(item, 0) for item in shards)
        projections = tuple(joined(item, 1) for item in projections)
        small = tuple(joined(item, 1) for item in small)

    out, along, input_grad, grad_a, grad_i, grad_d, sums = run_layer(
        inner, lengths, tokens, cotangent, shards, projections, small
    )
    if inner > 1:
        grad_a, grad_i, grad_d = (
            lax.psum_scatter(
                item, "dp", scatter_dimension=0, tiled=True, axis_index_groups=groups
            )
            for item in (grad_a, grad_i, grad_d)
        )
        sums = lax.psum(sums, "dp", axis_index_groups=groups)
    (
        out,
        input_grad,
        along,
        grad_qkv,
        grad_out,
        grad_i,
        grad_d,
        grad_gains,
        grad_shifts,
        grad_in_bias,
        grad_qvb,
    ) = run_finish(
        out, input_grad, along, grad_a, grad_i, grad_d, sums, head_cols, gains.shape[1], qv_bias.shape[2]
    )
    return (
        out,
        input_grad,
        along,
        grad_qkv.transpose(1, 0, 2),
        grad_qvb.reshape(qv_bias.shape),
        grad_out,
        grad_i,
        grad_in_bias,
        grad_d.T,
        grad_gains,
        grad_shifts,
    )


def solution(mesh):
    in_specs = (
        P("dp", None),
        P("dp", None),
        P("dp"),
        P("dp", None, "mp"),
        P(None, "mp", "dp"),
        P("mp", "dp"),
        P("dp", "mp"),
        P("mp", "dp"),
        P("mp", "dp"),
        P("mp", "dp"),
        P(None, "dp"),
        P(None, "dp"),
    )
    out_specs = (
        P("dp", None),
        P("dp", None),
        P("dp", None),
        P("dp", None, "mp"),
        P(None, "mp", "dp"),
        P("mp", "dp"),
        P("dp", "mp"),
        P("mp", "dp"),
        P("mp", "dp"),
        P(None, "dp"),
        P(None, "dp"),
    )
    return jax.shard_map(local, mesh=mesh, in_specs=in_specs, out_specs=out_specs, check_vma=False)
```

```python
import functools
import math

import jax
import jax.numpy as jnp
from jax import lax
from jax.experimental import pallas as pl
from jax.experimental.pallas import tpu as pltpu
from jax.sharding import PartitionSpec as P

HEAD_DIM = 64
SEQ_LEN = 256
EPSILON = 1e-06
NZ, NX, NY, NC = 4, 2, 2, 2
BLOCKS = NZ * NX
GROUP = NY * NC
SMALL_ROWS = 16
BIAS_ROW = 6
QKV_ROW = BIAS_ROW + GROUP
FWD_ROWS = 48
BWD_ROWS = 48
DEEP_ROWS = 32
F32 = jnp.float32
BF16 = jnp.bfloat16
QKV, IN, DOWN, PILOT = range(4)


def nt(a, b):
    return lax.dot_general(a, b, (((1,), (1,)), ((), ())), preferred_element_type=F32)


def tn(a, b):
    return lax.dot_general(a, b, (((0,), (0,)), ((), ())), preferred_element_type=F32)


def nn(a, b):
    return jnp.dot(a, b, preferred_element_type=F32)


def one_hot(rows, columns, offset, dtype=BF16):
    row = lax.broadcasted_iota(jnp.int32, (rows, columns), 0)
    column = lax.broadcasted_iota(jnp.int32, (rows, columns), 1)
    return (row + offset == column).astype(F32).astype(dtype)


def row_mean(v):
    return jnp.mean(v, -1, keepdims=True)


def col_sum(v):
    return jnp.sum(v, 0, keepdims=True)


def layer_kernel(
    inner,
    lens,
    tok,
    cot,
    shard_i,
    shard_d,
    shard_p,
    w_qkv,
    w_out,
    gains,
    shifts,
    in_bias,
    qv_bias,
    out_o,
    along_o,
    ig_o,
    grad_a,
    grad_i,
    grad_d,
    small_sum,
    w_a,
    w_i,
    w_d,
    w_p,
    g_i,
    g_d,
    r_core,
    r_yf,
    r_xf,
    r_xs,
    r_ys,
    r_z,
    r_deep,
    r_plane,
    par,
    par_in,
    gs,
    gs_in,
    xs,
    cots,
    qkv,
    prob,
    ctx,
    acc,
    xh1,
    rs1,
    low,
    low_t,
    hid,
    gder,
    xh2,
    rs2,
    sgrad,
    bl,
    bl_t,
    qg,
    own,
    s_load,
    s_z,
    r_zs,
    s_x,
    r_x,
    s_y,
    r_y,
    s_dx,
    r_dx,
    s_dy,
    r_dy,
    s_c,
    r_c,
    s_rc,
    r_rc,
    s_red,
    r_red,
    s_rz,
    r_rz,
    s_deep,
    r_deeps,
    s_plane,
    r_planes,
    s_sm,
    r_sm,
    s_out,
    r_out,
    s_own,
):
    weights = (w_a, w_i, w_d, w_p)
    width = xs.shape[1]
    block = w_a.shape[3]
    head_cols = ctx.shape[2]
    qkv_cols = 3 * head_cols
    heads_here = head_cols // HEAD_DIM
    rows = xs.shape[0]
    scale = HEAD_DIM ** (-0.5)

    dp = lax.axis_index("dp")
    mp = lax.axis_index("mp")
    spot = dp // inner
    rest = dp - spot * inner
    z, x = spot // NX, spot % NX
    y, c = mp // NC, mp % NC
    far_y, far_x, far_c = 1 - y, 1 - x, 1 - c
    mine = mp
    shards = (w_a.at[mine, z, x], shard_i, shard_d, shard_p)
    over_y = far_y * NC + c
    x_peer = {"dp": (z * NX + far_x) * inner + rest, "mp": mp}
    y_peer = {"dp": dp, "mp": over_y}
    c_peer = {"dp": dp, "mp": y * NC + far_c}
    corner_peer = {"dp": x_peer["dp"], "mp": over_y}

    def z_at(step):
        if step == 0:
            return z
        if step == 1:
            return z + 1 - 2 * (z % 2)
        if step == 2:
            return (z + NZ // 2) % NZ
        return NZ - 1 - z

    z_from = z_at

    def z_peer(step):
        return {"dp": (z_at(step) * NX + x) * inner + rest, "mp": mp}

    sends = []

    def remote(src, dst, send, recv, peer):
        return pltpu.make_async_remote_copy(
            src_ref=src,
            dst_ref=dst,
            send_sem=send,
            recv_sem=recv,
            device_id=peer,
            device_id_type=pl.DeviceIdType.MESH,
        )

    def push(src, dst, send, recv, peer, chunk=None):
        copy = remote(src, dst, send, recv, peer)
        copy.start()
        sends.append((chunk, copy))

    def arrived(dst, send, recv):
        remote(dst, dst, send, recv, c_peer).wait_recv()

    barrier = pltpu.get_barrier_semaphore()
    peers = [x_peer, y_peer, c_peer, corner_peer] + [z_peer(step) for step in range(1, NZ)]
    for peer in peers:
        pl.semaphore_signal(barrier, inc=1, device_id=peer, device_id_type=pl.DeviceIdType.MESH)

    for part in range(3):
        w_a[mine, z, x, :, part * head_cols : (part + 1) * head_cols] = w_qkv[part]
    w_a[mine, z, x, :, qkv_cols:] = nt(one_hot(block, block, 0), w_out[...]).astype(BF16)
    share = gains.shape[1]
    bias_share = qv_bias.shape[1]
    par[0] = jnp.zeros(par.shape[1:], F32)
    everyone = one_hot(share, width, spot * share)
    first_only = one_hot(share, width, jnp.where(mp == 0, spot * share, -width))
    par[0, 0:2, :] = nn(gains[...], first_only)
    par[0, 2:6, :] = nn(shifts[...], first_only)
    par[0, pl.ds(BIAS_ROW + mp, 1), :] = nn(in_bias[...], everyone)
    par[0, pl.ds(QKV_ROW + mp, 1), :] = nn(
        qv_bias[0:1, :], one_hot(bias_share, width, spot * bias_share)
    ) + nn(qv_bias[1:2, :], one_hot(bias_share, width, 2 * head_cols + spot * bias_share))

    pl.semaphore_wait(barrier, len(peers))

    loads = []
    for k in range(1, 4):
        loads.append(
            pltpu.make_async_copy(shards[k], weights[k].at[mine, z, x], s_load.at[k])
        )
    my_rows = pl.ds(mp * rows, rows)
    loads.append(pltpu.make_async_copy(tok.at[my_rows], xs, s_load.at[4]))
    loads.append(pltpu.make_async_copy(cot.at[my_rows], cots, s_load.at[5]))

    def send_z(k):
        for step in (1, 2):
            push(
                shards[k],
                weights[k].at[mine, z, x],
                s_z.at[k, step],
                r_zs.at[k, step],
                z_peer(step),
                k,
            )

    def send_own(k):
        for sem_s, sem_r, peer in ((s_x, r_x, x_peer), (s_y, r_y, y_peer)):
            push(shards[k], weights[k].at[mine, z, x], sem_s.at[k, 0], sem_r.at[k, 0], peer, k)

    def forward_z(k, step):
        src = weights[k].at[mine, z_from(step), x]
        arrived(src, s_z.at[k, step], r_zs.at[k, step])
        if step == 2:
            push(src, src, s_z.at[k, 3], r_zs.at[k, 3], z_peer(1), k)
        push(src, src, s_x.at[k, step], r_x.at[k, step], x_peer, k)
        push(src, src, s_y.at[k, step], r_y.at[k, step], y_peer, k)

    first = pl.ds(0, FWD_ROWS)
    second = pl.ds(FWD_ROWS, block - FWD_ROWS)

    def forward_diagonal(k, step):
        from_x = weights[k].at[mine, z_from(step), far_x]
        arrived(from_x, s_x.at[k, step], r_x.at[k, step])
        part = weights[k].at[mine, z_from(step), far_x, first]
        push(part, part, s_dy.at[k, step], r_dy.at[k, step], y_peer, k)
        from_y = weights[k].at[over_y, z_from(step), x]
        arrived(from_y, s_y.at[k, step], r_y.at[k, step])
        part = weights[k].at[over_y, z_from(step), x, second]
        push(part, part, s_dx.at[k, step], r_dx.at[k, step], x_peer, k)

    def to_core(k, index, block_index, column):
        src = weights[k].at[block_index, :, column]
        push(src, src, s_c.at[k, index], r_c.at[k, index], c_peer, k)

    def side_z(k):
        arrived(weights[k].at[mine, z, far_x], s_x.at[k, 0], r_x.at[k, 0])
        arrived(weights[k].at[over_y, z, x], s_y.at[k, 0], r_y.at[k, 0])
        for step in (1, 2):
            src = weights[k].at[mine, z, far_x]
            push(src, src, s_x.at[k, step], r_x.at[k, step], z_peer(step), k)
            src = weights[k].at[over_y, z, x]
            push(src, src, s_y.at[k, step], r_y.at[k, step], z_peer(step), k)

    def corner_x(k):
        src = weights[k].at[over_y, z, x]
        push(src, src, s_dx.at[k, 0], r_dx.at[k, 0], x_peer, k)

    def corner_z(k):
        src = weights[k].at[over_y, z, far_x]
        arrived(src, s_dx.at[k, 0], r_dx.at[k, 0])
        for step in (1, 2):
            push(src, src, s_dx.at[k, step], r_dx.at[k, step], z_peer(step), k)

    def side_relay(k):
        for src, send, recv in (
            (weights[k].at[mine, z_from(2), x], s_z, r_zs),
            (weights[k].at[mine, z_from(2), far_x], s_x, r_x),
            (weights[k].at[over_y, z_from(2), x], s_y, r_y),
        ):
            arrived(src, send.at[k, 2], recv.at[k, 2])
            push(src, src, send.at[k, 3], recv.at[k, 3], z_peer(1), k)

    def corner_relay(k):
        src = weights[k].at[over_y, z_from(2), far_x]
        arrived(src, s_dx.at[k, 2], r_dx.at[k, 2])
        push(src, src, s_dx.at[k, 3], r_dx.at[k, 3], z_peer(1), k)

    def finish_z(k):
        for step in (1, 3):
            at = z_from(step)
            arrived(weights[k].at[mine, at, x], s_z.at[k, step], r_zs.at[k, step])
            arrived(weights[k].at[mine, at, far_x], s_x.at[k, step], r_x.at[k, step])
            arrived(weights[k].at[over_y, at, x], s_y.at[k, step], r_y.at[k, step])
            arrived(weights[k].at[over_y, at, far_x], s_dx.at[k, step], r_dx.at[k, step])
        to_core(k, 0, mine, x)
        columns_to_core(k)
        exchange_core(k)

    def columns_to_core(k):
        to_core(k, 1, mine, far_x)
        to_core(k, 2, over_y, x)

    def finish(k):
        for step in range(NZ):
            arrived(
                weights[k].at[over_y, z_from(step), far_x, first],
                s_dy.at[k, step],
                r_dy.at[k, step],
            )
            arrived(
                weights[k].at[over_y, z_from(step), far_x, second],
                s_dx.at[k, step],
                r_dx.at[k, step],
            )

    def exchange_core(k):
        to_core(k, 3, over_y, far_x)
        from_core(k)

    def from_core(k):
        for index, (block_index, column) in enumerate(
            (
                (y * NC + far_c, x),
                (y * NC + far_c, far_x),
                (far_y * NC + far_c, x),
                (far_y * NC + far_c, far_x),
            )
        ):
            arrived(
                weights[k].at[block_index, :, column], s_c.at[k, index], r_c.at[k, index]
            )

    def small_stage(which, buf, buf_in, stage):
        if stage < 3:
            peer = (c_peer, y_peer, x_peer)[stage]
            push(buf.at[stage], buf_in.at[stage], s_sm.at[which, stage], r_sm.at[which, stage], peer)
        else:
            for step in range(1, NZ):
                push(
                    buf.at[3],
                    buf_in.at[2 + step],
                    s_sm.at[which, 2 + step],
                    r_sm.at[which, 2 + step],
                    z_peer(step),
                )

    def small_add(which, buf, buf_in, stage):
        arrived(buf_in.at[stage], s_sm.at[which, stage], r_sm.at[which, stage])
        buf[stage + 1] = buf[stage] + buf_in[stage]

    def small_last(which, buf, buf_in):
        for step in range(1, NZ):
            arrived(buf_in.at[2 + step], s_sm.at[which, 2 + step], r_sm.at[which, 2 + step])
        total = jnp.zeros(buf.shape[1:], F32)
        for place in range(NZ):
            term = buf[3]
            for step in range(1, NZ):
                term = jnp.where(z_from(step) == place, buf_in[2 + step], term)
            total = total + term
        return total

    send_z(QKV)
    for copy in loads:
        copy.start()
    send_own(QKV)
    small_stage(0, par, par_in, 0)
    send_own(IN)
    small_add(0, par, par_in, 0)
    small_stage(0, par, par_in, 1)
    send_own(DOWN)
    forward_z(QKV, 1)
    small_add(0, par, par_in, 1)
    small_stage(0, par, par_in, 2)
    send_own(PILOT)
    forward_diagonal(QKV, 0)
    forward_z(QKV, 2)
    send_z(IN)
    small_add(0, par, par_in, 2)
    small_stage(0, par, par_in, 3)
    forward_diagonal(QKV, 1)
    forward_z(QKV, 3)
    for copy in loads:
        copy.wait()
    to_core(QKV, 0, mine, x)
    forward_diagonal(QKV, 2)
    forward_z(IN, 1)
    forward_diagonal(QKV, 3)
    columns_to_core(QKV)
    forward_z(IN, 2)
    send_z(DOWN)
    forward_diagonal(IN, 0)
    forward_z(IN, 3)
    to_core(IN, 0, mine, x)
    par[4] = small_last(0, par, par_in)
    finish(QKV)
    exchange_core(QKV)

    length = lens[mp]
    key_keep = lax.broadcasted_iota(jnp.int32, (rows, rows), 1) < length
    row_keep = (lax.broadcasted_iota(jnp.int32, (rows, 1), 0) < length).astype(F32)

    def par_row(index):
        return par[4, index : index + 1, :]

    def square(ref, m, start, stop):
        value = ref[m, :, :, :, start:stop]
        return value.reshape(width, stop - start)

    def project(m, carry):
        bias = par[4, pl.ds(QKV_ROW + m, 1), :qkv_cols]
        qkv[m] = (nn(xs[...], square(w_a, m, 0, qkv_cols)) + bias).astype(BF16)
        return carry

    lax.fori_loop(0, GROUP, project, 0)

    def attend(m, carry):
        part = qkv[m]
        for h in range(heads_here):
            lo = h * HEAD_DIM
            q = part[:, lo : lo + HEAD_DIM]
            k = part[:, head_cols + lo : head_cols + lo + HEAD_DIM]
            v = part[:, 2 * head_cols + lo : 2 * head_cols + lo + HEAD_DIM]
            score = jnp.where(key_keep, nt(q, k) * scale, -1000000000.0)
            expo = jnp.exp(score - jnp.max(score, -1, keepdims=True))
            weight = expo / jnp.sum(expo, -1, keepdims=True)
            prob[m * heads_here + h] = weight
            ctx[m, :, lo : lo + HEAD_DIM] = nn(weight.astype(BF16), v).astype(BF16)
        return carry

    forward_diagonal(IN, 1)
    forward_diagonal(IN, 2)
    forward_z(DOWN, 1)
    lax.fori_loop(0, NY, attend, 0)
    forward_diagonal(IN, 3)
    columns_to_core(IN)
    forward_z(DOWN, 2)
    send_z(PILOT)
    side_z(PILOT)
    forward_diagonal(DOWN, 0)
    lax.fori_loop(NY, GROUP, attend, 0)

    acc[...] = jnp.zeros_like(acc)

    def attended(m, carry):
        acc[...] += nt(ctx[m], square(w_a, m, qkv_cols, width))
        return carry

    lax.fori_loop(0, GROUP, attended, 0)
    opening = xs[...].astype(F32) + acc[...] + par_row(2)
    centered = opening - row_mean(opening)
    rstd = lax.rsqrt(row_mean(centered * centered) + EPSILON)
    rs1[...] = rstd
    xhat = centered * rstd
    xh1[...] = xhat
    normed_low = (xhat * par_row(0) + par_row(3)).astype(BF16)
    low[...] = normed_low
    forward_z(DOWN, 3)
    to_core(DOWN, 0, mine, x)
    forward_diagonal(DOWN, 1)
    finish(IN)
    exchange_core(IN)
    forward_diagonal(DOWN, 2)

    def expand(m, carry):
        pre = nn(low[...], square(w_i, m, 0, width)) + par[4, pl.ds(BIAS_ROW + m, 1), :]
        gate = 0.5 + 0.5 * lax.erf(pre * math.sqrt(0.5))
        hid[m] = (pre * gate).astype(BF16)
        gder[m] = gate + pre * (jnp.exp(-0.5 * pre * pre) * (1.0 / math.sqrt(2.0 * math.pi)))
        return carry

    lax.fori_loop(0, GROUP, expand, 0)
    low_t[...] = low[...].T
    forward_diagonal(DOWN, 3)
    columns_to_core(DOWN)
    acc[...] = xh1[...] * par_row(0) + par_row(3) + par_row(4)

    def contract(m):
        acc[...] += nt(hid[m], square(w_d, m, 0, width))

    contract(mine)
    finish(DOWN)
    to_core(DOWN, 3, over_y, far_x)
    corner_x(PILOT)
    contract(over_y)
    from_core(DOWN)
    contract(y * NC + far_c)
    contract(far_y * NC + far_c)
    stream = acc[...]
    centered = stream - row_mean(stream)
    rstd = lax.rsqrt(row_mean(centered * centered) + EPSILON)
    rs2[...] = rstd
    xhat = centered * rstd
    xh2[...] = xhat
    own[0] = (xhat * par_row(1) + par_row(5)).astype(BF16)

    outs = (out_o, along_o, ig_o)

    def send_result(index):
        dst = outs[index].at[my_rows]
        pltpu.make_async_copy(own.at[index], dst, s_own.at[index]).start()
        push(own.at[index], dst, s_out.at[index, 0], r_out.at[index, 0], y_peer)
        push(own.at[index], dst, s_out.at[index, 1], r_out.at[index, 1], c_peer)

    def forward_result(index):
        part = outs[index].at[pl.ds(over_y * rows, rows)]
        arrived(part, s_out.at[index, 0], r_out.at[index, 0])
        push(part, part, s_out.at[index, 2], r_out.at[index, 2], c_peer)

    def finish_result(index):
        pltpu.make_async_copy(own.at[index], outs[index].at[my_rows], s_own.at[index]).wait()
        near = outs[index].at[pl.ds((y * NC + far_c) * rows, rows)]
        arrived(near, s_out.at[index, 1], r_out.at[index, 1])
        far = outs[index].at[pl.ds((far_y * NC + far_c) * rows, rows)]
        arrived(far, s_out.at[index, 2], r_out.at[index, 2])

    send_result(0)

    gs[0] = jnp.zeros(gs.shape[1:], F32)

    def norm_back(grad, xhat, rstd, gain):
        hat = grad * gain
        return rstd * (hat - row_mean(hat) - xhat * row_mean(hat * xhat))

    masked = cots[...].astype(F32) * row_keep
    xhat = xh2[...]
    gs[0, 1:2, :] = col_sum(masked * xhat)
    gs[0, 5:6, :] = col_sum(masked)
    stream_grad = norm_back(masked, xhat, rs2[...], par_row(1))
    gs[0, 4:5, :] = col_sum(stream_grad)
    sgrad[...] = stream_grad
    bl[...] = stream_grad.astype(BF16)
    bl_t[...] = bl[...].T
    acc[...] = stream_grad

    def block_of(i):
        return i * NC + far_c if i < NY else (i - NY) * NC + c

    slab = NX * block

    def outer(left_t, right, ref, m, start, stop):
        def one(zz, carry):
            top = pl.multiple_of(zz * slab, slab)
            value = nn(left_t[pl.ds(top, slab), :], right[...])
            ref[m, zz, :, :, start:stop] = value.astype(BF16).reshape(NX, block, stop - start)
            return carry

        lax.fori_loop(0, NZ, one, 0)

    def to_partner(ref, k, i):
        src = ref.at[i * NC + far_c]
        copy = remote(src, r_core.at[k, i], s_rc.at[k, i], r_rc.at[k, i], c_peer)
        return copy

    pre_low = own.at[1]

    def back_ff(i):
        m = block_of(i)
        grad = nn(bl[...], square(w_d, m, 0, width)) * gder[m]
        pre_low[...] = grad.astype(BF16)
        gs[0, pl.ds(BIAS_ROW + m, 1), :] = col_sum(pre_low[...].astype(F32))
        outer(low_t, pre_low, g_i, m, 0, width)
        acc[...] += nt(pre_low[...], square(w_i, m, 0, width))

        if i < NY:
            to_partner(g_i, 1, i).start()


    def flat_rows(k):
        return block - DEEP_ROWS if k == 0 else block

    def half_rows(k):
        return (block - DEEP_ROWS) // 2 if k == 0 else BWD_ROWS

    def top_rows(k):
        return pl.ds(0, half_rows(k))

    def low_rows(k):
        return pl.ds(half_rows(k), flat_rows(k) - half_rows(k))

    def low_part(k):
        return pl.ds(0, flat_rows(k) - half_rows(k))

    deep = pl.ds(block - DEEP_ROWS, DEEP_ROWS)

    def deep_first(ref):
        for step in range(1, NZ):
            for index, m in enumerate((mine, over_y)):
                push(
                    ref.at[m, z_at(step), :, deep],
                    r_deep.at[step - 1, index],
                    s_deep.at[step, index],
                    r_deeps.at[step, index],
                    z_peer(step),
                )

    def deep_second(ref):
        for index, m in enumerate((mine, over_y)):
            total = ref[m, z, :, deep, :].astype(F32)
            for step in range(1, NZ):
                arrived(r_deep.at[step - 1, index], s_deep.at[step, index], r_deeps.at[step, index])
                total = total + r_deep[step - 1, index].astype(F32)
            ref[m, z, :, deep, :] = total.astype(BF16)
        for index, (m, column, peer) in enumerate(
            ((over_y, x, y_peer), (mine, far_x, x_peer), (over_y, far_x, corner_peer))
        ):
            push(
                ref.at[m, z, column, deep],
                r_plane.at[index],
                s_plane.at[index],
                r_planes.at[index],
                peer,
            )

    def add_core_block(k, ref, yy):
        m = yy * NC + c
        remote(
            ref.at[m], r_core.at[k, yy], s_rc.at[k, yy], r_rc.at[k, yy], c_peer
        ).wait_recv()

        def one(zz, carry):
            ref[m, zz] = ref[m, zz] + r_core[k, yy, zz]
            return carry

        lax.fori_loop(0, NZ, one, 0)

    def first_over_y(k, ref):
        push(
            ref.at[over_y, :, :, top_rows(k)],
            r_yf.at[k, :, :, top_rows(k)],
            s_red.at[k, 0],
            r_red.at[k, 0],
            y_peer,
        )

    def first_over_x(k, ref, yy):
        push(
            ref.at[yy * NC + c, :, far_x, low_rows(k)],
            r_xf.at[k, yy, :, low_part(k)],
            s_red.at[k, 1 + yy],
            r_red.at[k, 1 + yy],
            x_peer,
        )

    def add_core(k, ref):
        for yy in range(NY):
            add_core_block(k, ref, yy)

    def reduce_first(k, ref):
        first_over_y(k, ref)
        for yy in range(NY):
            first_over_x(k, ref, yy)

    def reduce_second(k, ref):
        top, low, part = top_rows(k), low_rows(k), low_part(k)
        arrived(r_yf.at[k, :, :, top], s_red.at[k, 0], r_red.at[k, 0])
        ref[mine, :, :, top, :] = ref[mine, :, :, top, :] + r_yf[k, :, :, top, :]
        push(
            ref.at[mine, :, far_x, top],
            r_xs.at[k, :, top],
            s_red.at[k, 3],
            r_red.at[k, 3],
            x_peer,
        )
        for yy in range(NY):
            m = yy * NC + c
            arrived(r_xf.at[k, yy, :, part], s_red.at[k, 1 + yy], r_red.at[k, 1 + yy])
            ref[m, :, x, low, :] = ref[m, :, x, low, :] + r_xf[k, yy, :, part, :]
        push(
            ref.at[over_y, :, x, low],
            r_ys.at[k, :, part],
            s_red.at[k, 4],
            r_red.at[k, 4],
            y_peer,
        )

    def reduce_third(k, ref):
        top, low, part = top_rows(k), low_rows(k), low_part(k)
        arrived(r_xs.at[k, :, top], s_red.at[k, 3], r_red.at[k, 3])
        ref[mine, :, x, top, :] = ref[mine, :, x, top, :] + r_xs[k, :, top, :]
        arrived(r_ys.at[k, :, part], s_red.at[k, 4], r_red.at[k, 4])
        ref[mine, :, x, low, :] = ref[mine, :, x, low, :] + r_ys[k, :, part, :]
        flat = pl.ds(0, flat_rows(k))
        for step in range(1, NZ):
            push(
                ref.at[mine, z_at(step), x, flat],
                r_z.at[k, step - 1, flat],
                s_rz.at[k, step],
                r_rz.at[k, step],
                z_peer(step),
            )

    def reduce_last(k, ref, result):
        flat = pl.ds(0, flat_rows(k))
        total = ref[mine, z, x, flat, :].astype(F32)
        for step in range(1, NZ):
            arrived(r_z.at[k, step - 1, flat], s_rz.at[k, step], r_rz.at[k, step])
            total = total + r_z[k, step - 1, flat, :].astype(F32)
        result[flat, :] = total
        if k == 0:
            total = ref[mine, z, x, deep, :].astype(F32)
            for index in range(3):
                arrived(r_plane.at[index], s_plane.at[index], r_planes.at[index])
                total = total + r_plane[index].astype(F32)
            result[deep, :] = total

    for i in range(NY):
        outer(bl_t, hid.at[block_of(i)], g_d, block_of(i), 0, width)
        to_partner(g_d, 0, i).start()
    corner_z(PILOT)
    side_relay(PILOT)
    for yy in (far_y, y):
        outer(bl_t, hid.at[yy * NC + c], g_d, yy * NC + c, 0, width)
        add_core_block(0, g_d, yy)
        first_over_x(0, g_d, yy)
        if yy is far_y:
            first_over_y(0, g_d)
    deep_first(g_d)
    for i in range(GROUP):
        back_ff(i)
    add_core(1, g_i)
    reduce_first(1, g_i)
    forward_result(0)

    xhat = xh1[...]
    normed_grad = acc[...]
    gs[0, 0:1, :] = col_sum(normed_grad * xhat)
    gs[0, 3:4, :] = col_sum(normed_grad)
    first_grad = norm_back(normed_grad, xhat, rs1[...], par_row(0))
    gs[0, 2:3, :] = col_sum(first_grad)
    acc[...] = first_grad
    bl[...] = first_grad.astype(BF16)
    bl_t[...] = bl[...].T
    low_t[...] = xs[...].T
    g_a = w_d

    def back_attention(i):
        m = block_of(i)
        outer(bl_t, ctx.at[m], g_a, m, qkv_cols, width)
        context_grad = nn(bl[...], square(w_a, m, qkv_cols, width)).astype(BF16)
        part = qkv[m]
        for h in range(heads_here):
            lo = h * HEAD_DIM
            q = part[:, lo : lo + HEAD_DIM]
            k = part[:, head_cols + lo : head_cols + lo + HEAD_DIM]
            v = part[:, 2 * head_cols + lo : 2 * head_cols + lo + HEAD_DIM]
            d_ctx = context_grad[:, lo : lo + HEAD_DIM]
            weight = prob[m * heads_here + h]
            d_value = tn(weight.astype(BF16), d_ctx)
            d_prob = nt(d_ctx, v)
            spread = jnp.sum(weight * d_prob, -1, keepdims=True)
            d_score = (weight * (d_prob - spread)).astype(BF16)
            qg[:, lo : lo + HEAD_DIM] = (nn(d_score, k) * scale).astype(BF16)
            qg[:, head_cols + lo : head_cols + lo + HEAD_DIM] = (tn(d_score, q) * scale).astype(BF16)
            qg[:, 2 * head_cols + lo : 2 * head_cols + lo + HEAD_DIM] = d_value.astype(BF16)
        gs[0, pl.ds(QKV_ROW + m, 1), :qkv_cols] = col_sum(qg[...].astype(F32))
        outer(low_t, qg, g_a, m, 0, qkv_cols)
        acc[...] += nt(qg[...], square(w_a, m, 0, qkv_cols))

        if i < NY:
            to_partner(g_a, 2, i).start()

    for chunk, copy in sends:
        if chunk == DOWN:
            copy.wait_send()
    for i in range(GROUP):
        back_attention(i)
        if i == 0:
            corner_relay(PILOT)
        if i == 2:
            reduce_second(0, g_d)
    own[2] = acc[...].astype(BF16)
    small_stage(1, gs, gs_in, 0)
    add_core(2, g_a)
    reduce_second(1, g_i)
    reduce_first(2, g_a)
    small_add(1, gs, gs_in, 0)
    small_stage(1, gs, gs_in, 1)
    deep_second(g_d)
    reduce_third(0, g_d)
    finish_z(PILOT)
    acc[...] = jnp.zeros_like(acc)

    def steer(m, carry):
        acc[...] += nt(hid[m], square(w_p, m, 0, width))
        return carry

    lax.fori_loop(0, GROUP, steer, 0)
    tangent = acc[...]
    xhat = xh2[...]
    along = rs2[...] * (tangent - row_mean(tangent) - xhat * row_mean(tangent * xhat))
    own[1] = (par_row(1) * along).astype(BF16)
    reduce_third(1, g_i)
    reduce_second(2, g_a)
    small_add(1, gs, gs_in, 1)
    small_stage(1, gs, gs_in, 2)
    send_result(2)
    send_result(1)
    reduce_last(0, g_d, grad_d)
    small_add(1, gs, gs_in, 2)
    small_stage(1, gs, gs_in, 3)
    reduce_third(2, g_a)
    reduce_last(1, g_i, grad_i)
    forward_result(2)
    forward_result(1)
    small_sum[...] = small_last(1, gs, gs_in)
    reduce_last(2, g_a, grad_a)
    for index in range(3):
        finish_result(index)
    for k, ref in enumerate((g_d, g_i, g_a)):
        for i in range(NY):
            to_partner(ref, k, i).wait_send()
    for chunk, copy in sends:
        if chunk != DOWN:
            copy.wait_send()


def run_layer(inner, lens, tok, cot, shards, projections, small):
    width = tok.shape[1]
    rows = tok.shape[0] // GROUP
    block = width // BLOCKS
    head_cols = width // GROUP
    qkv_cols = 3 * head_cols
    heads = width // HEAD_DIM
    anywhere = pl.BlockSpec(memory_space=pl.ANY)
    vmem = pl.BlockSpec(memory_space=pltpu.VMEM)
    weight = pltpu.VMEM((GROUP, NZ, NX, block, width), BF16)
    act = pltpu.VMEM((rows, width), F32)
    act_low = pltpu.VMEM((rows, width), BF16)
    column = pltpu.VMEM((rows, 1), F32)
    dma = pltpu.SemaphoreType.DMA
    grads = 3
    scratch = (
        [weight] * 6
        + [
            pltpu.VMEM((grads, NY, NZ, NX, block, width), BF16),
            pltpu.VMEM((grads, NZ, NX, BWD_ROWS, width), BF16),
            pltpu.VMEM((grads, NY, NZ, block - BWD_ROWS, width), BF16),
            pltpu.VMEM((grads, NZ, BWD_ROWS, width), BF16),
            pltpu.VMEM((grads, NZ, block - BWD_ROWS, width), BF16),
            pltpu.VMEM((grads, NZ - 1, block, width), BF16),
            pltpu.VMEM((NZ - 1, 2, NX, DEEP_ROWS, width), BF16),
            pltpu.VMEM((3, DEEP_ROWS, width), BF16),
            pltpu.VMEM((5, SMALL_ROWS, width), F32),
            pltpu.VMEM((6, SMALL_ROWS, width), F32),
            pltpu.VMEM((4, SMALL_ROWS, width), F32),
            pltpu.VMEM((6, SMALL_ROWS, width), F32),
            act_low,
            act_low,
            pltpu.VMEM((GROUP, rows, qkv_cols), BF16),
            pltpu.VMEM((heads, rows, rows), F32),
            pltpu.VMEM((GROUP, rows, head_cols), BF16),
            act,
            act,
            column,
            act_low,
            pltpu.VMEM((width, rows), BF16),
            pltpu.VMEM((GROUP, rows, width), BF16),
            pltpu.VMEM((GROUP, rows, width), F32),
            act,
            column,
            act,
            act_low,
            pltpu.VMEM((width, rows), BF16),
            pltpu.VMEM((rows, qkv_cols), BF16),
            pltpu.VMEM((3, rows, width), BF16),
        ]
        + [dma((7,))]
        + [dma((4, NZ))] * 12
        + [dma((grads, NY))] * 2
        + [dma((grads, 5))] * 2
        + [dma((grads, NZ))] * 2
        + [dma((NZ, 2))] * 2
        + [dma((3,))] * 2
        + [dma((2, 6))] * 2
        + [dma((3, 3))] * 2
        + [dma((3,))]
    )
    whole = jax.ShapeDtypeStruct(tok.shape, BF16)
    piece = jax.ShapeDtypeStruct((block, width), F32)
    return pl.pallas_call(
        functools.partial(layer_kernel, inner),
        out_shape=(
            whole,
            whole,
            whole,
            piece,
            piece,
            piece,
            jax.ShapeDtypeStruct((SMALL_ROWS, width), F32),
        ),
        in_specs=[pl.BlockSpec(memory_space=pltpu.SMEM)] + [anywhere] * 5 + [vmem] * 6,
        out_specs=(anywhere,) * 3 + (vmem,) * 4,
        scratch_shapes=scratch,
        compiler_params=pltpu.CompilerParams(
            collective_id=0, has_side_effects=True, vmem_limit_bytes=67043328
        ),
        name="layer",
    )(lens, tok, cot, *shards, *projections, *small)


def finish_kernel(
    out,
    input_grad,
    along,
    grad_a,
    grad_i,
    grad_d,
    sums,
    out_o,
    input_grad_o,
    along_o,
    grad_qkv_o,
    grad_out_o,
    grad_i_o,
    grad_d_o,
    grad_gains_o,
    grad_shifts_o,
    grad_in_bias_o,
    grad_qvb_o,
):
    out_o[...] = out[...]
    input_grad_o[...] = input_grad[...].astype(F32)
    along_o[...] = along[...].astype(F32)

    @pl.when(pl.program_id(0) == 0)
    def _():
        dp = lax.axis_index("dp")
        mp = lax.axis_index("mp")
        rows, width = grad_a.shape
        head_cols = grad_out_o.shape[0]
        exact = lax.Precision.HIGHEST

        def pick(values, share, offset):
            places = one_hot(share, width, offset, F32)
            return lax.dot_general(
                values,
                places,
                (((1,), (1,)), ((), ())),
                precision=exact,
                preferred_element_type=F32,
            )

        for part in range(3):
            grad_qkv_o[part] = grad_a[:, part * head_cols : (part + 1) * head_cols]
        grad_out_o[...] = lax.dot_general(
            grad_a[:, 3 * head_cols :],
            one_hot(rows, rows, 0, F32),
            (((0,), (0,)), ((), ())),
            precision=exact,
            preferred_element_type=F32,
        )
        grad_i_o[...] = grad_i[...]
        grad_d_o[...] = grad_d[...]
        share = grad_gains_o.shape[1]
        bias_share = grad_qvb_o.shape[1]
        norms = pick(sums[0:8, :], share, dp * share)
        grad_gains_o[...] = norms[0:2]
        grad_shifts_o[...] = norms[2:6]
        grad_in_bias_o[...] = pick(sums[pl.ds(BIAS_ROW + mp, 1), :], share, dp * share)
        row = sums[pl.ds(QKV_ROW + mp, 1), :]
        grad_qvb_o[0:1, :] = pick(row, bias_share, dp * bias_share)
        grad_qvb_o[1:2, :] = pick(row, bias_share, 2 * head_cols + dp * bias_share)


def run_finish(
    out, input_grad, along, grad_a, grad_i, grad_d, sums, head_cols, share, bias_share
):
    steps = 2
    rows, width = out.shape
    local_rows = grad_a.shape[0]

    def whole(*shape):
        return pl.BlockSpec(shape, lambda i: (0,) * len(shape))

    slab = pl.BlockSpec((rows // steps, width), lambda i: (i, 0))
    shapes = (
        (3, local_rows, head_cols),
        (head_cols, local_rows),
        (local_rows, width),
        (local_rows, width),
        (2, share),
        (4, share),
        (1, share),
        (2, bias_share),
    )
    return pl.pallas_call(
        finish_kernel,
        grid=(steps,),
        out_shape=(
            jax.ShapeDtypeStruct(out.shape, BF16),
            jax.ShapeDtypeStruct(out.shape, F32),
            jax.ShapeDtypeStruct(out.shape, F32),
        )
        + tuple(jax.ShapeDtypeStruct(shape, F32) for shape in shapes),
        in_specs=[slab] * 3 + [whole(local_rows, width)] * 3 + [whole(*sums.shape)],
        out_specs=(slab,) * 3 + tuple(whole(*shape) for shape in shapes),
        name="finish",
    )(out, input_grad, along, grad_a, grad_i, grad_d, sums)


def local(
    tokens, cotangent, lengths, w_qkv, qv_bias, w_out, w_in, in_bias, w_down, pilot, gains, shifts
):
    n_dp = lax.axis_size("dp")
    inner = n_dp // BLOCKS
    groups = [[b * inner + i for i in range(inner)] for b in range(BLOCKS)]
    head_cols = w_out.shape[0]
    local_rows = w_qkv.shape[0]
    shards = (w_in, w_down.T, pilot.T)
    projections = (w_qkv.transpose(1, 0, 2), w_out)
    small = (gains, shifts, in_bias, qv_bias.reshape(2, -1))
    if inner > 1:

        def joined(item, axis):
            return lax.all_gather(item, "dp", axis=axis, tiled=True, axis_index_groups=groups)

        shards = tuple(joined(item, 0) for item in shards)
        projections = tuple(joined(item, 1) for item in projections)
        small = tuple(joined(item, 1) for item in small)

    out, along, input_grad, grad_a, grad_i, grad_d, sums = run_layer(
        inner, lengths, tokens, cotangent, shards, projections, small
    )
    if inner > 1:
        grad_a, grad_i, grad_d = (
            lax.psum_scatter(
                item, "dp", scatter_dimension=0, tiled=True, axis_index_groups=groups
            )
            for item in (grad_a, grad_i, grad_d)
        )
        sums = lax.psum(sums, "dp", axis_index_groups=groups)
    (
        out,
        input_grad,
        along,
        grad_qkv,
        grad_out,
        grad_i,
        grad_d,
        grad_gains,
        grad_shifts,
        grad_in_bias,
        grad_qvb,
    ) = run_finish(
        out, input_grad, along, grad_a, grad_i, grad_d, sums, head_cols, gains.shape[1], qv_bias.shape[2]
    )
    return (
        out,
        input_grad,
        along,
        grad_qkv.transpose(1, 0, 2),
        grad_qvb.reshape(qv_bias.shape),
        grad_out,
        grad_i,
        grad_in_bias,
        grad_d.T,
        grad_gains,
        grad_shifts,
    )


def solution(mesh):
    in_specs = (
        P("dp", None),
        P("dp", None),
        P("dp"),
        P("dp", None, "mp"),
        P(None, "mp", "dp"),
        P("mp", "dp"),
        P("dp", "mp"),
        P("mp", "dp"),
        P("mp", "dp"),
        P("mp", "dp"),
        P(None, "dp"),
        P(None, "dp"),
    )
    out_specs = (
        P("dp", None),
        P("dp", None),
        P("dp", None),
        P("dp", None, "mp"),
        P(None, "mp", "dp"),
        P("mp", "dp"),
        P("dp", "mp"),
        P("mp", "dp"),
        P("mp", "dp"),
        P(None, "dp"),
        P(None, "dp"),
    )
    return jax.shard_map(local, mesh=mesh, in_specs=in_specs, out_specs=out_specs, check_vma=False)
```
